128 devices in a mesh: row: 16 (over x_hi, y, core), proto: 8 (over z, x_lo).
Axes of the slice: x: 4 (x_hi: 2, x_lo: 2; x = x_hi * 2 + x_lo), y: 4, z: 4, core: 2. Of those that a mesh axis runs over, the one named last changes fastest.
Arguments:
- tokens: bfloat16 [8192, 4096], P('row'), may hold values from -6 to 6
- w_in: bfloat16 [4096, 8192], P('row', 'proto'), may hold values from -0.09375 to 0.09375
- w_out: bfloat16 [8192, 384], P('proto'), may hold values from -0.0625 to 0.0625
- teacher_z: bfloat16 [8192, 384], P(('row', 'proto')), may hold values from -6 to 6
- proto_student: bfloat16 [384, 49152], P(None, 'proto'), may hold values from -48 to 48
- proto_teacher: bfloat16 [384, 49152], P(None, 'proto'), may hold values from -48 to 48
- center: float32 [49152], P('proto'), may hold values from -0.6 to 0.6
- image_of: int32 [8192], P('row'), may hold values from 0 to 63
Outputs:
- loss: float32 [], replicated
- w_in_grad: float32 [4096, 8192], P('row', 'proto')
- w_out_grad: float32 [8192, 384], P('proto')
- proto_grad: float32 [384, 49152], P('row', 'proto')
The draws below stay inside these ranges and needn't reach their ends.
All inputs are finite; a program needn't handle non-finite values.
Results may differ from the reference program's by a relative error of at most 0.015.
Values may be sent and summed in bfloat16 or wider, within the bound.
A program may use at most 128 MiB of HBM per device.

```python
import math
import jax
import jax.numpy as jnp
from jax import lax

D = 4096
H = 8192
B = 384
K = 49152
ROWS = 8192
IMAGES = 64


def column_spread(key):
    logs = jax.random.uniform(jax.random.fold_in(key, 21), (K,), jnp.float32, math.log(0.1), math.log(1.0))
    values = jax.random.normal(jax.random.fold_in(key, 23), (B, K), jnp.float32)
    return values * jnp.exp(logs)[None, :]


def draw_teacher_z(key, part):
    values = jnp.clip(jax.random.normal(jax.random.fold_in(key, 11), (ROWS, B), jnp.float32), -6.0, 6.0)
    return values.astype(jnp.bfloat16)


def draw_proto_teacher(key, part):
    values = column_spread(key)
    return jnp.clip(values, -48.0, 48.0).astype(jnp.bfloat16)


def draw_proto_student(key, part):
    values = column_spread(jax.random.fold_in(key, 31))
    return jnp.clip(values, -48.0, 48.0).astype(jnp.bfloat16)


def touch_ends(entries, stream_key, least, high):
    spot = [jax.random.randint(jax.random.fold_in(stream_key, axis), (), 0, length) for axis, length in enumerate(entries.shape)]
    widest = entries.shape.index(max(entries.shape))
    next_to = spot[:widest] + [(spot[widest] + 1) % entries.shape[widest]] + spot[widest + 1:]
    return entries.at[tuple(spot)].set(least).at[tuple(next_to)].set(high)


def level_of(stream_key, dims, pieces, least, largest):
    loudness = 1.0
    for position, shards_of in pieces:
        steps = jax.random.uniform(jax.random.fold_in(jax.random.fold_in(stream_key, 6), position), (shards_of,), jnp.float32, least / len(pieces), largest / len(pieces))
        loudness = loudness * jnp.repeat(jnp.exp(steps), dims[position] // shards_of).reshape((-1,) + (1,) * (len(dims) - 1 - position))
    return loudness


def centred(rng, dims, spread, reach, shards=(), kind=jnp.bfloat16):
    values = jax.random.normal(rng, dims, jnp.float32) * spread
    if len(shards) > 0:
        values = level_of(rng, dims, shards, -0.22, 0.18) * values
    return jnp.clip(values, min=-reach, max=reach).astype(kind)


def setup_inputs(seed: int = 0) -> dict:
    key_of = jax.random.split(jax.random.key(seed), 9)
    return {
        "tokens": centred(key_of[0], (ROWS, D), 1.0, 6.0, ((0, 16),)),
        "w_in": centred(key_of[1], (D, H), D ** -0.5, 0.09375, ((0, 16), (1, 8))),
        "w_out": centred(key_of[2], (H, B), H ** -0.5, 0.0625, ((0, 8),)),
        "teacher_z": draw_teacher_z(jax.random.fold_in(key_of[8], 71), 0),
        "proto_student": draw_proto_student(jax.random.fold_in(key_of[8], 71), 0),
        "proto_teacher": draw_proto_teacher(jax.random.fold_in(key_of[8], 71), 0),
        "center": centred(key_of[6], (K,), 0.1, 0.6, ((0, 8),), jnp.float32),
        "image_of": touch_ends(jax.random.randint(key_of[7], (ROWS,), 0, IMAGES), jax.random.fold_in(key_of[7], 1), 0, IMAGES - 1).astype(jnp.int32),
    }


tau_teacher = 0.07
tau_student = 0.1
loss_scale = 1048576.0
norm_eps = 1e-06

def gelu_parts(values):
    cumul = 0.5 * (1.0 + jax.scipy.special.erf(values * 0.7071067811865476))
    density = jnp.exp(-0.5 * values * values) * 0.3989422804014327
    return (values * cumul, cumul + values * density)

def inner(left, right):
    return lax.dot_general(left, right, (((0,), (0,)), ((), ())), preferred_element_type=jnp.float32)

def outer_last(left, right):
    return lax.dot_general(left, right, (((1,), (1,)), ((), ())), preferred_element_type=jnp.float32)

def reference(tokens, w_in, w_out, teacher_z, proto_student, proto_teacher, center, image_of):
    pre = jnp.dot(tokens, w_in, preferred_element_type=jnp.float32)
    act, slope = gelu_parts(pre)
    hidden = act.astype(jnp.bfloat16)
    bott = jnp.dot(hidden, w_out, preferred_element_type=jnp.float32)
    recip = lax.rsqrt(lax.optimization_barrier(jnp.sum(bott * bott, axis=1, keepdims=True)) + norm_eps)
    unit = bott * recip
    student_n = unit.astype(jnp.bfloat16)
    teach = teacher_z.astype(jnp.float32)
    teacher_n = (teach * lax.rsqrt(lax.optimization_barrier(jnp.sum(teach * teach, axis=1, keepdims=True)) + norm_eps)).astype(jnp.bfloat16)
    onehot = (image_of[:, None] == jnp.arange(IMAGES, dtype=jnp.int32)[None, :]).astype(jnp.float32)
    counts = lax.optimization_barrier(jnp.sum(onehot, axis=0))
    weight = 1.0 / (IMAGES * lax.optimization_barrier(jnp.sum(onehot * counts[None, :], axis=1)))
    block = 128
    blocks = ROWS // block

    def one_block(carry, index):
        grad_acc, loss_acc = carry
        begin = index * block
        s_rows = lax.dynamic_slice_in_dim(student_n, begin, block, 0)
        t_rows = lax.dynamic_slice_in_dim(teacher_n, begin, block, 0)
        w_rows = lax.dynamic_slice_in_dim(weight, begin, block, 0)
        logit_t = (jnp.dot(t_rows, proto_teacher, preferred_element_type=jnp.float32) - center[None, :]) / tau_teacher
        logit_s = jnp.dot(s_rows, proto_student, preferred_element_type=jnp.float32) / tau_student
        prob_t = jax.nn.softmax(logit_t, axis=1)
        logp_s = jax.nn.log_softmax(logit_s, axis=1)
        cross = -lax.optimization_barrier(jnp.sum(prob_t * logp_s, axis=1))
        grad_s = (loss_scale * w_rows[:, None] * (jnp.exp(logp_s) - prob_t) / tau_student).astype(jnp.bfloat16)
        grad_acc = grad_acc + inner(s_rows, grad_s)
        dnorm = outer_last(grad_s, proto_student)
        return ((grad_acc, loss_acc + jnp.sum(w_rows * cross)), dnorm)
    start_carry = (jnp.zeros((B, K), jnp.float32), jnp.zeros((), jnp.float32))
    (proto_grad, loss), dnorm = lax.scan(one_block, start_carry, jnp.arange(blocks, dtype=jnp.int32))
    dnorm = dnorm.reshape(ROWS, B)
    dbott = (recip * (dnorm - unit * lax.optimization_barrier(jnp.sum(unit * dnorm, axis=1, keepdims=True)))).astype(jnp.bfloat16)
    w_out_grad = inner(hidden, dbott)
    dpre = (outer_last(dbott, w_out) * slope).astype(jnp.bfloat16)
    w_in_grad = inner(tokens, dpre)
    return (loss, w_in_grad, w_out_grad, proto_grad)
```

```python
import jax
import jax.numpy as jnp
from jax import lax
from jax.sharding import PartitionSpec as P
from jax.experimental import pallas as pl
from jax.experimental.pallas import tpu as pltpu

tau_teacher = 0.07
tau_student = 0.1
loss_scale = 1048576.0
norm_eps = 1e-06
MESH = pl.DeviceIdType.MESH
VMEM = pltpu.VMEM
f32 = jnp.float32
bf16 = jnp.bfloat16


def vspec():
    return pl.BlockSpec(memory_space=pltpu.VMEM)


def aspec():
    return pl.BlockSpec(memory_space=pl.ANY)


class Place:
    def __init__(self):
        self.r = lax.axis_index("row")
        self.p = lax.axis_index("proto")
        self.xh = self.r // 8
        self.y = (self.r // 2) % 4
        self.c = self.r % 2

    def chip(self, other, dy):
        fam = 1 - self.xh if other else self.xh
        return fam * 4 + (self.y + dy) % 4

    def slot(self, other, dy, core=None):
        return self.chip(other, dy) * 2 + (self.c if core is None else core)

    def dev(self, row):
        return (row, self.p)

    @property
    def X(self):
        return self.dev(self.slot(True, 0))

    @property
    def YP(self):
        return self.dev(self.slot(False, 1))

    @property
    def YM(self):
        return self.dev(self.slot(False, 3))

    @property
    def CO(self):
        return self.dev(self.slot(False, 0, 1 - self.c))

    def row_peer(self, d):
        return ((self.r + d) % 16, self.p)

    def proto_peer(self, d):
        return (self.r, (self.p + d) % 8)


class Copies:
    def __init__(self, send, recv):
        self.send, self.recv, self.all = send, recv, []

    def start(self, src, dst, dev):
        i = len(self.all)
        cp = pltpu.make_async_remote_copy(
            src_ref=src,
            dst_ref=dst,
            send_sem=self.send.at[i],
            recv_sem=self.recv.at[i],
            device_id=dev,
            device_id_type=MESH,
        )
        cp.start()
        self.all.append(cp)
        return cp

    def finish(self):
        for cp in self.all:
            cp.wait_send()


def greet(peers):
    bar = pltpu.get_barrier_semaphore()
    for dev in peers:
        pl.semaphore_signal(bar, inc=1, device_id=dev, device_id_type=MESH)


def met(count):
    pl.semaphore_wait(pltpu.get_barrier_semaphore(), count)


def gather_rows(cps, at, own, buf, a, h, al, work, tail=None):
    n = buf.shape[1]
    up, lo = pl.ds(h, n - h), pl.ds(0, h)
    A, B = pl.ds(0, a), pl.ds(a, n - a)
    aup, alo = pl.ds(al, a - al), pl.ds(0, al)
    me = at.slot(False, 0)
    x0 = cps.start(own, buf.at[me], at.X)
    p0 = cps.start(own, buf.at[me], at.YP)
    m0 = cps.start(own, buf.at[me], at.YM)
    c0 = cps.start(own, buf.at[me], at.CO)
    work("start", None)
    sx = at.slot(True, 0)
    sm, sp, sf = at.slot(False, 3), at.slot(False, 1), at.slot(False, 2)
    xm, xp, xf = at.slot(True, 3), at.slot(True, 1), at.slot(True, 2)
    x0.wait_recv()
    xap = cps.start(buf.at[sx, A], buf.at[sx, A], at.YP)
    xam = cps.start(buf.at[sx, A], buf.at[sx, A], at.YM)
    xc = cps.start(buf.at[sx], buf.at[sx], at.CO)
    p0.wait_recv()
    fup = cps.start(buf.at[sm, up], buf.at[sm, up], at.YP)
    bm = cps.start(buf.at[sm, B], buf.at[sm, B], at.X)
    cm = cps.start(buf.at[sm], buf.at[sm], at.CO)
    m0.wait_recv()
    flo = cps.start(buf.at[sp, lo], buf.at[sp, lo], at.YM)
    bp = cps.start(buf.at[sp, B], buf.at[sp, B], at.X)
    cp = cps.start(buf.at[sp], buf.at[sp], at.CO)
    c0.wait_recv()
    work("chip", at.chip(False, 0))
    xc.wait_recv()
    work("chip", at.chip(True, 0))
    fup.wait_recv()
    flo.wait_recv()
    bf = cps.start(buf.at[sf, B], buf.at[sf, B], at.X)
    cf = cps.start(buf.at[sf], buf.at[sf], at.CO)
    xap.wait_recv()
    gup = cps.start(buf.at[xm, aup], buf.at[xm, aup], at.YP)
    xam.wait_recv()
    glo = cps.start(buf.at[xp, alo], buf.at[xp, alo], at.YM)
    bm.wait_recv()
    cxm = cps.start(buf.at[xm], buf.at[xm], at.CO)
    bp.wait_recv()
    cxp = cps.start(buf.at[xp], buf.at[xp], at.CO)
    cm.wait_recv()
    work("chip", at.chip(False, 3))
    cp.wait_recv()
    work("chip", at.chip(False, 1))
    cf.wait_recv()
    work("chip", at.chip(False, 2))
    cxm.wait_recv()
    work("chip", at.chip(True, 3))
    cxp.wait_recv()
    work("chip", at.chip(True, 1))
    gup.wait_recv()
    glo.wait_recv()
    bf.wait_recv()
    cxf = cps.start(buf.at[xf], buf.at[xf], at.CO)
    cxf.wait_recv()
    work("chip", at.chip(True, 2))


def gelu_parts(values):
    cumul = 0.5 * (1.0 + lax.erf(values * 0.7071067811865476))
    density = jnp.exp(-0.5 * values * values) * 0.3989422804014327
    return (values * cumul, cumul + values * density)


def head_kernel(
    tokens, w_in, w_out, teacher, proto_t, center, img,
    hid_o, slope_o, sn_o, unit_o, recip_o, et_o, mt_o, st_o, wt_o,
    tok, wbuf, pt, lt, pre, tbuf, cbuf, part, rbuf, sbuf, send, recv, lsem,
):
    at = Place()
    cps = Copies(send, recv)
    rows, depth = tok.shape
    peers = [at.row_peer(d) for d in range(1, 16)] + [at.proto_peer(d) for d in range(1, 8)]
    greet(peers)
    me = at.slot(False, 0)
    own = pltpu.make_async_copy(w_in, wbuf.at[me], lsem.at[0])
    own.start()
    load_pt = pltpu.make_async_copy(proto_t, pt, lsem.at[1])
    load_pt.start()
    load_tok = pltpu.make_async_copy(tokens, tok, lsem.at[2])
    load_tok.start()
    lanes = lax.broadcasted_iota(jnp.int32, img.shape, 1)
    onehot = (img[...] == lanes).astype(f32)
    cbuf[at.r] = jnp.broadcast_to(jnp.sum(onehot, axis=0, keepdims=True), (8, 128))
    t = teacher[...].astype(f32)
    tbuf[at.p] = (t * lax.rsqrt(jnp.sum(t * t, axis=1, keepdims=True) + norm_eps)).astype(bf16)
    pre[...] = jnp.zeros_like(pre)
    met(len(peers))

    def scores():
        tc = [cps.start(tbuf.at[at.p], tbuf.at[at.p], at.proto_peer(d)) for d in range(1, 8)]
        cc = [cps.start(cbuf.at[at.r], cbuf.at[at.r], at.row_peer(d)) for d in range(1, 16)]
        load_pt.wait()
        for k in tc:
            k.wait_recv()
        tn = tbuf[...].reshape(rows, tbuf.shape[2])
        step = 512

        def one(j, top):
            cols = pl.ds(pl.multiple_of(j * step, step), step)
            v = jnp.dot(tn, pt[:, cols], preferred_element_type=f32)
            v = (v - center[:, cols]) * (1.0 / tau_teacher)
            lt[:, cols] = v
            for q in range(step // 128):
                top = jnp.maximum(top, v[:, q * 128 : (q + 1) * 128])
            return top

        mt_o[...] = lax.fori_loop(
            0, lt.shape[1] // step, one, jnp.full((rows, 128), -jnp.inf, f32)
        )
        mt_o[...] = jnp.broadcast_to(jnp.max(mt_o[...], axis=1, keepdims=True), (rows, 128))
        st_o[...] = jnp.zeros_like(st_o)

        def two(j, _):
            cols = pl.ds(pl.multiple_of(j * 128, 128), 128)
            e = jnp.exp(lt[:, cols] - mt_o[...])
            lt[:, cols] = e
            st_o[...] += e
            return 0

        lax.fori_loop(0, lt.shape[1] // 128, two, 0)
        for k in cc:
            k.wait_recv()
        counts = jnp.sum(cbuf[...], axis=0)[0:1]
        per_row = jnp.sum(onehot * counts, axis=1, keepdims=True)
        wt_o[...] = jnp.broadcast_to(1.0 / (64.0 * per_row), wt_o.shape)

    save = pltpu.make_async_copy(lt, et_o, lsem.at[3])

    def work(kind, chip):
        if kind == "start":
            scores()
            save.start()
            own.wait()
            load_tok.wait()
            return
        block = wbuf.shape[1] * 2
        lhs = tok[:, pl.ds(pl.multiple_of(chip * block, block), block)]

        def tile(j, _):
            cols = pl.ds(pl.multiple_of(j * 256, 256), 256)
            rhs = wbuf[pl.ds(chip * 2, 2), :, cols].reshape(block, 256)
            pre[:, cols] += jnp.dot(lhs, rhs, preferred_element_type=f32)
            return 0

        lax.fori_loop(0, pre.shape[1] // 256, tile, 0)

    gather_rows(cps, at, w_in, wbuf, 144, 128, 64, work)

    small = part.shape[1]

    def act(i, _):
        rs = pl.ds(pl.multiple_of(i * small, small), small)
        value, slope = gelu_parts(pre[rs, :])
        slope_o[rs, :] = slope
        h = value.astype(bf16)
        hid_o[rs, :] = h
        part[i] = jnp.dot(h, w_out[...], preferred_element_type=f32)
        return 0

    lax.fori_loop(0, rows // small, act, 0)
    rc = [
        cps.start(part.at[(at.p + d) % 8], rbuf.at[d], at.proto_peer(d)) for d in range(1, 8)
    ]
    total = part[at.p]
    for d in range(1, 8):
        rc[d - 1].wait_recv()
        total = total + rbuf[d]
    recip = lax.rsqrt(jnp.sum(total * total, axis=1, keepdims=True) + norm_eps)
    unit = total * recip
    unit_o[...] = unit
    recip_o[...] = jnp.broadcast_to(recip, recip_o.shape)
    sbuf[at.p] = unit.astype(bf16)
    sc = [cps.start(sbuf.at[at.p], sbuf.at[at.p], at.proto_peer(d)) for d in range(1, 8)]
    for k in sc:
        k.wait_recv()
    sn_o[...] = sbuf[...].reshape(rows, sbuf.shape[2])
    save.wait()
    cps.finish()


def head(tokens, w_in, w_out, teacher_z, proto_teacher, center, image_of):
    rows, depth = tokens.shape
    hid = w_in.shape[1]
    wide = w_out.shape[1]
    kk = proto_teacher.shape[1]
    img = jnp.broadcast_to(image_of[:, None], (rows, 128))
    small = teacher_z.shape[0]
    shp = jax.ShapeDtypeStruct
    copies = 20 + 7 + 15 + 7 + 7
    return pl.pallas_call(
        head_kernel,
        out_shape=(
            shp((rows, hid), bf16), shp((rows, hid), f32), shp((rows, wide), bf16),
            shp((small, wide), f32), shp((small, 128), f32), shp((rows, kk), f32),
            shp((rows, 128), f32), shp((rows, 128), f32), shp((rows, 128), f32),
        ),
        in_specs=[aspec(), aspec(), vspec(), vspec(), aspec(), vspec(), vspec()],
        out_specs=(vspec(),) * 5 + (aspec(),) + (vspec(),) * 3,
        scratch_shapes=[
            VMEM((rows, depth), bf16), VMEM((16,) + w_in.shape, bf16),
            VMEM(proto_teacher.shape, bf16), VMEM((rows, kk), f32), VMEM((rows, hid), f32),
            VMEM((8, small, wide), bf16), VMEM((16, 8, 128), f32), VMEM((8, small, wide), f32),
            VMEM((8, small, wide), f32), VMEM((8, small, wide), bf16),
            pltpu.SemaphoreType.DMA((copies,)), pltpu.SemaphoreType.DMA((copies,)),
            pltpu.SemaphoreType.DMA((4,)),
        ],
        compiler_params=pltpu.CompilerParams(
            collective_id=0, has_side_effects=True, vmem_limit_bytes=62 * 2**20
        ),
        name="head",
    )(tokens, w_in, w_out, teacher_z, proto_teacher, center[None, :], img)


def inner(left, right):
    return lax.dot_general(
        left, right, (((0,), (0,)), ((), ())), preferred_element_type=jnp.float32
    )


def outer_last(left, right):
    return lax.dot_general(
        left, right, (((1,), (1,)), ((), ())), preferred_element_type=jnp.float32
    )


def on_device(tokens, w_in, w_out, teacher_z, proto_student, proto_teacher, center, image_of):
    hidden, slope, student_n, unit, recip, exp_t, mt, st, wt = head(
        tokens, w_in, w_out, teacher_z, proto_teacher, center, image_of
    )
    recip = recip[:, :1]
    weight = wt[:, 0]
    local_t = mt[:, 0]
    logit_s = jnp.dot(student_n, proto_student, preferred_element_type=jnp.float32) / tau_student
    local_s = jnp.max(logit_s, axis=1)
    top_t, top_s = lax.pmax((local_t, local_s), "proto")
    fix = jnp.exp(local_t - top_t)
    exp_t = exp_t * fix[:, None]
    exp_s = jnp.exp(logit_s - top_s[:, None])
    total_t, total_s = lax.psum((jnp.sum(st, axis=1) * fix, jnp.sum(exp_s, axis=1)), "proto")
    prob_t = exp_t / total_t[:, None]
    prob_s = exp_s / total_s[:, None]
    logp_s = logit_s - top_s[:, None] - jnp.log(total_s)[:, None]
    cross = -jnp.sum(prob_t * logp_s, axis=1)
    loss = lax.psum(jnp.sum(weight * cross), ("row", "proto"))
    grad_s = (loss_scale * weight[:, None] * (prob_s - prob_t) / tau_student).astype(jnp.bfloat16)
    proto_grad = lax.psum_scatter(
        inner(student_n, grad_s).astype(jnp.bfloat16), "row", scatter_dimension=0, tiled=True
    ).astype(jnp.float32)
    dnorm = lax.psum_scatter(outer_last(grad_s, proto_student), "proto", scatter_dimension=0, tiled=True)
    dbott = (recip * (dnorm - unit * jnp.sum(unit * dnorm, axis=1, keepdims=True))).astype(bf16)
    dbott = lax.all_gather(dbott, "proto", axis=0, tiled=True)
    w_out_grad = lax.psum(inner(hidden, dbott).astype(jnp.bfloat16), "row").astype(jnp.float32)
    dpre = (outer_last(dbott, w_out) * slope).astype(jnp.bfloat16)
    w_in_grad = lax.psum_scatter(
        inner(tokens, dpre).astype(jnp.bfloat16), "row", scatter_dimension=0, tiled=True
    ).astype(jnp.float32)
    return (loss, w_in_grad, w_out_grad, proto_grad)


def solution(mesh):
    return jax.shard_map(
        on_device,
        mesh=mesh,
        in_specs=(
            P("row", None),
            P("row", "proto"),
            P("proto", None),
            P(("row", "proto"), None),
            P(None, "proto"),
            P(None, "proto"),
            P("proto"),
            P("row"),
        ),
        out_specs=(P(), P("row", "proto"), P("proto", None), P("row", "proto")),
        check_vma=False,
    )
```

```python
import jax
import jax.numpy as jnp
from jax import lax
from jax.sharding import PartitionSpec as P
from jax.experimental import pallas as pl
from jax.experimental.pallas import tpu as pltpu

tau_teacher = 0.07
tau_student = 0.1
loss_scale = 1048576.0
norm_eps = 1e-06
MESH = pl.DeviceIdType.MESH
VMEM = pltpu.VMEM
f32 = jnp.float32
bf16 = jnp.bfloat16


def vspec():
    return pl.BlockSpec(memory_space=pltpu.VMEM)


def aspec():
    return pl.BlockSpec(memory_space=pl.ANY)


class Place:
    def __init__(self):
        self.r = lax.axis_index("row")
        self.p = lax.axis_index("proto")
        self.xh = self.r // 8
        self.y = (self.r // 2) % 4
        self.c = self.r % 2

    def chip(self, other, dy):
        fam = 1 - self.xh if other else self.xh
        return fam * 4 + (self.y + dy) % 4

    def slot(self, other, dy, core=None):
        return self.chip(other, dy) * 2 + (self.c if core is None else core)

    def dev(self, row):
        return (row, self.p)

    @property
    def X(self):
        return self.dev(self.slot(True, 0))

    @property
    def YP(self):
        return self.dev(self.slot(False, 1))

    @property
    def YM(self):
        return self.dev(self.slot(False, 3))

    @property
    def CO(self):
        return self.dev(self.slot(False, 0, 1 - self.c))

    def row_peer(self, d):
        return ((self.r + d) % 16, self.p)

    def proto_peer(self, d):
        return (self.r, (self.p + d) % 8)


class Copies:
    def __init__(self, send, recv):
        self.send, self.recv, self.all = send, recv, []

    def start(self, src, dst, dev):
        i = len(self.all)
        cp = pltpu.make_async_remote_copy(
            src_ref=src,
            dst_ref=dst,
            send_sem=self.send.at[i],
            recv_sem=self.recv.at[i],
            device_id=dev,
            device_id_type=MESH,
        )
        cp.start()
        self.all.append(cp)
        return cp

    def finish(self):
        for cp in self.all:
            cp.wait_send()


def greet(peers):
    bar = pltpu.get_barrier_semaphore()
    for dev in peers:
        pl.semaphore_signal(bar, inc=1, device_id=dev, device_id_type=MESH)


def met(count):
    pl.semaphore_wait(pltpu.get_barrier_semaphore(), count)


def gather_rows(cps, at, own, buf, a, h, al):
    n = buf.shape[1]
    up, lo = pl.ds(h, n - h), pl.ds(0, h)
    A, B = pl.ds(0, a), pl.ds(a, n - a)
    aup, alo = pl.ds(al, a - al), pl.ds(0, al)

    def on(slot, part, dev):
        ref = buf.at[slot] if part is None else buf.at[slot, part]
        return cps.start(ref, ref, dev)

    me = at.slot(False, 0)
    x0 = cps.start(own, buf.at[me], at.X)
    p0 = cps.start(own, buf.at[me], at.YP)
    m0 = cps.start(own, buf.at[me], at.YM)
    c0 = cps.start(own, buf.at[me], at.CO)
    yield [(c0, at.chip(False, 0))]
    sx = at.slot(True, 0)
    sm, sp, sf = at.slot(False, 3), at.slot(False, 1), at.slot(False, 2)
    xm, xp, xf = at.slot(True, 3), at.slot(True, 1), at.slot(True, 2)
    x0.wait_recv()
    xap = on(sx, A, at.YP)
    xam = on(sx, A, at.YM)
    xc = on(sx, None, at.CO)
    p0.wait_recv()
    fup = on(sm, up, at.YP)
    bm = on(sm, B, at.X)
    cm = on(sm, None, at.CO)
    m0.wait_recv()
    flo = on(sp, lo, at.YM)
    bp = on(sp, B, at.X)
    cp = on(sp, None, at.CO)
    yield [(xc, at.chip(True, 0)), (cm, at.chip(False, 3)), (cp, at.chip(False, 1))]
    fup.wait_recv()
    flo.wait_recv()
    bf = on(sf, B, at.X)
    cf = on(sf, None, at.CO)
    xap.wait_recv()
    gup = on(xm, aup, at.YP)
    xam.wait_recv()
    glo = on(xp, alo, at.YM)
    bm.wait_recv()
    cxm = on(xm, None, at.CO)
    bp.wait_recv()
    cxp = on(xp, None, at.CO)
    yield [(cf, at.chip(False, 2)), (cxm, at.chip(True, 3)), (cxp, at.chip(True, 1))]
    gup.wait_recv()
    glo.wait_recv()
    bf.wait_recv()
    cxf = on(xf, None, at.CO)
    yield [(cxf, at.chip(True, 2))]


def gelu_parts(values):
    cumul = 0.5 * (1.0 + lax.erf(values * 0.7071067811865476))
    density = jnp.exp(-0.5 * values * values) * 0.3989422804014327
    return (values * cumul, cumul + values * density)


class Scatter:
    def __init__(self, cps, at, S, bufs, axis, a, al, bl):
        self.cps, self.at, self.S, self.axis = cps, at, S, axis
        self.far, self.nm, self.np, self.xb, self.xa = bufs
        n = S.shape[1 + axis]
        self.A, self.B = (0, a), (a, n - a)
        self.Alo, self.Aup = (0, al), (al, a - al)
        self.Blo, self.Bup = (a, bl), (a + bl, n - a - bl)
        self.got = {}

    def idx(self, i, part):
        cut = pl.ds(*part)
        return (i, cut) if self.axis == 0 else (i, slice(None), cut)

    def send(self, key, g, dst, i, part, dev):
        self.got[key] = self.cps.start(
            self.S.at[self.idx(g, part)], dst.at[self.idx(i, part)], dev
        )

    def add(self, g, part, *terms):
        where = self.idx(g, part)
        v = self.S[where].astype(f32)
        for ref, i in terms:
            v = v + ref[self.idx(i, part)].astype(f32)
        self.S[where] = v.astype(bf16)

    def wait(self, key):
        self.got[key].wait_recv()

    def ready(self, other, dy):
        g, k = self.at.chip(other, dy), int(other)
        if other:
            self.send(("x", dy), g, self.xb, dy, self.B, self.at.X)
        if dy == 2:
            self.send(("fu", k), g, self.far, k, self.Aup, self.at.YP)
            self.send(("fl", k), g, self.far, k, self.Alo, self.at.YM)
        if dy == 1:
            self.send(("ml", k), g, self.nm, k, self.Alo, self.at.YP)
        if dy == 3:
            self.send(("pu", k), g, self.np, k, self.Aup, self.at.YM)

    def mid_a(self, k):
        g1, g3 = self.at.chip(bool(k), 1), self.at.chip(bool(k), 3)
        self.wait(("fu", k))
        self.add(g1, self.Aup, (self.far, k))
        self.send(("mu", k), g1, self.nm, k, self.Aup, self.at.YP)
        self.wait(("fl", k))
        self.add(g3, self.Alo, (self.far, k))
        self.send(("pl", k), g3, self.np, k, self.Alo, self.at.YM)

    def mid_b(self):
        for dy in (2, 1, 3):
            g = self.at.chip(False, dy)
            self.wait(("x", dy))
            self.add(g, self.B, (self.xb, dy))
            if dy == 2:
                self.send("bfu", g, self.far, 0, self.Bup, self.at.YP)
                self.send("bfl", g, self.far, 0, self.Blo, self.at.YM)
            elif dy == 1:
                self.send("bml", g, self.nm, 0, self.Blo, self.at.YP)
            else:
                self.send("bpu", g, self.np, 0, self.Bup, self.at.YM)

    def late_a(self):
        for key in ("ml", "mu", "pl", "pu"):
            self.wait((key, 1))
        g = self.at.chip(True, 0)
        self.add(g, self.A, (self.nm, 1), (self.np, 1))
        self.send("xa", g, self.xa, 0, self.A, self.at.X)

    def late_b(self):
        g1, g3 = self.at.chip(False, 1), self.at.chip(False, 3)
        self.wait("bfu")
        self.add(g1, self.Bup, (self.far, 0))
        self.send("bmu", g1, self.nm, 0, self.Bup, self.at.YP)
        self.wait("bfl")
        self.add(g3, self.Blo, (self.far, 0))
        self.send("bpl", g3, self.np, 0, self.Blo, self.at.YM)

    def final(self, fin):
        g = self.at.chip(False, 0)
        for key in ("ml", "mu", "pl", "pu"):
            self.wait((key, 0))
        for key in ("xa", ("x", 0), "bml", "bmu", "bpl", "bpu"):
            self.wait(key)
        for part, last, i in ((self.A, self.xa, 0), (self.B, self.xb, 0)):
            v = self.S[self.idx(g, part)].astype(f32)
            for ref, j in ((self.nm, 0), (self.np, 0), (last, i)):
                v = v + ref[self.idx(j, part)].astype(f32)
            fin[self.idx(0, part)[1:]] = v


def scatter_bufs(shape):
    return [VMEM((n,) + shape, bf16) for n in (2, 2, 2, 4, 1)]


ORDER = [(True, 2), (True, 1), (True, 3), (True, 0), (False, 2), (False, 1), (False, 3), (False, 0)]


def head_kernel(
    tokens, w_in, w_out, teacher, proto_t, center, img,
    hid_o, slope_o, sn_o, unit_o, recip_o, et_o, mt_o, st_o, wt_o,
    tok, wbuf, pt, lt, pre, tbuf, cbuf, part, rbuf, sbuf, send, recv, lsem,
):
    at = Place()
    cps = Copies(send, recv)
    rows, depth = tok.shape
    peers = [at.row_peer(d) for d in range(1, 16)] + [at.proto_peer(d) for d in range(1, 8)]
    greet(peers)
    me = at.slot(False, 0)
    own = pltpu.make_async_copy(w_in, wbuf.at[me], lsem.at[0])
    own.start()
    load_pt = pltpu.make_async_copy(proto_t, pt, lsem.at[1])
    load_pt.start()
    load_tok = pltpu.make_async_copy(tokens, tok, lsem.at[2])
    load_tok.start()
    lanes = lax.broadcasted_iota(jnp.int32, img.shape, 1)
    onehot = (img[...] == lanes).astype(f32)
    cbuf[at.r] = jnp.broadcast_to(jnp.sum(onehot, axis=0, keepdims=True), (8, 128))
    t = teacher[...].astype(f32)
    tbuf[at.p] = (t * lax.rsqrt(jnp.sum(t * t, axis=1, keepdims=True) + norm_eps)).astype(bf16)
    pre[...] = jnp.zeros_like(pre)
    met(len(peers))

    def scores():
        tc = [cps.start(tbuf.at[at.p], tbuf.at[at.p], at.proto_peer(d)) for d in range(1, 8)]
        cc = [cps.start(cbuf.at[at.r], cbuf.at[at.r], at.row_peer(d)) for d in range(1, 16)]
        load_pt.wait()
        for k in tc:
            k.wait_recv()
        tn = tbuf[...].reshape(rows, tbuf.shape[2])
        step = 512

        def one(j, top):
            cols = pl.ds(pl.multiple_of(j * step, step), step)
            v = jnp.dot(tn, pt[:, cols], preferred_element_type=f32)
            v = (v - center[:, cols]) * (1.0 / tau_teacher)
            lt[:, cols] = v
            for q in range(step // 128):
                top = jnp.maximum(top, v[:, q * 128 : (q + 1) * 128])
            return top

        mt_o[...] = lax.fori_loop(
            0, lt.shape[1] // step, one, jnp.full((rows, 128), -jnp.inf, f32)
        )
        mt_o[...] = jnp.broadcast_to(jnp.max(mt_o[...], axis=1, keepdims=True), (rows, 128))
        st_o[...] = jnp.zeros_like(st_o)

        def two(j, _):
            cols = pl.ds(pl.multiple_of(j * 128, 128), 128)
            e = jnp.exp(lt[:, cols] - mt_o[...])
            lt[:, cols] = e
            st_o[...] += e
            return 0

        lax.fori_loop(0, lt.shape[1] // 128, two, 0)
        for k in cc:
            k.wait_recv()
        counts = jnp.sum(cbuf[...], axis=0)[0:1]
        per_row = jnp.sum(onehot * counts, axis=1, keepdims=True)
        wt_o[...] = jnp.broadcast_to(1.0 / (64.0 * per_row), wt_o.shape)

    save = pltpu.make_async_copy(lt, et_o, lsem.at[3])

    def accumulate(chip):
        block = wbuf.shape[1] * 2
        lhs = tok[:, pl.ds(pl.multiple_of(chip * block, block), block)]

        def tile(j, _):
            cols = pl.ds(pl.multiple_of(j * 256, 256), 256)
            rhs = wbuf[pl.ds(chip * 2, 2), :, cols].reshape(block, 256)
            pre[:, cols] += jnp.dot(lhs, rhs, preferred_element_type=f32)
            return 0

        lax.fori_loop(0, pre.shape[1] // 256, tile, 0)

    first = True
    for landed in gather_rows(cps, at, w_in, wbuf, 144, 128, 64):
        if first:
            scores()
            save.start()
            own.wait()
            load_tok.wait()
            first = False
        for copy, chip in landed:
            copy.wait_recv()
            accumulate(chip)

    small = part.shape[1]

    def act(i, _):
        rs = pl.ds(pl.multiple_of(i * small, small), small)
        value, slope = gelu_parts(pre[rs, :])
        slope_o[rs, :] = slope
        h = value.astype(bf16)
        hid_o[rs, :] = h
        part[i] = jnp.dot(h, w_out[...], preferred_element_type=f32)
        return 0

    lax.fori_loop(0, rows // small, act, 0)
    rc = [
        cps.start(part.at[(at.p + d) % 8], rbuf.at[d], at.proto_peer(d)) for d in range(1, 8)
    ]
    total = part[at.p]
    for d in range(1, 8):
        rc[d - 1].wait_recv()
        total = total + rbuf[d]
    recip = lax.rsqrt(jnp.sum(total * total, axis=1, keepdims=True) + norm_eps)
    unit = total * recip
    unit_o[...] = unit
    recip_o[...] = jnp.broadcast_to(recip, recip_o.shape)
    sbuf[at.p] = unit.astype(bf16)
    sc = [cps.start(sbuf.at[at.p], sbuf.at[at.p], at.proto_peer(d)) for d in range(1, 8)]
    for k in sc:
        k.wait_recv()
    sn_o[...] = sbuf[...].reshape(rows, sbuf.shape[2])
    save.wait()
    cps.finish()


def head(tokens, w_in, w_out, teacher_z, proto_teacher, center, image_of):
    rows, depth = tokens.shape
    hid = w_in.shape[1]
    wide = w_out.shape[1]
    kk = proto_teacher.shape[1]
    img = jnp.broadcast_to(image_of[:, None], (rows, 128))
    small = teacher_z.shape[0]
    shp = jax.ShapeDtypeStruct
    copies = 20 + 7 + 15 + 7 + 7
    return pl.pallas_call(
        head_kernel,
        out_shape=(
            shp((rows, hid), bf16), shp((rows, hid), f32), shp((rows, wide), bf16),
            shp((small, wide), f32), shp((small, 128), f32), shp((rows, kk), f32),
            shp((rows, 128), f32), shp((rows, 128), f32), shp((rows, 128), f32),
        ),
        in_specs=[aspec(), aspec(), vspec(), vspec(), aspec(), vspec(), vspec()],
        out_specs=(vspec(),) * 5 + (aspec(),) + (vspec(),) * 3,
        scratch_shapes=[
            VMEM((rows, depth), bf16), VMEM((16,) + w_in.shape, bf16),
            VMEM(proto_teacher.shape, bf16), VMEM((rows, kk), f32), VMEM((rows, hid), f32),
            VMEM((8, small, wide), bf16), VMEM((16, 8, 128), f32), VMEM((8, small, wide), f32),
            VMEM((8, small, wide), f32), VMEM((8, small, wide), bf16),
            pltpu.SemaphoreType.DMA((copies,)), pltpu.SemaphoreType.DMA((copies,)),
            pltpu.SemaphoreType.DMA((4,)),
        ],
        compiler_params=pltpu.CompilerParams(
            collective_id=0, has_side_effects=True, vmem_limit_bytes=62 * 2**20
        ),
        name="head",
    )(tokens, w_in, w_out, teacher_z, proto_teacher, center[None, :], img)


def across(row):
    return jnp.transpose(jnp.broadcast_to(row, (128, row.shape[1])))


def along(col):
    return jnp.transpose(col)


def middle_kernel(
    sn, proto_s, et_in, mt, st, wt, unit, recip,
    dbott_o, pgrad_o, loss_o,
    ps, et, ls, gs, snt, ms, ss, cs, stats, fsb, ftb, S, snd, rc, far, nm, np_, xb, xa, fin, fcore,
    dpart, drecv, dbuf, send, recv, lsem,
):
    at = Place()
    cps = Copies(send, recv)
    rows, kk = ls.shape
    half = kk // 2
    peers = [at.proto_peer(d) for d in range(1, 8)] + [at.X, at.YP, at.YM, at.CO]
    greet(peers)
    load_ps = pltpu.make_async_copy(proto_s, ps, lsem.at[0])
    load_ps.start()
    load_et = pltpu.make_async_copy(et_in, et, lsem.at[1])
    load_et.start()
    snt[...] = jnp.transpose(sn[...])
    load_ps.wait()
    step = 512

    def one(j, top):
        cols = pl.ds(pl.multiple_of(j * step, step), step)
        v = jnp.dot(sn[...], ps[:, cols], preferred_element_type=f32) * (1.0 / tau_student)
        ls[:, cols] = v
        for q in range(step // 128):
            top = jnp.maximum(top, v[:, q * 128 : (q + 1) * 128])
        return top

    ms[...] = lax.fori_loop(0, kk // step, one, jnp.full((rows, 128), -jnp.inf, f32))
    ms[...] = jnp.broadcast_to(jnp.max(ms[...], axis=1, keepdims=True), (rows, 128))
    ss[...] = jnp.zeros_like(ss)
    cs[...] = jnp.zeros_like(cs)
    load_et.wait()

    def two(j, _):
        cols = pl.ds(pl.multiple_of(j * 128, 128), 128)
        d = ls[:, cols] - ms[...]
        e = jnp.exp(d)
        ls[:, cols] = e
        ss[...] += e
        cs[...] += et[:, cols] * d
        return 0

    lax.fori_loop(0, kk // 128, two, 0)
    stats[at.p] = jnp.concatenate(
        [
            along(mt[...])[0:1],
            jnp.sum(along(st[...]), axis=0, keepdims=True),
            along(ms[...])[0:1],
            jnp.sum(along(ss[...]), axis=0, keepdims=True),
            jnp.sum(along(cs[...]), axis=0, keepdims=True),
            jnp.zeros((3, rows), f32),
        ],
        axis=0,
    )
    met(len(peers))
    sc = [cps.start(stats.at[at.p], stats.at[at.p], at.proto_peer(d)) for d in range(1, 8)]
    for k in sc:
        k.wait_recv()
    table = [stats[q] for q in range(8)]
    top_t = table[0][0:1]
    top_s = table[0][2:3]
    for q in table[1:]:
        top_t = jnp.maximum(top_t, q[0:1])
        top_s = jnp.maximum(top_s, q[2:3])
    total_t = total_s = cross = jnp.zeros((1, rows), f32)
    for q in table:
        scale = jnp.exp(q[0:1] - top_t)
        total_t = total_t + q[1:2] * scale
        total_s = total_s + q[3:4] * jnp.exp(q[2:3] - top_s)
        cross = cross + scale * (q[4:5] + q[1:2] * (q[2:3] - top_s))
    cross = jnp.log(total_s) - cross / total_t
    w_row = along(wt[...])[0:1]
    loss_o[...] = jnp.broadcast_to(w_row * cross, loss_o.shape)
    mine = stats[at.p]
    lift = (loss_scale / tau_student) * w_row
    fsb[...] = across(lift * jnp.exp(mine[2:3] - top_s) / total_s)
    ftb[...] = across(lift * jnp.exp(mine[0:1] - top_t) / total_t)
    dpart[...] = jnp.zeros_like(dpart)

    def grads(base, dst):
        def one(j, _):
            first = base + j * step
            for q in range(step // 128):
                cols = pl.ds(pl.multiple_of(first + q * 128, 128), 128)
                v = ls[:, cols] * fsb[...] - et[:, cols] * ftb[...]
                gs[:, q * 128 : (q + 1) * 128] = v.astype(bf16)
            cols = pl.ds(pl.multiple_of(first, step), step)
            g = gs[...]
            v = jnp.dot(snt[...], g, preferred_element_type=f32)
            dst[:, :, pl.ds(pl.multiple_of(j * step, step), step)] = v.astype(bf16).reshape(
                dst.shape[0], dst.shape[1], step
            )
            d = lax.dot_general(
                g, ps[:, cols], (((1,), (1,)), ((), ())), preferred_element_type=f32
            )
            dpart[...] += d.reshape(dpart.shape)
            return 0

        lax.fori_loop(0, half // step, one, 0)

    grads((1 - at.c) * half, snd)
    swap = cps.start(snd, rc, at.CO)
    grads(at.c * half, S)
    dc = [
        cps.start(dpart.at[(at.p + d) % 8], drecv.at[d], at.proto_peer(d)) for d in range(1, 8)
    ]
    swap.wait_recv()
    rs = Scatter(cps, at, S, (far, nm, np_, xb, xa), 1, 1792, 768, 640)
    for other, dy in ORDER:
        g = at.chip(other, dy)
        S[g] = (S[g].astype(f32) + rc[g].astype(f32)).astype(bf16)
        rs.ready(other, dy)
    rs.mid_a(1)
    total = dpart[at.p]
    for d in range(1, 8):
        dc[d - 1].wait_recv()
        total = total + drecv[d]
    u, r = unit[...], recip[:, 0:1]
    dbuf[at.p] = (r * (total - u * jnp.sum(u * total, axis=1, keepdims=True))).astype(bf16)
    bc = [cps.start(dbuf.at[at.p], dbuf.at[at.p], at.proto_peer(d)) for d in range(1, 8)]
    rs.mid_b()
    rs.mid_a(0)
    rs.late_a()
    rs.late_b()
    for k in bc:
        k.wait_recv()
    dbott_o[...] = dbuf[...].reshape(dbott_o.shape)
    rs.final(fin)
    n = fcore.shape[0]
    keep, give = at.c * n, (1 - at.c) * n
    fc = cps.start(fin.at[pl.ds(pl.multiple_of(give, 8), n)], fcore, at.CO)
    pgrad_o[:, pl.ds(pl.multiple_of(at.c * half, half), half)] = fin[pl.ds(pl.multiple_of(keep, 8), n), :]
    fc.wait_recv()
    pgrad_o[:, pl.ds(pl.multiple_of((1 - at.c) * half, half), half)] = fcore[...]
    cps.finish()


def middle(sn, proto_s, et, mt, st, wt, unit, recip):
    rows, wide = sn.shape
    kk = proto_s.shape[1]
    small = unit.shape[0]
    shp = jax.ShapeDtypeStruct
    chunk = (wide // 8, kk // 2)
    copies = 7 + 1 + 7 + 7 + 23 + 1
    lane = VMEM((rows, 128), f32)
    return pl.pallas_call(
        middle_kernel,
        out_shape=(shp((rows, wide), bf16), shp((wide // 16, kk), f32), shp((8, rows), f32)),
        in_specs=[vspec(), aspec(), aspec()] + [vspec()] * 5,
        out_specs=(vspec(),) * 3,
        scratch_shapes=[
            VMEM((wide, kk), bf16), VMEM((rows, kk), f32), VMEM((rows, kk), f32), VMEM((rows, 512), bf16),
            VMEM((wide, rows), bf16), lane, lane, lane, VMEM((8, 8, rows), f32), lane, lane,
            VMEM((8,) + chunk, bf16), VMEM((8,) + chunk, bf16), VMEM((8,) + chunk, bf16),
            *scatter_bufs(chunk), VMEM(chunk, f32), VMEM((chunk[0] // 2, chunk[1]), f32),
            VMEM((8, small, wide), f32), VMEM((8, small, wide), f32), VMEM((8, small, wide), bf16),
            pltpu.SemaphoreType.DMA((copies,)), pltpu.SemaphoreType.DMA((copies,)),
            pltpu.SemaphoreType.DMA((2,)),
        ],
        compiler_params=pltpu.CompilerParams(
            collective_id=1, has_side_effects=True, vmem_limit_bytes=62 * 2**20
        ),
        name="middle",
    )(sn, proto_s, et, mt, st, wt, unit, recip)


def tail_kernel(
    tokens, hid, slope_in, dbott, w_out, loss_in,
    wgrad_o, wout_o, loss_o,
    tok, slope, dp, S, snd, rc, far, nm, np_, xb, xa, fin, fcore,
    W, S2, rc2, far2, nm2, np2, xb2, xa2, fin2, own2, wbuf, lbuf, send, recv, lsem,
):
    at = Place()
    cps = Copies(send, recv)
    rows, hidden = dp.shape
    half = hidden // 2
    peers = [at.row_peer(d) for d in range(1, 16)]
    greet(peers)
    load_tok = pltpu.make_async_copy(tokens, tok, lsem.at[0])
    load_tok.start()
    load_slope = pltpu.make_async_copy(slope_in, slope, lsem.at[1])
    load_slope.start()
    lbuf[at.r] = jnp.broadcast_to(
        jnp.sum(loss_in[...], axis=1, keepdims=True), lbuf.shape[1:]
    )
    small = W.shape[2]
    for j in range(hidden // 256):
        cols = slice(j * 256, (j + 1) * 256)
        v = lax.dot_general(
            hid[:, cols], dbott[...], (((0,), (0,)), ((), ())), preferred_element_type=f32
        ).astype(bf16)
        for i in range(256 // small):
            k = j * (256 // small) + i
            W[k % 2, k // 2] = v[i * small : (i + 1) * small]
    met(len(peers))
    lc = [cps.start(lbuf.at[at.r], lbuf.at[at.r], at.row_peer(d)) for d in range(1, 16)]
    swap2 = cps.start(W.at[1 - at.c], rc2, at.CO)
    load_slope.wait()

    def back(j, _):
        cols = pl.ds(pl.multiple_of(j * 256, 256), 256)
        v = lax.dot_general(
            dbott[...], w_out[cols, :], (((1,), (1,)), ((), ())), preferred_element_type=f32
        )
        dp[:, cols] = (v * slope[:, cols]).astype(bf16)
        return 0

    lax.fori_loop(0, hidden // 256, back, 0)
    load_tok.wait()
    rs = Scatter(cps, at, S, (far, nm, np_, xb, xa), 0, 288, 128, 112)
    rs2 = Scatter(cps, at, S2, (far2, nm2, np2, xb2, xa2), 0, 32, 16, 16)
    swaps = {}

    def chunk(other, dy):
        g = at.chip(other, dy)
        lhs = pl.ds(pl.multiple_of(g * 512, 512), 512)
        for dst, side in ((snd, 1 - at.c), (S, at.c)):
            rhs = pl.ds(pl.multiple_of(side * half, half), half)
            dst[g] = lax.dot_general(
                tok[:, lhs], dp[:, rhs], (((0,), (0,)), ((), ())), preferred_element_type=f32
            ).astype(bf16)
            if dst is snd:
                swaps[other, dy] = cps.start(snd.at[g], rc.at[g], at.CO)

    def merge(other, dy):
        g = at.chip(other, dy)
        swaps[other, dy].wait_recv()
        S[g] = (S[g].astype(f32) + rc[g].astype(f32)).astype(bf16)
        rs.ready(other, dy)

    for i, key in enumerate(ORDER):
        chunk(*key)
        if i > 0:
            merge(*ORDER[i - 1])
        if i == 1:
            swap2.wait_recv()
            S2[...] = (W[at.c].astype(f32) + rc2[...].astype(f32)).astype(bf16)
            for k2 in ORDER:
                rs2.ready(*k2)
        if i == 3:
            rs2.mid_a(1)
            rs2.mid_b()
            rs2.mid_a(0)
        if i == 5:
            rs.mid_a(1)
            rs2.late_a()
            rs2.late_b()
    merge(*ORDER[-1])
    rs2.final(fin2)
    own2[...] = fin2[...].astype(bf16)
    wbuf[at.r] = own2[...]
    gather = gather_rows(cps, at, own2, wbuf, 32, 32, 16)
    landed = list(next(gather))
    rs.mid_b()
    rs.mid_a(0)
    landed += next(gather)
    rs.late_a()
    landed += next(gather)
    rs.late_b()
    landed += next(gather)
    rs.final(fin)
    n = fcore.shape[0]
    fc = cps.start(fin.at[pl.ds(pl.multiple_of((1 - at.c) * n, n), n)], fcore, at.CO)
    wgrad_o[:, pl.ds(pl.multiple_of(at.c * half, half), half)] = fin[pl.ds(pl.multiple_of(at.c * n, n), n), :]
    for copy, _ in landed:
        copy.wait_recv()
    wout_o[...] = wbuf[...].astype(f32).reshape(wout_o.shape)
    for k in lc:
        k.wait_recv()
    loss_o[...] = jnp.sum(lbuf[...], axis=0)
    fc.wait_recv()
    wgrad_o[:, pl.ds(pl.multiple_of((1 - at.c) * half, half), half)] = fcore[...]
    cps.finish()


def tail(tokens, hid, slope, dbott, w_out, loss_row):
    rows, depth = tokens.shape
    hidden, wide = w_out.shape
    shp = jax.ShapeDtypeStruct
    block = (depth // 8, hidden // 2)
    small = (hidden // 16, wide)
    copies = 15 + 1 + 8 + 23 + 23 + 20 + 1
    return pl.pallas_call(
        tail_kernel,
        out_shape=(shp((depth // 16, hidden), f32), shp((hidden, wide), f32), shp((8, 128), f32)),
        in_specs=[aspec(), vspec(), aspec(), vspec(), vspec(), vspec()],
        out_specs=(vspec(),) * 3,
        scratch_shapes=[
            VMEM((rows, depth), bf16), VMEM((rows, hidden), f32), VMEM((rows, hidden), bf16),
            VMEM((8,) + block, bf16), VMEM((8,) + block, bf16), VMEM((8,) + block, bf16),
            *scatter_bufs(block), VMEM(block, f32), VMEM((block[0] // 2, block[1]), f32),
            VMEM((2, 8) + small, bf16), VMEM((8,) + small, bf16), VMEM((8,) + small, bf16),
            *scatter_bufs(small), VMEM(small, f32), VMEM(small, bf16), VMEM((16,) + small, bf16),
            VMEM((16, 8, 128), f32),
            pltpu.SemaphoreType.DMA((copies,)), pltpu.SemaphoreType.DMA((copies,)),
            pltpu.SemaphoreType.DMA((2,)),
        ],
        compiler_params=pltpu.CompilerParams(
            collective_id=2, has_side_effects=True, vmem_limit_bytes=62 * 2**20
        ),
        name="tail",
    )(tokens, hid, slope, dbott, w_out, loss_row)


def on_device(tokens, w_in, w_out, teacher_z, proto_student, proto_teacher, center, image_of):
    hidden, slope, student_n, unit, recip, exp_t, mt, st, wt = head(
        tokens, w_in, w_out, teacher_z, proto_teacher, center, image_of
    )
    dbott, proto_grad, loss_row = middle(
        student_n, proto_student, exp_t, mt, st, wt, unit, recip
    )
    w_in_grad, w_out_grad, loss = tail(tokens, hidden, slope, dbott, w_out, loss_row)
    return (loss[0, 0], w_in_grad, w_out_grad, proto_grad)


def solution(mesh):
    return jax.shard_map(
        on_device,
        mesh=mesh,
        in_specs=(
            P("row", None),
            P("row", "proto"),
            P("proto", None),
            P(("row", "proto"), None),
            P(None, "proto"),
            P(None, "proto"),
            P("proto"),
            P("row"),
        ),
        out_specs=(P(), P("row", "proto"), P("proto", None), P("row", "proto")),
        check_vma=False,
    )
```

```python
import jax
import jax.numpy as jnp
from jax import lax
from jax.sharding import PartitionSpec as P
from jax.experimental import pallas as pl
from jax.experimental.pallas import tpu as pltpu

tau_teacher = 0.07
tau_student = 0.1
loss_scale = 1048576.0
norm_eps = 1e-06
MESH = pl.DeviceIdType.MESH
VMEM = pltpu.VMEM
f32 = jnp.float32
bf16 = jnp.bfloat16


def vspec():
    return pl.BlockSpec(memory_space=pltpu.VMEM)


def aspec():
    return pl.BlockSpec(memory_space=pl.ANY)


class Place:
    def __init__(self):
        self.r = lax.axis_index("row")
        self.p = lax.axis_index("proto")
        self.xh = self.r // 8
        self.y = (self.r // 2) % 4
        self.c = self.r % 2

    def chip(self, other, dy):
        fam = 1 - self.xh if other else self.xh
        return fam * 4 + (self.y + dy) % 4

    def slot(self, other, dy, core=None):
        return self.chip(other, dy) * 2 + (self.c if core is None else core)

    def dev(self, row):
        return (row, self.p)

    @property
    def X(self):
        return self.dev(self.slot(True, 0))

    @property
    def YP(self):
        return self.dev(self.slot(False, 1))

    @property
    def YM(self):
        return self.dev(self.slot(False, 3))

    @property
    def CO(self):
        return self.dev(self.slot(False, 0, 1 - self.c))

    def row_peer(self, d):
        return ((self.r + d) % 16, self.p)

    def proto_peer(self, d):
        return (self.r, (self.p + d) % 8)


class Copies:
    def __init__(self, send, recv):
        self.send, self.recv, self.all = send, recv, []

    def start(self, src, dst, dev):
        i = len(self.all)
        cp = pltpu.make_async_remote_copy(
            src_ref=src,
            dst_ref=dst,
            send_sem=self.send.at[i],
            recv_sem=self.recv.at[i],
            device_id=dev,
            device_id_type=MESH,
        )
        cp.start()
        self.all.append(cp)
        return cp

    def expect(self, dst, i, dev):
        cp = pltpu.make_async_remote_copy(
            src_ref=dst,
            dst_ref=dst,
            send_sem=self.send.at[i],
            recv_sem=self.recv.at[i],
            device_id=dev,
            device_id_type=MESH,
        )
        self.all.append(cp)
        return cp

    def finish(self):
        for cp in self.all:
            cp.wait_send()


def greet(peers):
    bar = pltpu.get_barrier_semaphore()
    for dev in peers:
        pl.semaphore_signal(bar, inc=1, device_id=dev, device_id_type=MESH)


def met(count):
    pl.semaphore_wait(pltpu.get_barrier_semaphore(), count)


def gather_rows(cps, at, own, buf, base, n, a, h, al):
    every = (0, n)
    up, lo = (h, n - h), (0, h)
    A, B = (0, a), (a, n - a)
    aup, alo = (al, a - al), (0, al)

    def on(slot, part, dev, src=None):
        ref = buf.at[slot, pl.ds(base + part[0], part[1])]
        return cps.start(ref if src is None else src, ref, dev)

    me = at.slot(False, 0)
    mine = own.at[pl.ds(base, n)]
    x0 = on(me, every, at.X, mine)
    p0 = on(me, every, at.YP, mine)
    m0 = on(me, every, at.YM, mine)
    c0 = on(me, every, at.CO, mine)
    yield [(c0, at.chip(False, 0))]
    sx = at.slot(True, 0)
    sm, sp, sf = at.slot(False, 3), at.slot(False, 1), at.slot(False, 2)
    xm, xp, xf = at.slot(True, 3), at.slot(True, 1), at.slot(True, 2)
    x0.wait_recv()
    xap = on(sx, A, at.YP)
    xam = on(sx, A, at.YM)
    xc = on(sx, every, at.CO)
    p0.wait_recv()
    fup = on(sm, up, at.YP)
    bm = on(sm, B, at.X)
    cm = on(sm, every, at.CO)
    m0.wait_recv()
    flo = on(sp, lo, at.YM)
    bp = on(sp, B, at.X)
    cp = on(sp, every, at.CO)
    yield [(xc, at.chip(True, 0)), (cm, at.chip(False, 3)), (cp, at.chip(False, 1))]
    xap.wait_recv()
    gup = on(xm, aup, at.YP)
    xam.wait_recv()
    glo = on(xp, alo, at.YM)
    fup.wait_recv()
    flo.wait_recv()
    bf = on(sf, B, at.X)
    cf = on(sf, every, at.CO)
    bm.wait_recv()
    cxm = on(xm, every, at.CO)
    bp.wait_recv()
    cxp = on(xp, every, at.CO)
    yield [(cf, at.chip(False, 2)), (cxm, at.chip(True, 3)), (cxp, at.chip(True, 1))]
    gup.wait_recv()
    glo.wait_recv()
    bf.wait_recv()
    cxf = on(xf, every, at.CO)
    yield [(cxf, at.chip(True, 2))]


def across(row):
    return jnp.transpose(jnp.broadcast_to(row, (128, row.shape[1])))


def gelu_parts(values):
    cumul = 0.5 * (1.0 + lax.erf(values * 0.7071067811865476))
    density = jnp.exp(-0.5 * values * values) * 0.3989422804014327
    return (values * cumul, cumul + values * density)


class Scatter:
    def __init__(self, cps, at, S, bufs, axis, a, al, bl):
        self.cps, self.at, self.S, self.axis = cps, at, S, axis
        self.far, self.nm, self.np, self.xb, self.xa = bufs
        n = S.shape[1 + axis]
        self.A, self.B = (0, a), (a, n - a)
        self.Alo, self.Aup = (0, al), (al, a - al)
        self.Blo, self.Bup = (a, bl), (a + bl, n - a - bl)
        self.got = {}

    def idx(self, i, part):
        cut = pl.ds(*part)
        return (i, cut) if self.axis == 0 else (i, slice(None), cut)

    def send(self, key, g, dst, i, part, dev):
        self.got[key] = self.cps.start(
            self.S.at[self.idx(g, part)], dst.at[self.idx(i, part)], dev
        )

    def add(self, g, part, *terms):
        where = self.idx(g, part)
        v = self.S[where].astype(f32)
        for ref, i in terms:
            v = v + ref[self.idx(i, part)].astype(f32)
        self.S[where] = v.astype(bf16)

    def wait(self, key):
        self.got[key].wait_recv()

    def ready(self, other, dy):
        g, k = self.at.chip(other, dy), int(other)
        if dy == 2:
            self.send(("fu", k), g, self.far, k, self.Aup, self.at.YP)
            self.send(("fl", k), g, self.far, k, self.Alo, self.at.YM)
        if dy == 1:
            self.send(("ml", k), g, self.nm, k, self.Alo, self.at.YP)
        if dy == 3:
            self.send(("pu", k), g, self.np, k, self.Aup, self.at.YM)

    def ready_x(self, dy):
        self.send(("x", dy), self.at.chip(True, dy), self.xb, dy, self.B, self.at.X)

    def mid_a(self, k):
        g1, g3 = self.at.chip(bool(k), 1), self.at.chip(bool(k), 3)
        self.wait(("fu", k))
        self.add(g1, self.Aup, (self.far, k))
        self.send(("mu", k), g1, self.nm, k, self.Aup, self.at.YP)
        self.wait(("fl", k))
        self.add(g3, self.Alo, (self.far, k))
        self.send(("pl", k), g3, self.np, k, self.Alo, self.at.YM)

    def mid_b(self):
        for dy in (2, 1, 3):
            g = self.at.chip(False, dy)
            self.wait(("x", dy))
            self.add(g, self.B, (self.xb, dy))
            if dy == 2:
                self.send("bfu", g, self.far, 0, self.Bup, self.at.YP)
                self.send("bfl", g, self.far, 0, self.Blo, self.at.YM)
            elif dy == 1:
                self.send("bml", g, self.nm, 0, self.Blo, self.at.YP)
            else:
                self.send("bpu", g, self.np, 0, self.Bup, self.at.YM)

    def late_a(self):
        for key in ("ml", "mu", "pl", "pu"):
            self.wait((key, 1))
        g = self.at.chip(True, 0)
        self.add(g, self.A, (self.nm, 1), (self.np, 1))
        self.send("xa", g, self.xa, 0, self.A, self.at.X)

    def late_b(self):
        g1, g3 = self.at.chip(False, 1), self.at.chip(False, 3)
        self.wait("bfu")
        self.add(g1, self.Bup, (self.far, 0))
        self.send("bmu", g1, self.nm, 0, self.Bup, self.at.YP)
        self.wait("bfl")
        self.add(g3, self.Blo, (self.far, 0))
        self.send("bpl", g3, self.np, 0, self.Blo, self.at.YM)

    def final(self, fin):
        g = self.at.chip(False, 0)
        for key in ("ml", "mu", "pl", "pu"):
            self.wait((key, 0))
        for key in ("xa", ("x", 0), "bml", "bmu", "bpl", "bpu"):
            self.wait(key)
        for part, last, i in ((self.A, self.xa, 0), (self.B, self.xb, 0)):
            v = self.S[self.idx(g, part)].astype(f32)
            for ref, j in ((self.nm, 0), (self.np, 0), (last, i)):
                v = v + ref[self.idx(j, part)].astype(f32)
            fin[self.idx(0, part)[1:]] = v


def scatter_bufs(shape):
    return [VMEM((n,) + shape, bf16) for n in (2, 2, 2, 4, 1)]


ORDER = [(True, 2), (True, 1), (True, 3), (True, 0), (False, 2), (False, 1), (False, 3), (False, 0)]


def head_kernel(
    tokens, w_in, w_out, teacher, proto_t, center,
    hid_o, slope_o, sn_o, unit_o, recip_o, et_o, stat_o,
    tok, wbuf, pt, lt, et, top, tot, pre, hid, slope, tbuf, part, rbuf, sbuf, send, recv, lsem,
):
    at = Place()
    cps = Copies(send, recv)
    rows, depth = tok.shape
    kk = lt.shape[1]
    peers = [at.X, at.YP, at.YM, at.CO] + [at.proto_peer(d) for d in range(1, 8)]
    greet(peers)
    me = at.slot(False, 0)
    load_pt = pltpu.make_async_copy(proto_t, pt, lsem.at[1])
    load_pt.start()
    own = pltpu.make_async_copy(w_in, wbuf.at[me], lsem.at[0])
    own.start()
    load_tok = pltpu.make_async_copy(tokens, tok, lsem.at[2])
    load_tok.start()
    t = teacher[...].astype(f32)
    tbuf[at.p] = (t * lax.rsqrt(jnp.sum(t * t, axis=1, keepdims=True) + norm_eps)).astype(bf16)
    met(len(peers))
    halves = [
        gather_rows(cps, at, w_in, wbuf, 0, 128, 80, 64, 32),
        gather_rows(cps, at, w_in, wbuf, 128, 128, 64, 64, 32),
    ]

    def advance():
        return list(zip(*[next(g) for g in halves]))

    def accumulate(landed):
        block = wbuf.shape[1] * 2
        for (one, chip), (two, _) in landed:
            one.wait_recv()
            two.wait_recv()
            lhs = tok[:, pl.ds(pl.multiple_of(chip * block, block), block)]

            def tile(j, _):
                cols = pl.ds(pl.multiple_of(j * 256, 256), 256)
                rhs = wbuf[pl.ds(chip * 2, 2), :, cols].reshape(block, 256)
                pre[:, cols] += jnp.dot(lhs, rhs, preferred_element_type=f32)
                return 0

            lax.fori_loop(0, pre.shape[1] // 256, tile, 0)

    started = advance()
    tc = [cps.start(tbuf.at[at.p], tbuf.at[at.p], at.proto_peer(d)) for d in range(1, 8)]
    pre[...] = jnp.zeros_like(pre)
    load_pt.wait()
    for k in tc:
        k.wait_recv()
    tn = tbuf[...].reshape(rows, tbuf.shape[2])
    step = 512

    def score(j, best):
        cols = pl.ds(pl.multiple_of(j * step, step), step)
        v = jnp.dot(tn, pt[:, cols], preferred_element_type=f32)
        v = (v - center[:, cols]) * (1.0 / tau_teacher)
        lt[:, cols] = v
        for q in range(step // 128):
            best = jnp.maximum(best, v[:, q * 128 : (q + 1) * 128])
        return best

    top[...] = lax.fori_loop(0, kk // step, score, jnp.full((rows, 128), -jnp.inf, f32))
    own.wait()
    load_tok.wait()
    first = advance()
    top[...] = jnp.broadcast_to(jnp.max(top[...], axis=1, keepdims=True), (rows, 128))
    tot[...] = jnp.zeros_like(tot)

    def lift(j, _):
        cols = pl.ds(pl.multiple_of(j * 128, 128), 128)
        e = jnp.exp(lt[:, cols] - top[...])
        et[:, cols] = e.astype(bf16)
        tot[...] += e
        return 0

    lax.fori_loop(0, kk // 128, lift, 0)
    save = pltpu.make_async_copy(et, et_o, lsem.at[3])
    save.start()
    accumulate(started)
    second = advance()
    stat_o[...] = jnp.concatenate(
        [
            jnp.transpose(top[...])[0:1],
            jnp.sum(jnp.transpose(tot[...]), axis=0, keepdims=True),
            jnp.zeros((6, rows), f32),
        ],
        axis=0,
    )
    accumulate(first)
    third = advance()
    accumulate(second)
    accumulate(third)

    small = part.shape[1]

    def act(q):
        rs = pl.ds(pl.multiple_of(q * small, small), small)
        value, grade = gelu_parts(pre[rs, :])
        slope[rs, :] = grade
        h = value.astype(bf16)
        hid[rs, :] = h
        part[q] = jnp.dot(h, w_out[...], preferred_element_type=f32)

    base = len(cps.all)

    def act_send(i, _):
        q = (at.p + i + 1) % 8
        act(q)
        pltpu.make_async_remote_copy(
            src_ref=part.at[q],
            dst_ref=rbuf.at[i],
            send_sem=send.at[base + i],
            recv_sem=recv.at[base + i],
            device_id=(at.r, q),
            device_id_type=MESH,
        ).start()
        return 0

    lax.fori_loop(0, 7, act_send, 0)
    act(at.p)
    save_hid = pltpu.make_async_copy(hid, hid_o, lsem.at[4])
    save_hid.start()
    save_slope = pltpu.make_async_copy(slope, slope_o, lsem.at[5])
    save_slope.start()
    total = part[at.p]
    for i in range(7):
        cps.expect(rbuf.at[i], base + i, at.proto_peer(i + 1)).wait_recv()
        total = total + rbuf[i]
    recip = lax.rsqrt(jnp.sum(total * total, axis=1, keepdims=True) + norm_eps)
    unit = total * recip
    sbuf[at.p] = unit.astype(bf16)
    sc = [cps.start(sbuf.at[at.p], sbuf.at[at.p], at.proto_peer(d)) for d in range(1, 8)]
    unit_o[...] = unit
    recip_o[...] = jnp.broadcast_to(recip, recip_o.shape)
    for k in sc:
        k.wait_recv()
    sn_o[...] = sbuf[...].reshape(rows, sbuf.shape[2])
    save.wait()
    save_hid.wait()
    save_slope.wait()
    cps.finish()


def head(tokens, w_in, w_out, teacher_z, proto_teacher, center):
    rows, depth = tokens.shape
    hidden = w_in.shape[1]
    wide = w_out.shape[1]
    kk = proto_teacher.shape[1]
    small = teacher_z.shape[0]
    shp = jax.ShapeDtypeStruct
    copies = 40 + 7 + 7 + 7
    return pl.pallas_call(
        head_kernel,
        out_shape=(
            shp((rows, hidden), bf16), shp((rows, hidden), f32), shp((rows, wide), bf16),
            shp((small, wide), f32), shp((small, 128), f32), shp((rows, kk), bf16), shp((8, rows), f32),
        ),
        in_specs=[aspec(), aspec(), vspec(), vspec(), aspec(), vspec()],
        out_specs=(aspec(), aspec(), vspec(), vspec(), vspec(), aspec(), vspec()),
        scratch_shapes=[
            VMEM((rows, depth), bf16), VMEM((16,) + w_in.shape, bf16),
            VMEM(proto_teacher.shape, bf16), VMEM((rows, kk), f32), VMEM((rows, kk), bf16),
            VMEM((rows, 128), f32), VMEM((rows, 128), f32),
            VMEM((rows, hidden), f32), VMEM((rows, hidden), bf16), VMEM((rows, hidden), f32),
            VMEM((8, small, wide), bf16), VMEM((8, small, wide), f32),
            VMEM((7, small, wide), f32), VMEM((8, small, wide), bf16),
            pltpu.SemaphoreType.DMA((copies,)), pltpu.SemaphoreType.DMA((copies,)),
            pltpu.SemaphoreType.DMA((6,)),
        ],
        compiler_params=pltpu.CompilerParams(
            collective_id=0, has_side_effects=True, vmem_limit_bytes=62 * 2**20
        ),
        name="head",
    )(tokens, w_in, w_out, teacher_z, proto_teacher, center[None, :])


def along(col):
    return jnp.transpose(col)


def middle_kernel(
    sn, proto_s, et_in, stat_t, image, unit, recip,
    dbott_o, pgrad_o, loss_o,
    ps, et, ls, gs, snt, ms, ss, cs, cbuf, stats, fsb, ftb, S, snd, rc, far, nm, np_, xb, xa, fin, fcore,
    dacc, dpart, drecv, dbuf, send, recv, lsem,
):
    at = Place()
    cps = Copies(send, recv)
    rows, kk = ls.shape
    half = kk // 2
    peers = [at.proto_peer(d) for d in range(1, 8)] + [at.row_peer(d) for d in range(1, 16)]
    greet(peers)
    load_ps = pltpu.make_async_copy(proto_s, ps, lsem.at[0])
    load_ps.start()
    load_et = pltpu.make_async_copy(et_in, et, lsem.at[1])
    load_et.start()
    snt[...] = jnp.transpose(sn[...])
    images = cbuf.shape[1]
    onehot = (lax.broadcasted_iota(jnp.int32, (images, rows), 0) == image[...]).astype(f32)
    cbuf[at.r] = jnp.broadcast_to(jnp.sum(onehot, axis=1, keepdims=True), cbuf.shape[1:])
    load_ps.wait()
    step = 512

    def one(j, top):
        cols = pl.ds(pl.multiple_of(j * step, step), step)
        v = jnp.dot(sn[...], ps[:, cols], preferred_element_type=f32) * (1.0 / tau_student)
        ls[:, cols] = v
        for q in range(step // 128):
            top = jnp.maximum(top, v[:, q * 128 : (q + 1) * 128])
        return top

    ms[...] = lax.fori_loop(0, kk // step, one, jnp.full((rows, 128), -jnp.inf, f32))
    met(len(peers))
    cc = [cps.start(cbuf.at[at.r], cbuf.at[at.r], at.row_peer(d)) for d in range(1, 16)]
    ms[...] = jnp.broadcast_to(jnp.max(ms[...], axis=1, keepdims=True), (rows, 128))
    ss[...] = jnp.zeros_like(ss)
    cs[...] = jnp.zeros_like(cs)
    load_et.wait()

    def two(j, _):
        cols = pl.ds(pl.multiple_of(j * 128, 128), 128)
        d = ls[:, cols] - ms[...]
        e = jnp.exp(d)
        ls[:, cols] = e
        ss[...] += e
        cs[...] += et[:, cols].astype(f32) * d
        return 0

    lax.fori_loop(0, kk // 128, two, 0)
    stats[at.p] = jnp.concatenate(
        [
            stat_t[0:2],
            along(ms[...])[0:1],
            jnp.sum(along(ss[...]), axis=0, keepdims=True),
            jnp.sum(along(cs[...]), axis=0, keepdims=True),
            jnp.zeros((3, rows), f32),
        ],
        axis=0,
    )
    sc = [cps.start(stats.at[at.p], stats.at[at.p], at.proto_peer(d)) for d in range(1, 8)]
    for k in cc:
        k.wait_recv()
    counts = jnp.sum(cbuf[...], axis=0)[:, 0:1]
    w_row = 1.0 / (images * jnp.sum(onehot * counts, axis=0, keepdims=True))
    for k in sc:
        k.wait_recv()
    table = [stats[q] for q in range(8)]
    top_t = table[0][0:1]
    top_s = table[0][2:3]
    for q in table[1:]:
        top_t = jnp.maximum(top_t, q[0:1])
        top_s = jnp.maximum(top_s, q[2:3])
    total_t = total_s = cross = jnp.zeros((1, rows), f32)
    for q in table:
        scale = jnp.exp(q[0:1] - top_t)
        total_t = total_t + q[1:2] * scale
        total_s = total_s + q[3:4] * jnp.exp(q[2:3] - top_s)
        cross = cross + scale * (q[4:5] + q[1:2] * (q[2:3] - top_s))
    cross = jnp.log(total_s) - cross / total_t
    loss_o[...] = jnp.broadcast_to(w_row * cross, loss_o.shape)
    mine = stats[at.p]
    lift = (loss_scale / tau_student) * w_row
    fsb[...] = across(lift * jnp.exp(mine[2:3] - top_s) / total_s)
    ftb[...] = across(lift * jnp.exp(mine[0:1] - top_t) / total_t)
    dacc[...] = jnp.zeros_like(dacc)

    def grads(base, dst):
        def one(j, _):
            first = base + j * step
            for q in range(step // 128):
                cols = pl.ds(pl.multiple_of(first + q * 128, 128), 128)
                v = ls[:, cols] * fsb[...] - et[:, cols].astype(f32) * ftb[...]
                gs[:, q * 128 : (q + 1) * 128] = v.astype(bf16)
            cols = pl.ds(pl.multiple_of(first, step), step)
            g = gs[...]
            v = jnp.dot(snt[...], g, preferred_element_type=f32)
            dst[:, :, pl.ds(pl.multiple_of(j * step, step), step)] = v.astype(bf16).reshape(
                dst.shape[0], dst.shape[1], step
            )
            d = lax.dot_general(
                g, ps[:, cols], (((1,), (1,)), ((), ())), preferred_element_type=f32
            )
            dacc[...] += d
            return 0

        lax.fori_loop(0, half // step, one, 0)

    grads((1 - at.c) * half, snd)
    swap = cps.start(snd, rc, at.CO)
    grads(at.c * half, S)
    dpart[...] = dacc[...].astype(bf16).reshape(dpart.shape)
    dc = [
        cps.start(dpart.at[(at.p + d) % 8], drecv.at[d], at.proto_peer(d)) for d in range(1, 8)
    ]
    swap.wait_recv()
    rs = Scatter(cps, at, S, (far, nm, np_, xb, xa), 1, 1792, 768, 640)
    for other, dy in ORDER:
        g = at.chip(other, dy)
        S[g] = (S[g].astype(f32) + rc[g].astype(f32)).astype(bf16)
        rs.ready(other, dy)
    total = dpart[at.p].astype(f32)
    for d in range(1, 8):
        dc[d - 1].wait_recv()
        total = total + drecv[d].astype(f32)
    u, r = unit[...], recip[:, 0:1]
    dbuf[at.p] = (r * (total - u * jnp.sum(u * total, axis=1, keepdims=True))).astype(bf16)
    bc = [cps.start(dbuf.at[at.p], dbuf.at[at.p], at.proto_peer(d)) for d in range(1, 8)]
    for dy in (2, 1, 3, 0):
        rs.ready_x(dy)
    rs.mid_a(1)
    rs.mid_a(0)
    rs.late_a()
    rs.mid_b()
    rs.late_b()
    for k in bc:
        k.wait_recv()
    dbott_o[...] = dbuf[...].reshape(dbott_o.shape)
    rs.final(fin)
    n = fcore.shape[0]
    keep, give = at.c * n, (1 - at.c) * n
    fc = cps.start(fin.at[pl.ds(pl.multiple_of(give, 8), n)], fcore, at.CO)
    pgrad_o[:, pl.ds(pl.multiple_of(at.c * half, half), half)] = fin[pl.ds(pl.multiple_of(keep, 8), n), :]
    fc.wait_recv()
    pgrad_o[:, pl.ds(pl.multiple_of((1 - at.c) * half, half), half)] = fcore[...]
    cps.finish()


def middle(sn, proto_s, et, stat_t, image, unit, recip):
    rows, wide = sn.shape
    kk = proto_s.shape[1]
    small = unit.shape[0]
    shp = jax.ShapeDtypeStruct
    chunk = (wide // 8, kk // 2)
    copies = 15 + 7 + 1 + 7 + 7 + 23 + 1
    lane = VMEM((rows, 128), f32)
    return pl.pallas_call(
        middle_kernel,
        out_shape=(shp((rows, wide), bf16), shp((wide // 16, kk), f32), shp((8, rows), f32)),
        in_specs=[vspec(), aspec(), aspec()] + [vspec()] * 4,
        out_specs=(vspec(),) * 3,
        scratch_shapes=[
            VMEM((wide, kk), bf16), VMEM((rows, kk), bf16), VMEM((rows, kk), f32), VMEM((rows, 512), bf16),
            VMEM((wide, rows), bf16), lane, lane, lane, VMEM((16, 64, 128), f32), VMEM((8, 8, rows), f32), lane, lane,
            VMEM((8,) + chunk, bf16), VMEM((8,) + chunk, bf16), VMEM((8,) + chunk, bf16),
            *scatter_bufs(chunk), VMEM(chunk, f32), VMEM((chunk[0] // 2, chunk[1]), f32),
            VMEM((rows, wide), f32), VMEM((8, small, wide), bf16), VMEM((8, small, wide), bf16), VMEM((8, small, wide), bf16),
            pltpu.SemaphoreType.DMA((copies,)), pltpu.SemaphoreType.DMA((copies,)),
            pltpu.SemaphoreType.DMA((2,)),
        ],
        compiler_params=pltpu.CompilerParams(
            collective_id=1, has_side_effects=True, vmem_limit_bytes=62 * 2**20
        ),
        name="middle",
    )(sn, proto_s, et, stat_t, image, unit, recip)


def tail_kernel(
    tokens, hid_in, slope_in, dbott, w_out, loss_in,
    wgrad_o, wout_o, loss_o,
    tok, hid, slope, dp, S, snd, rc, far, nm, np_, xb, xa, fin, fcore,
    W, S2, rc2, far2, nm2, np2, xb2, xa2, fin2, own2, wbuf, lbuf, send, recv, lsem,
):
    at = Place()
    cps = Copies(send, recv)
    rows, hidden = dp.shape
    half = hidden // 2
    peers = [at.row_peer(d) for d in range(1, 16)]
    greet(peers)
    load_tok = pltpu.make_async_copy(tokens, tok, lsem.at[0])
    load_tok.start()
    load_hid = pltpu.make_async_copy(hid_in, hid, lsem.at[2])
    load_hid.start()
    load_slope = pltpu.make_async_copy(slope_in, slope, lsem.at[1])
    load_slope.start()
    lbuf[at.r] = jnp.broadcast_to(
        jnp.sum(loss_in[...], axis=1, keepdims=True), lbuf.shape[1:]
    )
    load_slope.wait()

    def back(j, _):
        cols = pl.ds(pl.multiple_of(j * 256, 256), 256)
        v = lax.dot_general(
            dbott[...], w_out[cols, :], (((1,), (1,)), ((), ())), preferred_element_type=f32
        )
        dp[:, cols] = (v * slope[:, cols]).astype(bf16)
        return 0

    lax.fori_loop(0, hidden // 256, back, 0)
    load_tok.wait()
    met(len(peers))
    rs = Scatter(cps, at, S, (far, nm, np_, xb, xa), 0, 288, 128, 112)
    rs2 = Scatter(cps, at, S2, (far2, nm2, np2, xb2, xa2), 0, 32, 16, 16)
    swaps = {}

    def chunk(other, dy):
        g = at.chip(other, dy)
        lhs = pl.ds(pl.multiple_of(g * 512, 512), 512)
        for dst, side in ((snd, 1 - at.c), (S, at.c)):
            rhs = pl.ds(pl.multiple_of(side * half, half), half)
            dst[g] = lax.dot_general(
                tok[:, lhs], dp[:, rhs], (((0,), (0,)), ((), ())), preferred_element_type=f32
            ).astype(bf16)
            if dst is snd:
                swaps[other, dy] = cps.start(snd.at[g], rc.at[g], at.CO)

    def merge(other, dy):
        g = at.chip(other, dy)
        swaps[other, dy].wait_recv()
        S[g] = (S[g].astype(f32) + rc[g].astype(f32)).astype(bf16)
        rs.ready(other, dy)
        if other:
            rs.ready_x(dy)

    def out_grad():
        load_hid.wait()
        small = W.shape[2]
        for j in range(hidden // 256):
            cols = slice(j * 256, (j + 1) * 256)
            v = lax.dot_general(
                hid[:, cols], dbott[...], (((0,), (0,)), ((), ())), preferred_element_type=f32
            ).astype(bf16)
            for i in range(256 // small):
                k = j * (256 // small) + i
                W[k % 2, k // 2] = v[i * small : (i + 1) * small]
        loss_c = [cps.start(lbuf.at[at.r], lbuf.at[at.r], at.row_peer(d)) for d in range(1, 16)]
        swap = cps.start(W.at[1 - at.c], rc2, at.CO)
        return loss_c, swap

    for i, key in enumerate(ORDER):
        chunk(*key)
        if i > 0:
            merge(*ORDER[i - 1])
        if i == 1:
            lc, swap2 = out_grad()
        if i == 2:
            swap2.wait_recv()
            S2[...] = (W[at.c].astype(f32) + rc2[...].astype(f32)).astype(bf16)
            for k2 in ORDER:
                rs2.ready(*k2)
                if k2[0]:
                    rs2.ready_x(k2[1])
        if i == 4:
            rs2.mid_a(1)
            rs2.mid_b()
            rs2.mid_a(0)
        if i == 5:
            rs.mid_a(1)
        if i == 6:
            rs2.late_a()
            rs2.late_b()
    merge(*ORDER[-1])
    rs2.final(fin2)
    own2[...] = fin2[...].astype(bf16)
    wbuf[at.r] = own2[...]
    gather = gather_rows(cps, at, own2, wbuf, 0, 64, 32, 32, 16)
    landed = list(next(gather))
    rs.mid_b()
    rs.mid_a(0)
    landed += next(gather)
    rs.late_a()
    landed += next(gather)
    rs.late_b()
    landed += next(gather)
    rs.final(fin)
    n = fcore.shape[0]
    fc = cps.start(fin.at[pl.ds(pl.multiple_of((1 - at.c) * n, n), n)], fcore, at.CO)
    wgrad_o[:, pl.ds(pl.multiple_of(at.c * half, half), half)] = fin[pl.ds(pl.multiple_of(at.c * n, n), n), :]
    for copy, _ in landed:
        copy.wait_recv()
    wout_o[...] = wbuf[...].reshape(wout_o.shape)
    for k in lc:
        k.wait_recv()
    loss_o[...] = jnp.sum(lbuf[...], axis=0)
    fc.wait_recv()
    wgrad_o[:, pl.ds(pl.multiple_of((1 - at.c) * half, half), half)] = fcore[...]
    cps.finish()


def tail(tokens, hid, slope, dbott, w_out, loss_row):
    rows, depth = tokens.shape
    hidden, wide = w_out.shape
    shp = jax.ShapeDtypeStruct
    block = (depth // 8, hidden // 2)
    small = (hidden // 16, wide)
    copies = 15 + 1 + 8 + 23 + 23 + 20 + 1
    return pl.pallas_call(
        tail_kernel,
        out_shape=(shp((depth // 16, hidden), f32), shp((hidden, wide), bf16), shp((8, 128), f32)),
        in_specs=[aspec(), aspec(), aspec(), vspec(), vspec(), vspec()],
        out_specs=(vspec(),) * 3,
        scratch_shapes=[
            VMEM((rows, depth), bf16), VMEM((rows, hidden), bf16), VMEM((rows, hidden), f32), VMEM((rows, hidden), bf16),
            VMEM((8,) + block, bf16), VMEM((8,) + block, bf16), VMEM((8,) + block, bf16),
            *scatter_bufs(block), VMEM(block, f32), VMEM((block[0] // 2, block[1]), f32),
            VMEM((2, 8) + small, bf16), VMEM((8,) + small, bf16), VMEM((8,) + small, bf16),
            *scatter_bufs(small), VMEM(small, f32), VMEM(small, bf16), VMEM((16,) + small, bf16),
            VMEM((16, 8, 128), f32),
            pltpu.SemaphoreType.DMA((copies,)), pltpu.SemaphoreType.DMA((copies,)),
            pltpu.SemaphoreType.DMA((3,)),
        ],
        compiler_params=pltpu.CompilerParams(
            collective_id=2, has_side_effects=True, vmem_limit_bytes=62 * 2**20
        ),
        name="tail",
    )(tokens, hid, slope, dbott, w_out, loss_row)


def close_kernel(wg, wo, pg, loss, wg_o, wo_o, pg_o, loss_o):
    wg_o[...] = wg[...]
    wo_o[...] = wo[...].astype(f32)
    pg_o[...] = pg[...]
    loss_o[0, 0] = loss[0, 0]


def close(wg, wo, pg, loss):
    shp = jax.ShapeDtypeStruct
    n = 2
    specs = [
        pl.BlockSpec((wg.shape[0] // n, wg.shape[1]), lambda i: (i, 0)),
        pl.BlockSpec((wo.shape[0] // n, wo.shape[1]), lambda i: (i, 0)),
        pl.BlockSpec((pg.shape[0], pg.shape[1] // n), lambda i: (0, i)),
    ]
    return pl.pallas_call(
        close_kernel,
        grid=(n,),
        out_shape=(shp(wg.shape, f32), shp(wo.shape, f32), shp(pg.shape, f32), shp((1, 1), f32)),
        in_specs=specs + [pl.BlockSpec((8, 128), lambda i: (0, 0))],
        out_specs=tuple(specs) + (pl.BlockSpec((1, 1), lambda i: (0, 0), memory_space=pltpu.SMEM),),
        name="close",
    )(wg, wo, pg, loss)


def on_device(tokens, w_in, w_out, teacher_z, proto_student, proto_teacher, center, image_of):
    hidden, slope, student_n, unit, recip, exp_t, stat_t = head(
        tokens, w_in, w_out, teacher_z, proto_teacher, center
    )
    dbott, proto_grad, loss_row = middle(
        student_n, proto_student, exp_t, stat_t, image_of[None, :], unit, recip
    )
    w_in_grad, w_out_grad, loss = tail(tokens, hidden, slope, dbott, w_out, loss_row)
    w_in_grad, w_out_grad, proto_grad, loss = close(w_in_grad, w_out_grad, proto_grad, loss)
    return (loss[0, 0], w_in_grad, w_out_grad, proto_grad)


def solution(mesh):
    return jax.shard_map(
        on_device,
        mesh=mesh,
        in_specs=(
            P("row", None),
            P("row", "proto"),
            P("proto", None),
            P(("row", "proto"), None),
            P(None, "proto"),
            P(None, "proto"),
            P("proto"),
            P("row"),
        ),
        out_specs=(P(), P("row", "proto"), P("proto", None), P("row", "proto")),
        check_vma=False,
    )
```

```python
import jax
import jax.numpy as jnp
from jax import lax
from jax.sharding import PartitionSpec as P
from jax.experimental import pallas as pl
from jax.experimental.pallas import tpu as pltpu

tau_teacher = 0.07
tau_student = 0.1
loss_scale = 1048576.0
norm_eps = 1e-06
MESH = pl.DeviceIdType.MESH
VMEM = pltpu.VMEM
f32 = jnp.float32
bf16 = jnp.bfloat16


def vspec():
    return pl.BlockSpec(memory_space=pltpu.VMEM)


def aspec():
    return pl.BlockSpec(memory_space=pl.ANY)


class Place:
    def __init__(self):
        self.r = lax.axis_index("row")
        self.p = lax.axis_index("proto")
        self.xh = self.r // 8
        self.y = (self.r // 2) % 4
        self.c = self.r % 2

    def chip(self, other, dy):
        fam = 1 - self.xh if other else self.xh
        return fam * 4 + (self.y + dy) % 4

    def slot(self, other, dy, core=None):
        return self.chip(other, dy) * 2 + (self.c if core is None else core)

    def dev(self, row):
        return (row, self.p)

    @property
    def X(self):
        return self.dev(self.slot(True, 0))

    @property
    def YP(self):
        return self.dev(self.slot(False, 1))

    @property
    def YM(self):
        return self.dev(self.slot(False, 3))

    @property
    def CO(self):
        return self.dev(self.slot(False, 0, 1 - self.c))

    def row_peer(self, d):
        return ((self.r + d) % 16, self.p)

    def proto_peer(self, d):
        return (self.r, (self.p + d) % 8)


class Copies:
    def __init__(self, send, recv):
        self.send, self.recv, self.all = send, recv, []

    def start(self, src, dst, dev):
        i = len(self.all)
        cp = pltpu.make_async_remote_copy(
            src_ref=src,
            dst_ref=dst,
            send_sem=self.send.at[i],
            recv_sem=self.recv.at[i],
            device_id=dev,
            device_id_type=MESH,
        )
        cp.start()
        self.all.append(cp)
        return cp

    def expect(self, dst, i, dev):
        cp = pltpu.make_async_remote_copy(
            src_ref=dst,
            dst_ref=dst,
            send_sem=self.send.at[i],
            recv_sem=self.recv.at[i],
            device_id=dev,
            device_id_type=MESH,
        )
        self.all.append(cp)
        return cp

    def finish(self):
        for cp in self.all:
            cp.wait_send()


def greet(peers):
    bar = pltpu.get_barrier_semaphore()
    for dev in peers:
        pl.semaphore_signal(bar, inc=1, device_id=dev, device_id_type=MESH)


def met(count):
    pl.semaphore_wait(pltpu.get_barrier_semaphore(), count)


def gather_rows(cps, at, own, buf, base, n, a, h, al):
    every = (0, n)
    up, lo = (h, n - h), (0, h)
    A, B = (0, a), (a, n - a)
    aup, alo = (al, a - al), (0, al)

    def on(slot, part, dev, src=None):
        ref = buf.at[slot, pl.ds(base + part[0], part[1])]
        return cps.start(ref if src is None else src, ref, dev)

    me = at.slot(False, 0)
    mine = own.at[pl.ds(base, n)]
    x0 = on(me, every, at.X, mine)
    p0 = on(me, every, at.YP, mine)
    m0 = on(me, every, at.YM, mine)
    c0 = on(me, every, at.CO, mine)
    yield [(c0, at.chip(False, 0))]
    sx = at.slot(True, 0)
    sm, sp, sf = at.slot(False, 3), at.slot(False, 1), at.slot(False, 2)
    xm, xp, xf = at.slot(True, 3), at.slot(True, 1), at.slot(True, 2)
    x0.wait_recv()
    xap = on(sx, A, at.YP)
    xam = on(sx, A, at.YM)
    xc = on(sx, every, at.CO)
    p0.wait_recv()
    fup = on(sm, up, at.YP)
    bm = on(sm, B, at.X)
    cm = on(sm, every, at.CO)
    m0.wait_recv()
    flo = on(sp, lo, at.YM)
    bp = on(sp, B, at.X)
    cp = on(sp, every, at.CO)
    yield [(xc, at.chip(True, 0)), (cm, at.chip(False, 3)), (cp, at.chip(False, 1))]
    xap.wait_recv()
    gup = on(xm, aup, at.YP)
    xam.wait_recv()
    glo = on(xp, alo, at.YM)
    fup.wait_recv()
    flo.wait_recv()
    bf = on(sf, B, at.X)
    cf = on(sf, every, at.CO)
    bm.wait_recv()
    cxm = on(xm, every, at.CO)
    bp.wait_recv()
    cxp = on(xp, every, at.CO)
    yield [(cf, at.chip(False, 2)), (cxm, at.chip(True, 3)), (cxp, at.chip(True, 1))]
    gup.wait_recv()
    glo.wait_recv()
    bf.wait_recv()
    cxf = on(xf, every, at.CO)
    yield [(cxf, at.chip(True, 2))]


def across(row):
    return jnp.transpose(jnp.broadcast_to(row, (128, row.shape[1])))


def gelu_parts(values):
    cumul = 0.5 * (1.0 + lax.erf(values * 0.7071067811865476))
    density = jnp.exp(-0.5 * values * values) * 0.3989422804014327
    return (values * cumul, cumul + values * density)


class Scatter:
    def __init__(self, cps, at, S, bufs, axis, a, al, bl):
        self.cps, self.at, self.S, self.axis = cps, at, S, axis
        self.far, self.nm, self.np, self.xb, self.xa = bufs
        n = S.shape[1 + axis]
        self.A, self.B = (0, a), (a, n - a)
        self.Alo, self.Aup = (0, al), (al, a - al)
        self.Blo, self.Bup = (a, bl), (a + bl, n - a - bl)
        self.got = {}

    def idx(self, i, part):
        cut = pl.ds(*part)
        return (i, cut) if self.axis == 0 else (i, slice(None), cut)

    def send(self, key, g, dst, i, part, dev):
        self.got[key] = self.cps.start(
            self.S.at[self.idx(g, part)], dst.at[self.idx(i, part)], dev
        )

    def add(self, g, part, *terms):
        where = self.idx(g, part)
        v = self.S[where].astype(f32)
        for ref, i in terms:
            v = v + ref[self.idx(i, part)].astype(f32)
        self.S[where] = v.astype(bf16)

    def wait(self, key):
        self.got[key].wait_recv()

    def ready(self, other, dy):
        g, k = self.at.chip(other, dy), int(other)
        if dy == 2:
            self.send(("fu", k), g, self.far, k, self.Aup, self.at.YP)
            self.send(("fl", k), g, self.far, k, self.Alo, self.at.YM)
        if dy == 1:
            self.send(("ml", k), g, self.nm, k, self.Alo, self.at.YP)
        if dy == 3:
            self.send(("pu", k), g, self.np, k, self.Aup, self.at.YM)

    def ready_x(self, dy):
        self.send(("x", dy), self.at.chip(True, dy), self.xb, dy, self.B, self.at.X)

    def mid_a(self, k):
        g1, g3 = self.at.chip(bool(k), 1), self.at.chip(bool(k), 3)
        self.wait(("fu", k))
        self.add(g1, self.Aup, (self.far, k))
        self.send(("mu", k), g1, self.nm, k, self.Aup, self.at.YP)
        self.wait(("fl", k))
        self.add(g3, self.Alo, (self.far, k))
        self.send(("pl", k), g3, self.np, k, self.Alo, self.at.YM)

    def mid_b(self, dy):
        g = self.at.chip(False, dy)
        self.wait(("x", dy))
        self.add(g, self.B, (self.xb, dy))
        if dy == 2:
            self.send("bfu", g, self.far, 0, self.Bup, self.at.YP)
            self.send("bfl", g, self.far, 0, self.Blo, self.at.YM)
        elif dy == 1:
            self.send("bml", g, self.nm, 0, self.Blo, self.at.YP)
        else:
            self.send("bpu", g, self.np, 0, self.Bup, self.at.YM)

    def late_a(self):
        for key in ("ml", "mu", "pl", "pu"):
            self.wait((key, 1))
        g = self.at.chip(True, 0)
        self.add(g, self.A, (self.nm, 1), (self.np, 1))
        self.send("xa", g, self.xa, 0, self.A, self.at.X)

    def late_b(self):
        g1, g3 = self.at.chip(False, 1), self.at.chip(False, 3)
        self.wait("bfu")
        self.add(g1, self.Bup, (self.far, 0))
        self.send("bmu", g1, self.nm, 0, self.Bup, self.at.YP)
        self.wait("bfl")
        self.add(g3, self.Blo, (self.far, 0))
        self.send("bpl", g3, self.np, 0, self.Blo, self.at.YM)

    def final(self, fin):
        g = self.at.chip(False, 0)
        for key in ("ml", "mu", "pl", "pu"):
            self.wait((key, 0))
        for key in ("xa", ("x", 0), "bml", "bmu", "bpl", "bpu"):
            self.wait(key)
        for part, last, i in ((self.A, self.xa, 0), (self.B, self.xb, 0)):
            v = self.S[self.idx(g, part)].astype(f32)
            for ref, j in ((self.nm, 0), (self.np, 0), (last, i)):
                v = v + ref[self.idx(j, part)].astype(f32)
            fin[self.idx(0, part)[1:]] = v


def scatter_bufs(shape):
    return [VMEM((n,) + shape, bf16) for n in (2, 2, 2, 4, 1)]


ORDER = [(True, 2), (True, 1), (True, 3), (True, 0), (False, 2), (False, 1), (False, 3), (False, 0)]


def head_kernel(
    tokens, w_in, w_out, teacher, proto_t, center,
    hid_o, slope_o, sn_o, unit_o, recip_o, et_o, stat_o,
    tok, wbuf, pt, lt, et, top, tot, pre, hid, slope, tbuf, part, rbuf, sbuf, send, recv, lsem,
):
    at = Place()
    cps = Copies(send, recv)
    rows, depth = tok.shape
    kk = lt.shape[1]
    peers = [at.X, at.YP, at.YM, at.CO] + [at.proto_peer(d) for d in range(1, 8)]
    greet(peers)
    me = at.slot(False, 0)
    load_pt = pltpu.make_async_copy(proto_t, pt, lsem.at[1])
    load_pt.start()
    own = pltpu.make_async_copy(w_in, wbuf.at[me], lsem.at[0])
    own.start()
    load_tok = pltpu.make_async_copy(tokens, tok, lsem.at[2])
    load_tok.start()
    t = teacher[...].astype(f32)
    tbuf[at.p] = (t * lax.rsqrt(jnp.sum(t * t, axis=1, keepdims=True) + norm_eps)).astype(bf16)
    met(len(peers))
    halves = [
        gather_rows(cps, at, w_in, wbuf, 0, 128, 80, 64, 32),
        gather_rows(cps, at, w_in, wbuf, 128, 128, 64, 64, 32),
    ]

    def advance():
        return list(zip(*[next(g) for g in halves]))

    def accumulate(landed):
        block = wbuf.shape[1] * 2
        for (one, chip), (two, _) in landed:
            one.wait_recv()
            two.wait_recv()
            lhs = tok[:, pl.ds(pl.multiple_of(chip * block, block), block)]

            def tile(j, _):
                cols = pl.ds(pl.multiple_of(j * 256, 256), 256)
                rhs = wbuf[pl.ds(chip * 2, 2), :, cols].reshape(block, 256)
                pre[:, cols] += jnp.dot(lhs, rhs, preferred_element_type=f32)
                return 0

            lax.fori_loop(0, pre.shape[1] // 256, tile, 0)

    tc = [cps.start(tbuf.at[at.p], tbuf.at[at.p], at.proto_peer(d)) for d in range(1, 8)]
    started = advance()
    pre[...] = jnp.zeros_like(pre)
    load_pt.wait()
    for k in tc:
        k.wait_recv()
    tn = tbuf[...].reshape(rows, tbuf.shape[2])
    step = 512

    def score(j, best):
        cols = pl.ds(pl.multiple_of(j * step, step), step)
        v = jnp.dot(tn, pt[:, cols], preferred_element_type=f32)
        v = (v - center[:, cols]) * (1.0 / tau_teacher)
        lt[:, cols] = v
        for q in range(step // 128):
            best = jnp.maximum(best, v[:, q * 128 : (q + 1) * 128])
        return best

    top[...] = lax.fori_loop(0, kk // step, score, jnp.full((rows, 128), -jnp.inf, f32))
    own.wait()
    load_tok.wait()
    first = advance()
    top[...] = jnp.broadcast_to(jnp.max(top[...], axis=1, keepdims=True), (rows, 128))

    def lift(i, _):
        rs = pl.ds(pl.multiple_of(i * 64, 64), 64)
        peak = top[rs, :]

        def tile(j, acc):
            for q in range(4):
                cols = pl.ds(pl.multiple_of(j * 512 + q * 128, 128), 128)
                e = jnp.exp(lt[rs, cols] - peak)
                et[rs, cols] = e.astype(bf16)
                acc = acc + e
            return acc

        tot[rs, :] = lax.fori_loop(0, kk // 512, tile, jnp.zeros((64, 128), f32))
        return 0

    lax.fori_loop(0, rows // 64, lift, 0)
    save = pltpu.make_async_copy(et, et_o, lsem.at[3])
    save.start()
    accumulate(started)
    second = advance()
    stat_o[...] = jnp.concatenate(
        [
            jnp.transpose(top[...])[0:1],
            jnp.sum(jnp.transpose(tot[...]), axis=0, keepdims=True),
            jnp.zeros((6, rows), f32),
        ],
        axis=0,
    )
    accumulate(first)
    accumulate(second)
    third = advance()
    accumulate(third)

    small = part.shape[1]

    def act(q):
        rs = pl.ds(pl.multiple_of(q * small, small), small)
        value, grade = gelu_parts(pre[rs, :])
        slope[rs, :] = grade
        h = value.astype(bf16)
        hid[rs, :] = h
        part[q] = jnp.dot(h, w_out[...], preferred_element_type=f32)

    base = len(cps.all)

    def act_send(i, _):
        q = (at.p + i + 1) % 8
        act(q)
        pltpu.make_async_remote_copy(
            src_ref=part.at[q],
            dst_ref=rbuf.at[i],
            send_sem=send.at[base + i],
            recv_sem=recv.at[base + i],
            device_id=(at.r, q),
            device_id_type=MESH,
        ).start()
        return 0

    lax.fori_loop(0, 7, act_send, 0)
    act(at.p)
    save_hid = pltpu.make_async_copy(hid, hid_o, lsem.at[4])
    save_hid.start()
    save_slope = pltpu.make_async_copy(slope, slope_o, lsem.at[5])
    save_slope.start()
    total = part[at.p]
    for i in range(7):
        cps.expect(rbuf.at[i], base + i, at.proto_peer(i + 1)).wait_recv()
        total = total + rbuf[i]
    recip = lax.rsqrt(jnp.sum(total * total, axis=1, keepdims=True) + norm_eps)
    unit = total * recip
    sbuf[at.p] = unit.astype(bf16)
    sc = [cps.start(sbuf.at[at.p], sbuf.at[at.p], at.proto_peer(d)) for d in range(1, 8)]
    unit_o[...] = unit
    recip_o[...] = jnp.broadcast_to(recip, recip_o.shape)
    for k in sc:
        k.wait_recv()
    sn_o[...] = sbuf[...].reshape(rows, sbuf.shape[2])
    save.wait()
    save_hid.wait()
    save_slope.wait()
    cps.finish()


def head(tokens, w_in, w_out, teacher_z, proto_teacher, center):
    rows, depth = tokens.shape
    hidden = w_in.shape[1]
    wide = w_out.shape[1]
    kk = proto_teacher.shape[1]
    small = teacher_z.shape[0]
    shp = jax.ShapeDtypeStruct
    copies = 40 + 7 + 7 + 7
    return pl.pallas_call(
        head_kernel,
        out_shape=(
            shp((rows, hidden), bf16), shp((rows, hidden), f32), shp((rows, wide), bf16),
            shp((small, wide), f32), shp((small, 128), f32), shp((rows, kk), bf16), shp((8, rows), f32),
        ),
        in_specs=[aspec(), aspec(), vspec(), vspec(), aspec(), vspec()],
        out_specs=(aspec(), aspec(), vspec(), vspec(), vspec(), aspec(), vspec()),
        scratch_shapes=[
            VMEM((rows, depth), bf16), VMEM((16,) + w_in.shape, bf16),
            VMEM(proto_teacher.shape, bf16), VMEM((rows, kk), f32), VMEM((rows, kk), bf16),
            VMEM((rows, 128), f32), VMEM((rows, 128), f32),
            VMEM((rows, hidden), f32), VMEM((rows, hidden), bf16), VMEM((rows, hidden), f32),
            VMEM((8, small, wide), bf16), VMEM((8, small, wide), f32),
            VMEM((7, small, wide), f32), VMEM((8, small, wide), bf16),
            pltpu.SemaphoreType.DMA((copies,)), pltpu.SemaphoreType.DMA((copies,)),
            pltpu.SemaphoreType.DMA((6,)),
        ],
        compiler_params=pltpu.CompilerParams(
            collective_id=0, has_side_effects=True, vmem_limit_bytes=62 * 2**20
        ),
        name="head",
    )(tokens, w_in, w_out, teacher_z, proto_teacher, center[None, :])


def along(col):
    return jnp.transpose(col)


def middle_kernel(
    sn, proto_s, et_in, stat_t, image, unit, recip,
    dbott_o, pgrad_o, loss_o,
    ps, et, ls, gs, snt, ms, ss, cs, cbuf, stats, fsb, ftb,
    S, snd, rc, far, nm, np_, xb, xa, fin, fcore,
    S_, snd_, rc_, far_, nm_, np__, xb_, xa_, fin_, fcore_,
    dacc, dpart, drecv, dbuf, send, recv, lsem,
):
    at = Place()
    cps = Copies(send, recv)
    rows, kk = ls.shape
    half = kk // 2
    peers = [at.proto_peer(d) for d in range(1, 8)] + [at.row_peer(d) for d in range(1, 16)]
    greet(peers)
    load_ps = pltpu.make_async_copy(proto_s, ps, lsem.at[0])
    load_ps.start()
    load_et = pltpu.make_async_copy(et_in, et, lsem.at[1])
    load_et.start()
    snt[...] = jnp.transpose(sn[...])
    images = cbuf.shape[1]
    onehot = (lax.broadcasted_iota(jnp.int32, (images, rows), 0) == image[...]).astype(f32)
    cbuf[at.r] = jnp.broadcast_to(jnp.sum(onehot, axis=1, keepdims=True), cbuf.shape[1:])
    load_ps.wait()
    step = 512

    def one(j, top):
        cols = pl.ds(pl.multiple_of(j * step, step), step)
        v = jnp.dot(sn[...], ps[:, cols], preferred_element_type=f32) * (1.0 / tau_student)
        ls[:, cols] = v
        for q in range(step // 128):
            top = jnp.maximum(top, v[:, q * 128 : (q + 1) * 128])
        return top

    ms[...] = lax.fori_loop(0, kk // step, one, jnp.full((rows, 128), -jnp.inf, f32))
    met(len(peers))
    cc = [cps.start(cbuf.at[at.r], cbuf.at[at.r], at.row_peer(d)) for d in range(1, 16)]
    ms[...] = jnp.broadcast_to(jnp.max(ms[...], axis=1, keepdims=True), (rows, 128))
    load_et.wait()

    def two(i, _):
        rs = pl.ds(pl.multiple_of(i * 64, 64), 64)
        peak = ms[rs, :]

        def tile(j, acc):
            s, c = acc
            for q in range(4):
                cols = pl.ds(pl.multiple_of(j * 512 + q * 128, 128), 128)
                d = ls[rs, cols] - peak
                e = jnp.exp(d)
                ls[rs, cols] = e
                s = s + e
                c = c + et[rs, cols].astype(f32) * d
            return s, c

        zero = jnp.zeros((64, 128), f32)
        ss[rs, :], cs[rs, :] = lax.fori_loop(0, kk // 512, tile, (zero, zero))
        return 0

    lax.fori_loop(0, rows // 64, two, 0)
    stats[at.p] = jnp.concatenate(
        [
            stat_t[0:2],
            along(ms[...])[0:1],
            jnp.sum(along(ss[...]), axis=0, keepdims=True),
            jnp.sum(along(cs[...]), axis=0, keepdims=True),
            jnp.zeros((3, rows), f32),
        ],
        axis=0,
    )
    sc = [cps.start(stats.at[at.p], stats.at[at.p], at.proto_peer(d)) for d in range(1, 8)]
    for k in cc:
        k.wait_recv()
    counts = jnp.sum(cbuf[...], axis=0)[:, 0:1]
    w_row = 1.0 / (images * jnp.sum(onehot * counts, axis=0, keepdims=True))
    for k in sc:
        k.wait_recv()
    table = [stats[q] for q in range(8)]
    top_t = table[0][0:1]
    top_s = table[0][2:3]
    for q in table[1:]:
        top_t = jnp.maximum(top_t, q[0:1])
        top_s = jnp.maximum(top_s, q[2:3])
    total_t = total_s = cross = jnp.zeros((1, rows), f32)
    for q in table:
        scale = jnp.exp(q[0:1] - top_t)
        total_t = total_t + q[1:2] * scale
        total_s = total_s + q[3:4] * jnp.exp(q[2:3] - top_s)
        cross = cross + scale * (q[4:5] + q[1:2] * (q[2:3] - top_s))
    cross = jnp.log(total_s) - cross / total_t
    loss_o[...] = jnp.broadcast_to(w_row * cross, loss_o.shape)
    mine = stats[at.p]
    lift = (loss_scale / tau_student) * w_row
    fsb[...] = across(lift * jnp.exp(mine[2:3] - top_s) / total_s)
    ftb[...] = across(lift * jnp.exp(mine[0:1] - top_t) / total_t)
    dacc[...] = jnp.zeros_like(dacc)

    def grads(base, dst):
        def one(j, _):
            first = base + j * step

            def block(i, _):
                rs = pl.ds(pl.multiple_of(i * 64, 64), 64)
                f_s, f_t = fsb[rs, :], ftb[rs, :]
                for q in range(step // 128):
                    cols = pl.ds(pl.multiple_of(first + q * 128, 128), 128)
                    v = ls[rs, cols] * f_s - et[rs, cols].astype(f32) * f_t
                    gs[rs, q * 128 : (q + 1) * 128] = v.astype(bf16)
                return 0

            lax.fori_loop(0, rows // 64, block, 0)
            cols = pl.ds(pl.multiple_of(first, step), step)
            g = gs[...]
            v = jnp.dot(snt[...], g, preferred_element_type=f32)
            dst[:, :, pl.ds(pl.multiple_of(j * step, step), step)] = v.astype(bf16).reshape(
                dst.shape[0], dst.shape[1], step
            )
            d = lax.dot_general(
                g, ps[:, cols], (((1,), (1,)), ((), ())), preferred_element_type=f32
            )
            dacc[...] += d
            return 0

        lax.fori_loop(0, dst.shape[2] // step, one, 0)

    quarter = half // 2
    mine_at, other_at = at.c * half, (1 - at.c) * half
    one = Scatter(cps, at, S, (far, nm, np_, xb, xa), 1, 896, 384, 256)
    two = Scatter(cps, at, S_, (far_, nm_, np__, xb_, xa_), 1, 896, 512, 384)

    def merge(rs, S, rc, swap):
        swap.wait_recv()
        for other, dy in ORDER:
            g = at.chip(other, dy)
            S[g] = (S[g].astype(f32) + rc[g].astype(f32)).astype(bf16)
            rs.ready(other, dy)
            if other:
                rs.ready_x(dy)

    grads(other_at, snd)
    swap = cps.start(snd, rc, at.CO)
    grads(mine_at, S)
    grads(other_at + quarter, snd_)
    swap_ = cps.start(snd_, rc_, at.CO)
    merge(one, S, rc, swap)
    grads(mine_at + quarter, S_)
    dpart[...] = dacc[...].astype(bf16).reshape(dpart.shape)
    dc = [
        cps.start(dpart.at[(at.p + d) % 8], drecv.at[d], at.proto_peer(d)) for d in range(1, 8)
    ]
    one.mid_a(1)
    merge(two, S_, rc_, swap_)
    one.mid_b(2)
    one.mid_a(0)
    total = dpart[at.p].astype(f32)
    for d in range(1, 8):
        dc[d - 1].wait_recv()
        total = total + drecv[d].astype(f32)
    u, r = unit[...], recip[:, 0:1]
    dbuf[at.p] = (r * (total - u * jnp.sum(u * total, axis=1, keepdims=True))).astype(bf16)
    bc = [cps.start(dbuf.at[at.p], dbuf.at[at.p], at.proto_peer(d)) for d in range(1, 8)]
    one.mid_b(1)
    one.late_a()
    one.mid_b(3)
    two.mid_a(1)
    one.late_b()
    two.mid_b(2)
    two.mid_a(0)
    two.mid_b(1)
    two.late_a()
    two.mid_b(3)
    two.late_b()
    n = fcore.shape[0]
    keep, give = pl.ds(pl.multiple_of(at.c * n, 8), n), pl.ds(pl.multiple_of((1 - at.c) * n, 8), n)

    def settle(rs, fin, fcore, where):
        rs.final(fin)
        fc = cps.start(fin.at[give], fcore, at.CO)
        pgrad_o[:, pl.ds(pl.multiple_of(mine_at + where, quarter), quarter)] = fin[keep, :]
        return fc

    fc = settle(one, fin, fcore, 0)
    for k in bc:
        k.wait_recv()
    dbott_o[...] = dbuf[...].reshape(dbott_o.shape)
    fc_ = settle(two, fin_, fcore_, quarter)
    fc.wait_recv()
    pgrad_o[:, pl.ds(pl.multiple_of(other_at, half), quarter)] = fcore[...]
    fc_.wait_recv()
    pgrad_o[:, pl.ds(pl.multiple_of(other_at + quarter, quarter), quarter)] = fcore_[...]
    cps.finish()


def middle(sn, proto_s, et, stat_t, image, unit, recip):
    rows, wide = sn.shape
    kk = proto_s.shape[1]
    small = unit.shape[0]
    shp = jax.ShapeDtypeStruct
    chunk = (wide // 8, kk // 4)
    copies = 15 + 7 + 7 + 7 + 2 * (1 + 23 + 1)
    lane = VMEM((rows, 128), f32)
    part = [VMEM((8,) + chunk, bf16)] * 3 + scatter_bufs(chunk)
    part += [VMEM(chunk, f32), VMEM((chunk[0] // 2, chunk[1]), f32)]
    return pl.pallas_call(
        middle_kernel,
        out_shape=(shp((rows, wide), bf16), shp((wide // 16, kk), f32), shp((8, rows), f32)),
        in_specs=[vspec(), aspec(), aspec()] + [vspec()] * 4,
        out_specs=(vspec(),) * 3,
        scratch_shapes=[
            VMEM((wide, kk), bf16), VMEM((rows, kk), bf16), VMEM((rows, kk), f32), VMEM((rows, 512), bf16),
            VMEM((wide, rows), bf16), lane, lane, lane, VMEM((16, 64, 128), f32), VMEM((8, 8, rows), f32), lane, lane,
            *(part + part),
            VMEM((rows, wide), f32), VMEM((8, small, wide), bf16), VMEM((8, small, wide), bf16), VMEM((8, small, wide), bf16),
            pltpu.SemaphoreType.DMA((copies,)), pltpu.SemaphoreType.DMA((copies,)),
            pltpu.SemaphoreType.DMA((2,)),
        ],
        compiler_params=pltpu.CompilerParams(
            collective_id=1, has_side_effects=True, vmem_limit_bytes=62 * 2**20
        ),
        name="middle",
    )(sn, proto_s, et, stat_t, image, unit, recip)


def tail_kernel(
    tokens, hid_in, slope_in, dbott, w_out, loss_in,
    wgrad_o, wout_o, loss_o,
    tok, hid, slope, dp, S, snd, rc, far, nm, np_, xb, xa, fin, fcore,
    W, S2, rc2, r2, own2, wbuf, lbuf, send, recv, lsem,
):
    at = Place()
    cps = Copies(send, recv)
    rows, hidden = dp.shape
    half = hidden // 2
    peers = [at.row_peer(d) for d in range(1, 16)]
    greet(peers)
    load_tok = pltpu.make_async_copy(tokens, tok, lsem.at[0])
    load_tok.start()
    load_hid = pltpu.make_async_copy(hid_in, hid, lsem.at[2])
    load_hid.start()
    load_slope = pltpu.make_async_copy(slope_in, slope, lsem.at[1])
    load_slope.start()
    lbuf[at.r] = jnp.broadcast_to(
        jnp.sum(loss_in[...], axis=1, keepdims=True), lbuf.shape[1:]
    )
    load_hid.wait()
    small = W.shape[2]
    for j in range(hidden // 256):
        cols = slice(j * 256, (j + 1) * 256)
        v = lax.dot_general(
            hid[:, cols], dbott[...], (((0,), (0,)), ((), ())), preferred_element_type=f32
        ).astype(bf16)
        for i in range(256 // small):
            k = j * (256 // small) + i
            W[k % 2, k // 2] = v[i * small : (i + 1) * small]
    met(len(peers))
    swap2 = cps.start(W.at[1 - at.c], rc2, at.CO)
    lc = [cps.start(lbuf.at[at.r], lbuf.at[at.r], at.row_peer(d)) for d in range(1, 16)]
    load_slope.wait()

    def back(j, _):
        cols = pl.ds(pl.multiple_of(j * 256, 256), 256)
        v = lax.dot_general(
            dbott[...], w_out[cols, :], (((1,), (1,)), ((), ())), preferred_element_type=f32
        )
        dp[:, cols] = (v * slope[:, cols]).astype(bf16)
        return 0

    lax.fori_loop(0, hidden // 256, back, 0)
    load_tok.wait()
    rs = Scatter(cps, at, S, (far, nm, np_, xb, xa), 0, 288, 128, 112)
    swaps = {}

    def chunk(other, dy):
        g = at.chip(other, dy)
        lhs = pl.ds(pl.multiple_of(g * 512, 512), 512)
        for dst, side in ((snd, 1 - at.c), (S, at.c)):
            rhs = pl.ds(pl.multiple_of(side * half, half), half)
            dst[g] = lax.dot_general(
                tok[:, lhs], dp[:, rhs], (((0,), (0,)), ((), ())), preferred_element_type=f32
            ).astype(bf16)
            if dst is snd:
                swaps[other, dy] = cps.start(snd.at[g], rc.at[g], at.CO)

    def merge(other, dy):
        g = at.chip(other, dy)
        swaps[other, dy].wait_recv()
        S[g] = (S[g].astype(f32) + rc[g].astype(f32)).astype(bf16)
        rs.ready(other, dy)
        if other:
            rs.ready_x(dy)

    swap2.wait_recv()
    S2[...] = (W[at.c].astype(f32) + rc2[...].astype(f32)).astype(bf16)
    around = [k for k in ORDER if k != (False, 0)]
    sums = [
        cps.start(S2.at[at.chip(o, dy)], r2.at[k], at.dev(at.slot(o, dy)))
        for k, (o, dy) in enumerate(around)
    ]
    spread = []
    for i, key in enumerate(ORDER):
        chunk(*key)
        if i > 0:
            merge(*ORDER[i - 1])
        if i == 4:
            total = S2[at.chip(False, 0)].astype(f32)
            for k, cp in enumerate(sums):
                cp.wait_recv()
                total = total + r2[k].astype(f32)
            own2[...] = total.astype(bf16)
            wbuf[at.r] = own2[...]
            spread = [
                cps.start(own2, wbuf.at[at.r], at.dev(at.slot(o, dy))) for o, dy in around
            ]
            spread.append(cps.start(own2, wbuf.at[at.r], at.CO))
        if i == 6:
            rs.mid_a(1)
    rs.mid_b(2)
    merge(*ORDER[-1])
    rs.mid_a(0)
    rs.mid_b(1)
    rs.late_a()
    rs.mid_b(3)
    landed = [spread[-1]]
    for (o, dy), cp in zip(around, spread):
        cp.wait_recv()
        ref = wbuf.at[at.slot(o, (4 - dy) % 4)]
        landed.append(cps.start(ref, ref, at.CO))
    rs.late_b()
    rs.final(fin)
    n = fcore.shape[0]
    fc = cps.start(fin.at[pl.ds(pl.multiple_of((1 - at.c) * n, n), n)], fcore, at.CO)
    wgrad_o[:, pl.ds(pl.multiple_of(at.c * half, half), half)] = fin[pl.ds(pl.multiple_of(at.c * n, n), n), :]
    for copy in landed:
        copy.wait_recv()
    wout_o[...] = wbuf[...].reshape(wout_o.shape)
    for k in lc:
        k.wait_recv()
    loss_o[...] = jnp.sum(lbuf[...], axis=0)
    fc.wait_recv()
    wgrad_o[:, pl.ds(pl.multiple_of((1 - at.c) * half, half), half)] = fcore[...]
    cps.finish()


def tail(tokens, hid, slope, dbott, w_out, loss_row):
    rows, depth = tokens.shape
    hidden, wide = w_out.shape
    shp = jax.ShapeDtypeStruct
    block = (depth // 8, hidden // 2)
    small = (hidden // 16, wide)
    copies = 15 + 1 + 8 + 23 + 7 + 8 + 7 + 1
    return pl.pallas_call(
        tail_kernel,
        out_shape=(shp((depth // 16, hidden), f32), shp((hidden, wide), bf16), shp((8, 128), f32)),
        in_specs=[aspec(), aspec(), aspec(), vspec(), vspec(), vspec()],
        out_specs=(vspec(),) * 3,
        scratch_shapes=[
            VMEM((rows, depth), bf16), VMEM((rows, hidden), bf16), VMEM((rows, hidden), f32), VMEM((rows, hidden), bf16),
            VMEM((8,) + block, bf16), VMEM((8,) + block, bf16), VMEM((8,) + block, bf16),
            *scatter_bufs(block), VMEM(block, f32), VMEM((block[0] // 2, block[1]), f32),
            VMEM((2, 8) + small, bf16), VMEM((8,) + small, bf16), VMEM((8,) + small, bf16),
            VMEM((7,) + small, bf16), VMEM(small, bf16), VMEM((16,) + small, bf16),
            VMEM((16, 8, 128), f32),
            pltpu.SemaphoreType.DMA((copies,)), pltpu.SemaphoreType.DMA((copies,)),
            pltpu.SemaphoreType.DMA((3,)),
        ],
        compiler_params=pltpu.CompilerParams(
            collective_id=2, has_side_effects=True, vmem_limit_bytes=62 * 2**20
        ),
        name="tail",
    )(tokens, hid, slope, dbott, w_out, loss_row)


def close_kernel(wg, wo, pg, loss, wg_o, wo_o, pg_o, loss_o):
    wg_o[...] = wg[...]
    wo_o[...] = wo[...].astype(f32)
    pg_o[...] = pg[...]
    loss_o[0, 0] = loss[0, 0]


def close(wg, wo, pg, loss):
    shp = jax.ShapeDtypeStruct
    n = 2
    specs = [
        pl.BlockSpec((wg.shape[0] // n, wg.shape[1]), lambda i: (i, 0)),
        pl.BlockSpec((wo.shape[0] // n, wo.shape[1]), lambda i: (i, 0)),
        pl.BlockSpec((pg.shape[0], pg.shape[1] // n), lambda i: (0, i)),
    ]
    return pl.pallas_call(
        close_kernel,
        grid=(n,),
        out_shape=(shp(wg.shape, f32), shp(wo.shape, f32), shp(pg.shape, f32), shp((1, 1), f32)),
        in_specs=specs + [pl.BlockSpec((8, 128), lambda i: (0, 0))],
        out_specs=tuple(specs) + (pl.BlockSpec((1, 1), lambda i: (0, 0), memory_space=pltpu.SMEM),),
        name="close",
    )(wg, wo, pg, loss)


def on_device(tokens, w_in, w_out, teacher_z, proto_student, proto_teacher, center, image_of):
    hidden, slope, student_n, unit, recip, exp_t, stat_t = head(
        tokens, w_in, w_out, teacher_z, proto_teacher, center
    )
    dbott, proto_grad, loss_row = middle(
        student_n, proto_student, exp_t, stat_t, image_of[None, :], unit, recip
    )
    w_in_grad, w_out_grad, loss = tail(tokens, hidden, slope, dbott, w_out, loss_row)
    w_in_grad, w_out_grad, proto_grad, loss = close(w_in_grad, w_out_grad, proto_grad, loss)
    return (loss[0, 0], w_in_grad, w_out_grad, proto_grad)


def solution(mesh):
    return jax.shard_map(
        on_device,
        mesh=mesh,
        in_specs=(
            P("row", None),
            P("row", "proto"),
            P("proto", None),
            P(("row", "proto"), None),
            P(None, "proto"),
            P(None, "proto"),
            P("proto"),
            P("row"),
        ),
        out_specs=(P(), P("row", "proto"), P("proto", None), P("row", "proto")),
        check_vma=False,
    )
```

```python
import jax
import jax.numpy as jnp
from jax import lax
from jax.sharding import PartitionSpec as P
from jax.experimental import pallas as pl
from jax.experimental.pallas import tpu as pltpu

tau_teacher = 0.07
tau_student = 0.1
loss_scale = 1048576.0
norm_eps = 1e-06
MESH = pl.DeviceIdType.MESH
VMEM = pltpu.VMEM
f32 = jnp.float32
bf16 = jnp.bfloat16


def vspec():
    return pl.BlockSpec(memory_space=pltpu.VMEM)


def aspec():
    return pl.BlockSpec(memory_space=pl.ANY)


class Place:
    def __init__(self):
        self.r = lax.axis_index("row")
        self.p = lax.axis_index("proto")
        self.xh = self.r // 8
        self.y = (self.r // 2) % 4
        self.c = self.r % 2

    def chip(self, other, dy):
        fam = 1 - self.xh if other else self.xh
        return fam * 4 + (self.y + dy) % 4

    def slot(self, other, dy, core=None):
        return self.chip(other, dy) * 2 + (self.c if core is None else core)

    def dev(self, row):
        return (row, self.p)

    @property
    def X(self):
        return self.dev(self.slot(True, 0))

    @property
    def YP(self):
        return self.dev(self.slot(False, 1))

    @property
    def YM(self):
        return self.dev(self.slot(False, 3))

    @property
    def CO(self):
        return self.dev(self.slot(False, 0, 1 - self.c))

    def row_peer(self, d):
        return ((self.r + d) % 16, self.p)

    def proto_peer(self, d):
        return (self.r, (self.p + d) % 8)


class Copies:
    def __init__(self, send, recv):
        self.send, self.recv, self.all = send, recv, []

    def start(self, src, dst, dev):
        i = len(self.all)
        cp = pltpu.make_async_remote_copy(
            src_ref=src,
            dst_ref=dst,
            send_sem=self.send.at[i],
            recv_sem=self.recv.at[i],
            device_id=dev,
            device_id_type=MESH,
        )
        cp.start()
        self.all.append(cp)
        return cp

    def expect(self, dst, i, dev):
        cp = pltpu.make_async_remote_copy(
            src_ref=dst,
            dst_ref=dst,
            send_sem=self.send.at[i],
            recv_sem=self.recv.at[i],
            device_id=dev,
            device_id_type=MESH,
        )
        self.all.append(cp)
        return cp

    def finish(self):
        for cp in self.all:
            cp.wait_send()


def greet(peers):
    bar = pltpu.get_barrier_semaphore()
    for dev in peers:
        pl.semaphore_signal(bar, inc=1, device_id=dev, device_id_type=MESH)


def met(count):
    pl.semaphore_wait(pltpu.get_barrier_semaphore(), count)


def gather_rows(cps, at, own, buf, base, n, a, h, al):
    every = (0, n)
    up, lo = (h, n - h), (0, h)
    A, B = (0, a), (a, n - a)
    aup, alo = (al, a - al), (0, al)

    def on(slot, part, dev, src=None):
        ref = buf.at[slot, pl.ds(base + part[0], part[1])]
        return cps.start(ref if src is None else src, ref, dev)

    me = at.slot(False, 0)
    mine = own.at[pl.ds(base, n)]
    x0 = on(me, every, at.X, mine)
    p0 = on(me, every, at.YP, mine)
    m0 = on(me, every, at.YM, mine)
    c0 = on(me, every, at.CO, mine)
    yield [(c0, at.chip(False, 0))]
    sx = at.slot(True, 0)
    sm, sp, sf = at.slot(False, 3), at.slot(False, 1), at.slot(False, 2)
    xm, xp, xf = at.slot(True, 3), at.slot(True, 1), at.slot(True, 2)
    x0.wait_recv()
    xap = on(sx, A, at.YP)
    xam = on(sx, A, at.YM)
    xc = on(sx, every, at.CO)
    p0.wait_recv()
    fup = on(sm, up, at.YP)
    bm = on(sm, B, at.X)
    cm = on(sm, every, at.CO)
    m0.wait_recv()
    flo = on(sp, lo, at.YM)
    bp = on(sp, B, at.X)
    cp = on(sp, every, at.CO)
    yield [(xc, at.chip(True, 0)), (cm, at.chip(False, 3)), (cp, at.chip(False, 1))]
    xap.wait_recv()
    gup = on(xm, aup, at.YP)
    xam.wait_recv()
    glo = on(xp, alo, at.YM)
    fup.wait_recv()
    flo.wait_recv()
    bf = on(sf, B, at.X)
    cf = on(sf, every, at.CO)
    bm.wait_recv()
    cxm = on(xm, every, at.CO)
    bp.wait_recv()
    cxp = on(xp, every, at.CO)
    yield [(cf, at.chip(False, 2)), (cxm, at.chip(True, 3)), (cxp, at.chip(True, 1))]
    gup.wait_recv()
    glo.wait_recv()
    bf.wait_recv()
    cxf = on(xf, every, at.CO)
    yield [(cxf, at.chip(True, 2))]


def gather_small(cps, at, buf):
    xl = at.p % 2
    other = at.p + 1 - 2 * xl
    ring = [(at.r, (at.p + 2 * k) % 8) for k in (1, 2, 3)]
    over = cps.start(buf.at[at.p], buf.at[at.p], (at.r, other))
    first = [cps.start(buf.at[at.p], buf.at[at.p], dev) for dev in ring]
    yield
    over.wait_recv()
    second = [cps.start(buf.at[other], buf.at[other], dev) for dev in ring]
    yield
    for k in first + second:
        k.wait_recv()
    yield


def across(row):
    return jnp.transpose(jnp.broadcast_to(row, (128, row.shape[1])))


def gelu_parts(values):
    cumul = 0.5 * (1.0 + lax.erf(values * 0.7071067811865476))
    density = jnp.exp(-0.5 * values * values) * 0.3989422804014327
    return (values * cumul, cumul + values * density)


class Scatter:
    def __init__(self, cps, at, S, bufs, axis, a, al, bl):
        self.cps, self.at, self.S, self.axis = cps, at, S, axis
        self.far, self.nm, self.np, self.xb, self.xa = bufs
        n = S.shape[1 + axis]
        self.A, self.B = (0, a), (a, n - a)
        self.Alo, self.Aup = (0, al), (al, a - al)
        self.Blo, self.Bup = (a, bl), (a + bl, n - a - bl)
        self.got = {}

    def idx(self, i, part):
        cut = pl.ds(*part)
        return (i, cut) if self.axis == 0 else (i, slice(None), cut)

    def send(self, key, g, dst, i, part, dev):
        self.got[key] = self.cps.start(
            self.S.at[self.idx(g, part)], dst.at[self.idx(i, part)], dev
        )

    def add(self, g, part, *terms):
        where = self.idx(g, part)
        v = self.S[where].astype(f32)
        for ref, i in terms:
            v = v + ref[self.idx(i, part)].astype(f32)
        self.S[where] = v.astype(bf16)

    def wait(self, key):
        self.got[key].wait_recv()

    def ready(self, other, dy):
        g, k = self.at.chip(other, dy), int(other)
        if dy == 2:
            self.send(("fu", k), g, self.far, k, self.Aup, self.at.YP)
            self.send(("fl", k), g, self.far, k, self.Alo, self.at.YM)
        if dy == 1:
            self.send(("ml", k), g, self.nm, k, self.Alo, self.at.YP)
        if dy == 3:
            self.send(("pu", k), g, self.np, k, self.Aup, self.at.YM)

    def ready_x(self, dy):
        self.send(("x", dy), self.at.chip(True, dy), self.xb, dy, self.B, self.at.X)

    def mid_a(self, k):
        g1, g3 = self.at.chip(bool(k), 1), self.at.chip(bool(k), 3)
        self.wait(("fu", k))
        self.add(g1, self.Aup, (self.far, k))
        self.send(("mu", k), g1, self.nm, k, self.Aup, self.at.YP)
        self.wait(("fl", k))
        self.add(g3, self.Alo, (self.far, k))
        self.send(("pl", k), g3, self.np, k, self.Alo, self.at.YM)

    def mid_b(self, dy):
        g = self.at.chip(False, dy)
        self.wait(("x", dy))
        self.add(g, self.B, (self.xb, dy))
        if dy == 2:
            self.send("bfu", g, self.far, 0, self.Bup, self.at.YP)
            self.send("bfl", g, self.far, 0, self.Blo, self.at.YM)
        elif dy == 1:
            self.send("bml", g, self.nm, 0, self.Blo, self.at.YP)
        else:
            self.send("bpu", g, self.np, 0, self.Bup, self.at.YM)

    def late_a(self):
        for key in ("ml", "mu", "pl", "pu"):
            self.wait((key, 1))
        g = self.at.chip(True, 0)
        self.add(g, self.A, (self.nm, 1), (self.np, 1))
        self.send("xa", g, self.xa, 0, self.A, self.at.X)

    def late_b(self):
        g1, g3 = self.at.chip(False, 1), self.at.chip(False, 3)
        self.wait("bfu")
        self.add(g1, self.Bup, (self.far, 0))
        self.send("bmu", g1, self.nm, 0, self.Bup, self.at.YP)
        self.wait("bfl")
        self.add(g3, self.Blo, (self.far, 0))
        self.send("bpl", g3, self.np, 0, self.Blo, self.at.YM)

    def final(self, fin):
        g = self.at.chip(False, 0)
        for key in ("ml", "mu", "pl", "pu"):
            self.wait((key, 0))
        for key in ("xa", ("x", 0), "bml", "bmu", "bpl", "bpu"):
            self.wait(key)
        for part, last, i in ((self.A, self.xa, 0), (self.B, self.xb, 0)):
            v = self.S[self.idx(g, part)].astype(f32)
            for ref, j in ((self.nm, 0), (self.np, 0), (last, i)):
                v = v + ref[self.idx(j, part)].astype(f32)
            fin[self.idx(0, part)[1:]] = v


def scatter_bufs(shape):
    return [VMEM((n,) + shape, bf16) for n in (2, 2, 2, 4, 1)]


ORDER = [(True, 2), (True, 1), (True, 3), (True, 0), (False, 2), (False, 1), (False, 3), (False, 0)]


def head_kernel(
    tokens, w_in, w_out, teacher, proto_t, center,
    hid_o, slope_o, sn_o, unit_o, recip_o, et_o, stat_o,
    tok, wbuf, pt, lt, et, top, tot, pre, hid, slope, tbuf, part, rbuf, sbuf, send, recv, lsem,
):
    at = Place()
    cps = Copies(send, recv)
    rows, depth = tok.shape
    kk = lt.shape[1]
    peers = [at.X, at.YP, at.YM, at.CO] + [at.proto_peer(d) for d in range(1, 8)]
    greet(peers)
    me = at.slot(False, 0)
    load_pt = pltpu.make_async_copy(proto_t, pt, lsem.at[1])
    load_pt.start()
    own = pltpu.make_async_copy(w_in, wbuf.at[me], lsem.at[0])
    own.start()
    load_tok = pltpu.make_async_copy(tokens, tok, lsem.at[2])
    load_tok.start()
    t = teacher[...].astype(f32)
    tbuf[at.p] = (t * lax.rsqrt(jnp.sum(t * t, axis=1, keepdims=True) + norm_eps)).astype(bf16)
    met(len(peers))
    halves = [
        gather_rows(cps, at, w_in, wbuf, 0, 128, 80, 64, 32),
        gather_rows(cps, at, w_in, wbuf, 128, 128, 64, 64, 32),
    ]

    def accumulate(*landed):
        block = wbuf.shape[1] * 2
        for (one, chip), (two, _) in zip(*landed):
            one.wait_recv()
            two.wait_recv()
            lhs = tok[:, pl.ds(pl.multiple_of(chip * block, block), block)]

            def tile(j, _):
                cols = pl.ds(pl.multiple_of(j * 256, 256), 256)
                rhs = wbuf[pl.ds(chip * 2, 2), :, cols].reshape(block, 256)
                pre[:, cols] += jnp.dot(lhs, rhs, preferred_element_type=f32)
                return 0

            lax.fori_loop(0, pre.shape[1] // 256, tile, 0)

    teach = gather_small(cps, at, tbuf)
    next(teach)
    a0, b0 = (next(g) for g in halves)
    pre[...] = jnp.zeros_like(pre)
    load_pt.wait()
    next(teach)
    a1 = next(halves[0])
    next(teach)
    tn = tbuf[...].reshape(rows, tbuf.shape[2])
    step = 512

    def score(j, best):
        cols = pl.ds(pl.multiple_of(j * step, step), step)
        v = jnp.dot(tn, pt[:, cols], preferred_element_type=f32)
        v = (v - center[:, cols]) * (1.0 / tau_teacher)
        lt[:, cols] = v
        for q in range(step // 128):
            best = jnp.maximum(best, v[:, q * 128 : (q + 1) * 128])
        return best

    top[...] = lax.fori_loop(0, kk // step, score, jnp.full((rows, 128), -jnp.inf, f32))
    b1 = next(halves[1])
    top[...] = jnp.broadcast_to(jnp.max(top[...], axis=1, keepdims=True), (rows, 128))

    def lift(i, _):
        rs = pl.ds(pl.multiple_of(i * 64, 64), 64)
        peak = top[rs, :]

        def tile(j, acc):
            for q in range(8):
                cols = pl.ds(pl.multiple_of(j * 1024 + q * 128, 128), 128)
                e = jnp.exp(lt[rs, cols] - peak)
                et[rs, cols] = e.astype(bf16)
                acc = acc + e
            return acc

        tot[rs, :] = lax.fori_loop(0, kk // 1024, tile, jnp.zeros((64, 128), f32))
        return 0

    lax.fori_loop(0, rows // 128, lift, 0)
    own.wait()
    load_tok.wait()
    a2 = next(halves[0])
    lax.fori_loop(rows // 128, rows // 64, lift, 0)
    save = pltpu.make_async_copy(et, et_o, lsem.at[3])
    save.start()
    b2 = next(halves[1])
    accumulate(a0, b0)
    accumulate(a1, b1)
    a3 = next(halves[0])
    accumulate(a2, b2)
    b3 = next(halves[1])
    stat_o[...] = jnp.concatenate(
        [
            jnp.transpose(top[...])[0:1],
            jnp.sum(jnp.transpose(tot[...]), axis=0, keepdims=True),
            jnp.zeros((6, rows), f32),
        ],
        axis=0,
    )
    accumulate(a3, b3)

    small = part.shape[1]

    def act(q):
        rs = pl.ds(pl.multiple_of(q * small, small), small)
        value, grade = gelu_parts(pre[rs, :])
        slope[rs, :] = grade
        h = value.astype(bf16)
        hid[rs, :] = h
        part[q] = jnp.dot(h, w_out[...], preferred_element_type=f32)

    base = len(cps.all)

    def act_send(i, _):
        q = (at.p + i + 1) % 8
        act(q)
        pltpu.make_async_remote_copy(
            src_ref=part.at[q],
            dst_ref=rbuf.at[i],
            send_sem=send.at[base + i],
            recv_sem=recv.at[base + i],
            device_id=(at.r, q),
            device_id_type=MESH,
        ).start()
        return 0

    lax.fori_loop(0, 7, act_send, 0)
    act(at.p)
    save_hid = pltpu.make_async_copy(hid, hid_o, lsem.at[4])
    save_hid.start()
    save_slope = pltpu.make_async_copy(slope, slope_o, lsem.at[5])
    save_slope.start()
    total = part[at.p]
    for i in range(7):
        cps.expect(rbuf.at[i], base + i, at.proto_peer(i + 1)).wait_recv()
        total = total + rbuf[i]
    recip = lax.rsqrt(jnp.sum(total * total, axis=1, keepdims=True) + norm_eps)
    unit = total * recip
    sbuf[at.p] = unit.astype(bf16)
    sc = [cps.start(sbuf.at[at.p], sbuf.at[at.p], at.proto_peer(d)) for d in range(1, 8)]
    unit_o[...] = unit
    recip_o[...] = jnp.broadcast_to(recip, recip_o.shape)
    for k in sc:
        k.wait_recv()
    sn_o[...] = sbuf[...].reshape(rows, sbuf.shape[2])
    save.wait()
    save_hid.wait()
    save_slope.wait()
    cps.finish()


def head(tokens, w_in, w_out, teacher_z, proto_teacher, center):
    rows, depth = tokens.shape
    hidden = w_in.shape[1]
    wide = w_out.shape[1]
    kk = proto_teacher.shape[1]
    small = teacher_z.shape[0]
    shp = jax.ShapeDtypeStruct
    copies = 40 + 7 + 7 + 7
    return pl.pallas_call(
        head_kernel,
        out_shape=(
            shp((rows, hidden), bf16), shp((rows, hidden), f32), shp((rows, wide), bf16),
            shp((small, wide), f32), shp((small, 128), f32), shp((rows, kk), bf16), shp((8, rows), f32),
        ),
        in_specs=[aspec(), aspec(), vspec(), vspec(), aspec(), vspec()],
        out_specs=(aspec(), aspec(), vspec(), vspec(), vspec(), aspec(), vspec()),
        scratch_shapes=[
            VMEM((rows, depth), bf16), VMEM((16,) + w_in.shape, bf16),
            VMEM(proto_teacher.shape, bf16), VMEM((rows, kk), f32), VMEM((rows, kk), bf16),
            VMEM((rows, 128), f32), VMEM((rows, 128), f32),
            VMEM((rows, hidden), f32), VMEM((rows, hidden), bf16), VMEM((rows, hidden), f32),
            VMEM((8, small, wide), bf16), VMEM((8, small, wide), f32),
            VMEM((7, small, wide), f32), VMEM((8, small, wide), bf16),
            pltpu.SemaphoreType.DMA((copies,)), pltpu.SemaphoreType.DMA((copies,)),
            pltpu.SemaphoreType.DMA((6,)),
        ],
        compiler_params=pltpu.CompilerParams(
            collective_id=0, has_side_effects=True, vmem_limit_bytes=62 * 2**20
        ),
        name="head",
    )(tokens, w_in, w_out, teacher_z, proto_teacher, center[None, :])


def along(col):
    return jnp.transpose(col)


def middle_kernel(
    sn, proto_s, et_in, stat_t, image, unit, recip,
    dbott_o, pgrad_o, loss_o,
    ps, et, ls, gs, gs_, snt, ms, ss, cs, cbuf, stats, fsb, ftb,
    S, snd, rc, far, nm, np_, xb, xa, fin, fcore,
    S_, snd_, rc_, far_, nm_, np__, xb_, xa_, fin_, fcore_,
    dacc, dpart, drecv, dbuf, send, recv, lsem,
):
    at = Place()
    cps = Copies(send, recv)
    rows, kk = ls.shape
    half = kk // 2
    peers = [at.proto_peer(d) for d in range(1, 8)] + [at.row_peer(d) for d in range(1, 16)]
    greet(peers)
    third = kk // 3
    load_ps = [
        pltpu.make_async_copy(
            proto_s.at[:, pl.ds(i * third, third)], ps.at[:, pl.ds(i * third, third)], lsem.at[2 + i]
        )
        for i in range(3)
    ]
    for k in load_ps:
        k.start()
    load_et = pltpu.make_async_copy(et_in, et, lsem.at[1])
    load_et.start()
    snt[...] = jnp.transpose(sn[...])
    images = cbuf.shape[1]
    onehot = (lax.broadcasted_iota(jnp.int32, (images, rows), 0) == image[...]).astype(f32)
    cbuf[at.r] = jnp.broadcast_to(jnp.sum(onehot, axis=1, keepdims=True), cbuf.shape[1:])
    step = 512

    def one(j, top):
        cols = pl.ds(pl.multiple_of(j * step, step), step)
        v = jnp.dot(sn[...], ps[:, cols], preferred_element_type=f32) * (1.0 / tau_student)
        ls[:, cols] = v
        for q in range(step // 128):
            top = jnp.maximum(top, v[:, q * 128 : (q + 1) * 128])
        return top

    ms[...] = jnp.full((rows, 128), -jnp.inf, f32)
    for i in range(3):
        load_ps[i].wait()
        ms[...] = lax.fori_loop(i * third // step, (i + 1) * third // step, one, ms[...])
    met(len(peers))
    cc = [cps.start(cbuf.at[at.r], cbuf.at[at.r], at.row_peer(d)) for d in range(1, 16)]
    ms[...] = jnp.broadcast_to(jnp.max(ms[...], axis=1, keepdims=True), (rows, 128))
    load_et.wait()

    def two(i, _):
        rs = pl.ds(pl.multiple_of(i * 64, 64), 64)
        peak = ms[rs, :]

        def tile(j, acc):
            s, c = acc
            for q in range(8):
                cols = pl.ds(pl.multiple_of(j * 1024 + q * 128, 128), 128)
                d = ls[rs, cols] - peak
                e = jnp.exp(d)
                ls[rs, cols] = e
                s = s + e
                c = c + et[rs, cols].astype(f32) * d
            return s, c

        zero = jnp.zeros((64, 128), f32)
        ss[rs, :], cs[rs, :] = lax.fori_loop(0, kk // 1024, tile, (zero, zero))
        return 0

    lax.fori_loop(0, rows // 64, two, 0)
    stats[at.p] = jnp.concatenate(
        [
            stat_t[0:2],
            along(ms[...])[0:1],
            jnp.sum(along(ss[...]), axis=0, keepdims=True),
            jnp.sum(along(cs[...]), axis=0, keepdims=True),
            jnp.zeros((3, rows), f32),
        ],
        axis=0,
    )
    sc = [cps.start(stats.at[at.p], stats.at[at.p], at.proto_peer(d)) for d in range(1, 8)]
    for k in cc:
        k.wait_recv()
    counts = jnp.sum(cbuf[...], axis=0)[:, 0:1]
    w_row = 1.0 / (images * jnp.sum(onehot * counts, axis=0, keepdims=True))
    for k in sc:
        k.wait_recv()
    table = [stats[q] for q in range(8)]
    top_t = table[0][0:1]
    top_s = table[0][2:3]
    for q in table[1:]:
        top_t = jnp.maximum(top_t, q[0:1])
        top_s = jnp.maximum(top_s, q[2:3])
    total_t = total_s = cross = jnp.zeros((1, rows), f32)
    for q in table:
        scale = jnp.exp(q[0:1] - top_t)
        total_t = total_t + q[1:2] * scale
        total_s = total_s + q[3:4] * jnp.exp(q[2:3] - top_s)
        cross = cross + scale * (q[4:5] + q[1:2] * (q[2:3] - top_s))
    cross = jnp.log(total_s) - cross / total_t
    loss_o[...] = jnp.broadcast_to(w_row * cross, loss_o.shape)
    mine = stats[at.p]
    lift = (loss_scale / tau_student) * w_row
    fsb[...] = across(lift * jnp.exp(mine[2:3] - top_s) / total_s)
    ftb[...] = across(lift * jnp.exp(mine[0:1] - top_t) / total_t)
    dacc[...] = jnp.zeros_like(dacc)

    mine_at, other_at = at.c * half, (1 - at.c) * half
    quarter = half // 2
    firsts = [
        base + where + j * step
        for where in (0, quarter)
        for base in (other_at, mine_at)
        for j in range(quarter // step)
    ]

    def fill(t):
        dst = (gs, gs_)[t % 2]
        for i in range(0, rows, 64):
            f_s, f_t = fsb[i : i + 64, :], ftb[i : i + 64, :]
            for q in range(step // 128):
                cols = pl.ds(pl.multiple_of(firsts[t] + q * 128, 128), 128)
                v = ls[i : i + 64, cols] * f_s - et[i : i + 64, cols].astype(f32) * f_t
                dst[i : i + 64, q * 128 : (q + 1) * 128] = v.astype(bf16)

    def grads(segment, dst):
        count = quarter // step
        for j in range(count):
            t = segment * count + j
            g = (gs, gs_)[t % 2][...]
            v = jnp.dot(snt[...], g, preferred_element_type=f32)
            dst[:, :, j * step : (j + 1) * step] = v.astype(bf16).reshape(
                dst.shape[0], dst.shape[1], step
            )
            cols = pl.ds(pl.multiple_of(firsts[t], step), step)
            dacc[...] += lax.dot_general(
                g, ps[:, cols], (((1,), (1,)), ((), ())), preferred_element_type=f32
            )
            if t + 1 < len(firsts):
                fill(t + 1)

    one = Scatter(cps, at, S, (far, nm, np_, xb, xa), 1, 896, 384, 256)
    two = Scatter(cps, at, S_, (far_, nm_, np__, xb_, xa_), 1, 896, 512, 384)

    def merge(rs, S, rc, swap):
        swap.wait_recv()
        for other, dy in ORDER:
            g = at.chip(other, dy)
            S[g] = (S[g].astype(f32) + rc[g].astype(f32)).astype(bf16)
            rs.ready(other, dy)
            if other:
                rs.ready_x(dy)

    fill(0)
    grads(0, snd)
    swap = cps.start(snd, rc, at.CO)
    grads(1, S)
    grads(2, snd_)
    swap_ = cps.start(snd_, rc_, at.CO)
    merge(one, S, rc, swap)
    grads(3, S_)
    dpart[...] = dacc[...].astype(bf16).reshape(dpart.shape)
    dc = [
        cps.start(dpart.at[(at.p + d) % 8], drecv.at[d], at.proto_peer(d)) for d in range(1, 8)
    ]
    one.mid_a(1)
    merge(two, S_, rc_, swap_)
    one.mid_b(2)
    one.mid_a(0)
    total = dpart[at.p].astype(f32)
    for d in range(1, 8):
        dc[d - 1].wait_recv()
        total = total + drecv[d].astype(f32)
    u, r = unit[...], recip[:, 0:1]
    dbuf[at.p] = (r * (total - u * jnp.sum(u * total, axis=1, keepdims=True))).astype(bf16)
    bc = [cps.start(dbuf.at[at.p], dbuf.at[at.p], at.proto_peer(d)) for d in range(1, 8)]
    one.mid_b(1)
    one.late_a()
    one.mid_b(3)
    two.mid_a(1)
    one.late_b()
    two.mid_b(2)
    two.mid_a(0)
    two.mid_b(1)
    two.late_a()
    two.mid_b(3)
    two.late_b()
    n = fcore.shape[0]
    keep, give = pl.ds(pl.multiple_of(at.c * n, 8), n), pl.ds(pl.multiple_of((1 - at.c) * n, 8), n)

    def settle(rs, fin, fcore, where):
        rs.final(fin)
        fc = cps.start(fin.at[give], fcore, at.CO)
        pgrad_o[:, pl.ds(pl.multiple_of(mine_at + where, quarter), quarter)] = fin[keep, :]
        return fc

    fc = settle(one, fin, fcore, 0)
    for k in bc:
        k.wait_recv()
    dbott_o[...] = dbuf[...].reshape(dbott_o.shape)
    fc_ = settle(two, fin_, fcore_, quarter)
    fc.wait_recv()
    pgrad_o[:, pl.ds(pl.multiple_of(other_at, half), quarter)] = fcore[...]
    fc_.wait_recv()
    pgrad_o[:, pl.ds(pl.multiple_of(other_at + quarter, quarter), quarter)] = fcore_[...]
    cps.finish()


def middle(sn, proto_s, et, stat_t, image, unit, recip):
    rows, wide = sn.shape
    kk = proto_s.shape[1]
    small = unit.shape[0]
    shp = jax.ShapeDtypeStruct
    chunk = (wide // 8, kk // 4)
    copies = 15 + 7 + 7 + 7 + 2 * (1 + 23 + 1)
    lane = VMEM((rows, 128), f32)
    part = [VMEM((8,) + chunk, bf16)] * 3 + scatter_bufs(chunk)
    part += [VMEM(chunk, f32), VMEM((chunk[0] // 2, chunk[1]), f32)]
    return pl.pallas_call(
        middle_kernel,
        out_shape=(shp((rows, wide), bf16), shp((wide // 16, kk), f32), shp((8, rows), f32)),
        in_specs=[vspec(), aspec(), aspec()] + [vspec()] * 4,
        out_specs=(vspec(),) * 3,
        scratch_shapes=[
            VMEM((wide, kk), bf16), VMEM((rows, kk), bf16), VMEM((rows, kk), f32), VMEM((rows, 512), bf16), VMEM((rows, 512), bf16),
            VMEM((wide, rows), bf16), lane, lane, lane, VMEM((16, 64, 128), f32), VMEM((8, 8, rows), f32), lane, lane,
            *(part + part),
            VMEM((rows, wide), f32), VMEM((8, small, wide), bf16), VMEM((8, small, wide), bf16), VMEM((8, small, wide), bf16),
            pltpu.SemaphoreType.DMA((copies,)), pltpu.SemaphoreType.DMA((copies,)),
            pltpu.SemaphoreType.DMA((5,)),
        ],
        compiler_params=pltpu.CompilerParams(
            collective_id=1, has_side_effects=True, vmem_limit_bytes=62 * 2**20
        ),
        name="middle",
    )(sn, proto_s, et, stat_t, image, unit, recip)


def tail_kernel(
    tokens, hid_in, slope_in, dbott, w_out, loss_in,
    wgrad_o, wout_o, loss_o,
    tok, hid, slope, dp, S, snd, rc, far, nm, np_, xb, xa, fin, fcore,
    W, S2, rc2, r2, own2, wbuf, lbuf, send, recv, lsem,
):
    at = Place()
    cps = Copies(send, recv)
    rows, hidden = dp.shape
    half = hidden // 2
    peers = [at.row_peer(d) for d in range(1, 16)]
    greet(peers)
    load_tok = pltpu.make_async_copy(tokens, tok, lsem.at[0])
    load_tok.start()
    load_hid = pltpu.make_async_copy(hid_in, hid, lsem.at[2])
    load_hid.start()
    load_slope = pltpu.make_async_copy(slope_in, slope, lsem.at[1])
    load_slope.start()
    lbuf[at.r] = jnp.broadcast_to(
        jnp.sum(loss_in[...], axis=1, keepdims=True), lbuf.shape[1:]
    )
    load_hid.wait()
    small = W.shape[2]
    for j in range(hidden // 256):
        cols = slice(j * 256, (j + 1) * 256)
        v = lax.dot_general(
            hid[:, cols], dbott[...], (((0,), (0,)), ((), ())), preferred_element_type=f32
        ).astype(bf16)
        for i in range(256 // small):
            k = j * (256 // small) + i
            W[k % 2, k // 2] = v[i * small : (i + 1) * small]
    met(len(peers))
    swap2 = cps.start(W.at[1 - at.c], rc2, at.CO)
    lc = [cps.start(lbuf.at[at.r], lbuf.at[at.r], at.row_peer(d)) for d in range(1, 16)]
    load_slope.wait()

    def back(j, _):
        cols = pl.ds(pl.multiple_of(j * 256, 256), 256)
        v = lax.dot_general(
            dbott[...], w_out[cols, :], (((1,), (1,)), ((), ())), preferred_element_type=f32
        )
        dp[:, cols] = (v * slope[:, cols]).astype(bf16)
        return 0

    lax.fori_loop(0, hidden // 256, back, 0)
    load_tok.wait()
    rs = Scatter(cps, at, S, (far, nm, np_, xb, xa), 0, 288, 128, 112)
    swaps = {}

    def chunk(other, dy):
        g = at.chip(other, dy)
        lhs = pl.ds(pl.multiple_of(g * 512, 512), 512)
        for dst, side in ((snd, 1 - at.c), (S, at.c)):
            rhs = pl.ds(pl.multiple_of(side * half, half), half)
            dst[g] = lax.dot_general(
                tok[:, lhs], dp[:, rhs], (((0,), (0,)), ((), ())), preferred_element_type=f32
            ).astype(bf16)
            if dst is snd:
                swaps[other, dy] = cps.start(snd.at[g], rc.at[g], at.CO)

    def merge(other, dy):
        g = at.chip(other, dy)
        swaps[other, dy].wait_recv()
        S[g] = (S[g].astype(f32) + rc[g].astype(f32)).astype(bf16)
        rs.ready(other, dy)
        if other:
            rs.ready_x(dy)

    swap2.wait_recv()
    S2[...] = (W[at.c].astype(f32) + rc2[...].astype(f32)).astype(bf16)
    around = [k for k in ORDER if k != (False, 0)]
    sums = [
        cps.start(S2.at[at.chip(o, dy)], r2.at[k], at.dev(at.slot(o, dy)))
        for k, (o, dy) in enumerate(around)
    ]
    spread = []
    for i, key in enumerate(ORDER):
        chunk(*key)
        if i > 0:
            merge(*ORDER[i - 1])
        if i == 4:
            total = S2[at.chip(False, 0)].astype(f32)
            for k, cp in enumerate(sums):
                cp.wait_recv()
                total = total + r2[k].astype(f32)
            own2[...] = total.astype(bf16)
            wbuf[at.r] = own2[...]
            spread = [
                cps.start(own2, wbuf.at[at.r], at.dev(at.slot(o, dy))) for o, dy in around
            ]
            spread.append(cps.start(own2, wbuf.at[at.r], at.CO))
        if i == 6:
            rs.mid_a(1)
    rs.mid_b(2)
    merge(*ORDER[-1])
    rs.mid_a(0)
    rs.mid_b(1)
    rs.late_a()
    rs.mid_b(3)
    landed = [spread[-1]]
    for (o, dy), cp in zip(around, spread):
        cp.wait_recv()
        ref = wbuf.at[at.slot(o, (4 - dy) % 4)]
        landed.append(cps.start(ref, ref, at.CO))
    rs.late_b()
    rs.final(fin)
    n = fcore.shape[0]
    fc = cps.start(fin.at[pl.ds(pl.multiple_of((1 - at.c) * n, n), n)], fcore, at.CO)
    wgrad_o[:, pl.ds(pl.multiple_of(at.c * half, half), half)] = fin[pl.ds(pl.multiple_of(at.c * n, n), n), :]
    for copy in landed:
        copy.wait_recv()
    wout_o[...] = wbuf[...].reshape(wout_o.shape)
    for k in lc:
        k.wait_recv()
    loss_o[...] = jnp.sum(lbuf[...], axis=0)
    fc.wait_recv()
    wgrad_o[:, pl.ds(pl.multiple_of((1 - at.c) * half, half), half)] = fcore[...]
    cps.finish()


def tail(tokens, hid, slope, dbott, w_out, loss_row):
    rows, depth = tokens.shape
    hidden, wide = w_out.shape
    shp = jax.ShapeDtypeStruct
    block = (depth // 8, hidden // 2)
    small = (hidden // 16, wide)
    copies = 15 + 1 + 8 + 23 + 7 + 8 + 7 + 1
    return pl.pallas_call(
        tail_kernel,
        out_shape=(shp((depth // 16, hidden), f32), shp((hidden, wide), bf16), shp((8, 128), f32)),
        in_specs=[aspec(), aspec(), aspec(), vspec(), vspec(), vspec()],
        out_specs=(vspec(),) * 3,
        scratch_shapes=[
            VMEM((rows, depth), bf16), VMEM((rows, hidden), bf16), VMEM((rows, hidden), f32), VMEM((rows, hidden), bf16),
            VMEM((8,) + block, bf16), VMEM((8,) + block, bf16), VMEM((8,) + block, bf16),
            *scatter_bufs(block), VMEM(block, f32), VMEM((block[0] // 2, block[1]), f32),
            VMEM((2, 8) + small, bf16), VMEM((8,) + small, bf16), VMEM((8,) + small, bf16),
            VMEM((7,) + small, bf16), VMEM(small, bf16), VMEM((16,) + small, bf16),
            VMEM((16, 8, 128), f32),
            pltpu.SemaphoreType.DMA((copies,)), pltpu.SemaphoreType.DMA((copies,)),
            pltpu.SemaphoreType.DMA((3,)),
        ],
        compiler_params=pltpu.CompilerParams(
            collective_id=2, has_side_effects=True, vmem_limit_bytes=62 * 2**20
        ),
        name="tail",
    )(tokens, hid, slope, dbott, w_out, loss_row)


def close_kernel(wg, wo, pg, loss, wg_o, wo_o, pg_o, loss_o):
    wg_o[...] = wg[...]
    wo_o[...] = wo[...].astype(f32)
    pg_o[...] = pg[...]
    loss_o[0, 0] = loss[0, 0]


def close(wg, wo, pg, loss):
    shp = jax.ShapeDtypeStruct
    n = 2
    specs = [
        pl.BlockSpec((wg.shape[0] // n, wg.shape[1]), lambda i: (i, 0)),
        pl.BlockSpec((wo.shape[0] // n, wo.shape[1]), lambda i: (i, 0)),
        pl.BlockSpec((pg.shape[0], pg.shape[1] // n), lambda i: (0, i)),
    ]
    return pl.pallas_call(
        close_kernel,
        grid=(n,),
        out_shape=(shp(wg.shape, f32), shp(wo.shape, f32), shp(pg.shape, f32), shp((1, 1), f32)),
        in_specs=specs + [pl.BlockSpec((8, 128), lambda i: (0, 0))],
        out_specs=tuple(specs) + (pl.BlockSpec((1, 1), lambda i: (0, 0), memory_space=pltpu.SMEM),),
        name="close",
    )(wg, wo, pg, loss)


def on_device(tokens, w_in, w_out, teacher_z, proto_student, proto_teacher, center, image_of):
    hidden, slope, student_n, unit, recip, exp_t, stat_t = head(
        tokens, w_in, w_out, teacher_z, proto_teacher, center
    )
    dbott, proto_grad, loss_row = middle(
        student_n, proto_student, exp_t, stat_t, image_of[None, :], unit, recip
    )
    w_in_grad, w_out_grad, loss = tail(tokens, hidden, slope, dbott, w_out, loss_row)
    w_in_grad, w_out_grad, proto_grad, loss = close(w_in_grad, w_out_grad, proto_grad, loss)
    return (loss[0, 0], w_in_grad, w_out_grad, proto_grad)


def solution(mesh):
    return jax.shard_map(
        on_device,
        mesh=mesh,
        in_specs=(
            P("row", None),
            P("row", "proto"),
            P("proto", None),
            P(("row", "proto"), None),
            P(None, "proto"),
            P(None, "proto"),
            P("proto"),
            P("row"),
        ),
        out_specs=(P(), P("row", "proto"), P("proto", None), P("row", "proto")),
        check_vma=False,
    )
```

```python
import jax
import jax.numpy as jnp
from jax import lax
from jax.sharding import PartitionSpec as P
from jax.experimental import pallas as pl
from jax.experimental.pallas import tpu as pltpu

tau_teacher = 0.07
tau_student = 0.1
loss_scale = 1048576.0
norm_eps = 1e-06
MESH = pl.DeviceIdType.MESH
VMEM = pltpu.VMEM
f32 = jnp.float32
bf16 = jnp.bfloat16


def vspec():
    return pl.BlockSpec(memory_space=pltpu.VMEM)


def aspec():
    return pl.BlockSpec(memory_space=pl.ANY)


class Place:
    def __init__(self):
        self.r = lax.axis_index("row")
        self.p = lax.axis_index("proto")
        self.xh = self.r // 8
        self.y = (self.r // 2) % 4
        self.c = self.r % 2

    def chip(self, other, dy):
        fam = 1 - self.xh if other else self.xh
        return fam * 4 + (self.y + dy) % 4

    def slot(self, other, dy, core=None):
        return self.chip(other, dy) * 2 + (self.c if core is None else core)

    def dev(self, row):
        return (row, self.p)

    @property
    def X(self):
        return self.dev(self.slot(True, 0))

    @property
    def YP(self):
        return self.dev(self.slot(False, 1))

    @property
    def YM(self):
        return self.dev(self.slot(False, 3))

    @property
    def CO(self):
        return self.dev(self.slot(False, 0, 1 - self.c))

    def row_peer(self, d):
        return ((self.r + d) % 16, self.p)

    def proto_peer(self, d):
        return (self.r, (self.p + d) % 8)


class Copies:
    def __init__(self, send, recv):
        self.send, self.recv, self.all, self.sent = send, recv, [], []

    def start(self, src, dst, dev):
        i = len(self.all)
        cp = pltpu.make_async_remote_copy(
            src_ref=src,
            dst_ref=dst,
            send_sem=self.send.at[i],
            recv_sem=self.recv.at[i],
            device_id=dev,
            device_id_type=MESH,
        )
        cp.start()
        self.all.append(cp)
        return cp

    def expect(self, dst, i, dev):
        cp = pltpu.make_async_remote_copy(
            src_ref=dst,
            dst_ref=dst,
            send_sem=self.send.at[i],
            recv_sem=self.recv.at[i],
            device_id=dev,
            device_id_type=MESH,
        )
        self.all.append(cp)
        return cp

    def drained(self, cp):
        cp.wait_send()
        self.sent.append(cp)

    def finish(self):
        for cp in self.all:
            if not any(cp is k for k in self.sent):
                cp.wait_send()


def greet(peers):
    bar = pltpu.get_barrier_semaphore()
    for dev in peers:
        pl.semaphore_signal(bar, inc=1, device_id=dev, device_id_type=MESH)


def met(count):
    pl.semaphore_wait(pltpu.get_barrier_semaphore(), count)


def gather_rows(cps, at, own, buf, base, n, a, h, al):
    every = (0, n)
    up, lo = (h, n - h), (0, h)
    A, B = (0, a), (a, n - a)
    aup, alo = (al, a - al), (0, al)

    def on(slot, part, dev, src=None):
        ref = buf.at[slot, pl.ds(base + part[0], part[1])]
        return cps.start(ref if src is None else src, ref, dev)

    me = at.slot(False, 0)
    mine = own.at[pl.ds(base, n)]
    x0 = on(me, every, at.X, mine)
    p0 = on(me, every, at.YP, mine)
    m0 = on(me, every, at.YM, mine)
    c0 = on(me, every, at.CO, mine)
    yield [(c0, at.chip(False, 0))]
    sx = at.slot(True, 0)
    sm, sp, sf = at.slot(False, 3), at.slot(False, 1), at.slot(False, 2)
    xm, xp, xf = at.slot(True, 3), at.slot(True, 1), at.slot(True, 2)
    x0.wait_recv()
    xap = on(sx, A, at.YP)
    xam = on(sx, A, at.YM)
    xc = on(sx, every, at.CO)
    p0.wait_recv()
    fup = on(sm, up, at.YP)
    bm = on(sm, B, at.X)
    cm = on(sm, every, at.CO)
    m0.wait_recv()
    flo = on(sp, lo, at.YM)
    bp = on(sp, B, at.X)
    cp = on(sp, every, at.CO)
    yield [(xc, at.chip(True, 0)), (cm, at.chip(False, 3)), (cp, at.chip(False, 1))]
    xap.wait_recv()
    gup = on(xm, aup, at.YP)
    xam.wait_recv()
    glo = on(xp, alo, at.YM)
    fup.wait_recv()
    flo.wait_recv()
    bf = on(sf, B, at.X)
    cf = on(sf, every, at.CO)
    bm.wait_recv()
    cxm = on(xm, every, at.CO)
    bp.wait_recv()
    cxp = on(xp, every, at.CO)
    yield [(cf, at.chip(False, 2)), (cxm, at.chip(True, 3)), (cxp, at.chip(True, 1))]
    gup.wait_recv()
    glo.wait_recv()
    bf.wait_recv()
    cxf = on(xf, every, at.CO)
    yield [(cxf, at.chip(True, 2))]


def gather_small(cps, at, buf):
    xl = at.p % 2
    other = at.p + 1 - 2 * xl
    ring = [(at.r, (at.p + 2 * k) % 8) for k in (1, 2, 3)]
    over = cps.start(buf.at[at.p], buf.at[at.p], (at.r, other))
    first = [cps.start(buf.at[at.p], buf.at[at.p], dev) for dev in ring]
    yield
    over.wait_recv()
    second = [cps.start(buf.at[other], buf.at[other], dev) for dev in ring]
    yield
    for k in first + second:
        k.wait_recv()
    yield


def across(row):
    return jnp.transpose(jnp.broadcast_to(row, (128, row.shape[1])))


def gelu_parts(values):
    cumul = 0.5 * (1.0 + lax.erf(values * 0.7071067811865476))
    density = jnp.exp(-0.5 * values * values) * 0.3989422804014327
    return (values * cumul, cumul + values * density)


class Scatter:
    def __init__(self, cps, at, S, bufs, axis, a, al, bl):
        self.cps, self.at, self.S, self.axis = cps, at, S, axis
        self.far, self.nm, self.np, self.xb, self.xa = bufs
        n = S.shape[1 + axis]
        self.A, self.B = (0, a), (a, n - a)
        self.Alo, self.Aup = (0, al), (al, a - al)
        self.Blo, self.Bup = (a, bl), (a + bl, n - a - bl)
        self.got = {}

    def idx(self, i, part):
        cut = pl.ds(*part)
        return (i, cut) if self.axis == 0 else (i, slice(None), cut)

    def send(self, key, g, dst, i, part, dev):
        self.got[key] = self.cps.start(
            self.S.at[self.idx(g, part)], dst.at[self.idx(i, part)], dev
        )

    def add(self, g, part, *terms):
        where = self.idx(g, part)
        v = self.S[where].astype(f32)
        for ref, i in terms:
            v = v + ref[self.idx(i, part)].astype(f32)
        self.S[where] = v.astype(bf16)

    def wait(self, key):
        self.got[key].wait_recv()

    def ready(self, other, dy):
        g, k = self.at.chip(other, dy), int(other)
        if dy == 2:
            self.send(("fu", k), g, self.far, k, self.Aup, self.at.YP)
            self.send(("fl", k), g, self.far, k, self.Alo, self.at.YM)
        if dy == 1:
            self.send(("ml", k), g, self.nm, k, self.Alo, self.at.YP)
        if dy == 3:
            self.send(("pu", k), g, self.np, k, self.Aup, self.at.YM)

    def ready_x(self, dy):
        self.send(("x", dy), self.at.chip(True, dy), self.xb, dy, self.B, self.at.X)

    def mid_a(self, k):
        g1, g3 = self.at.chip(bool(k), 1), self.at.chip(bool(k), 3)
        self.wait(("fu", k))
        self.add(g1, self.Aup, (self.far, k))
        self.send(("mu", k), g1, self.nm, k, self.Aup, self.at.YP)
        self.wait(("fl", k))
        self.add(g3, self.Alo, (self.far, k))
        self.send(("pl", k), g3, self.np, k, self.Alo, self.at.YM)

    def mid_b(self, dy):
        g = self.at.chip(False, dy)
        self.wait(("x", dy))
        self.add(g, self.B, (self.xb, dy))
        if dy == 2:
            self.send("bfu", g, self.far, 0, self.Bup, self.at.YP)
            self.send("bfl", g, self.far, 0, self.Blo, self.at.YM)
        elif dy == 1:
            self.send("bml", g, self.nm, 0, self.Blo, self.at.YP)
        else:
            self.send("bpu", g, self.np, 0, self.Bup, self.at.YM)

    def late_a(self):
        for key in ("ml", "mu", "pl", "pu"):
            self.wait((key, 1))
        g = self.at.chip(True, 0)
        self.add(g, self.A, (self.nm, 1), (self.np, 1))
        self.send("xa", g, self.xa, 0, self.A, self.at.X)

    def late_b(self):
        g1, g3 = self.at.chip(False, 1), self.at.chip(False, 3)
        self.wait("bfu")
        self.add(g1, self.Bup, (self.far, 0))
        self.send("bmu", g1, self.nm, 0, self.Bup, self.at.YP)
        self.wait("bfl")
        self.add(g3, self.Blo, (self.far, 0))
        self.send("bpl", g3, self.np, 0, self.Blo, self.at.YM)

    def final(self, fin):
        g = self.at.chip(False, 0)
        for key in ("ml", "mu", "pl", "pu"):
            self.wait((key, 0))
        for key in ("xa", ("x", 0), "bml", "bmu", "bpl", "bpu"):
            self.wait(key)
        for part, last, i in ((self.A, self.xa, 0), (self.B, self.xb, 0)):
            v = self.S[self.idx(g, part)].astype(f32)
            for ref, j in ((self.nm, 0), (self.np, 0), (last, i)):
                v = v + ref[self.idx(j, part)].astype(f32)
            fin[self.idx(0, part)[1:]] = v


def scatter_bufs(shape):
    return [VMEM((n,) + shape, bf16) for n in (2, 2, 2, 4, 1)]


ORDER = [(True, 2), (True, 1), (True, 3), (True, 0), (False, 2), (False, 1), (False, 3), (False, 0)]


def head_kernel(
    tokens, w_in, w_out, teacher, proto_t, center,
    hid_o, slope_o, sn_o, unit_o, recip_o, et_o, stat_o,
    tok, wbuf, pt, lt, et, top, tot, pre, hid, slope, tbuf, part, rbuf, sbuf, send, recv, lsem,
):
    at = Place()
    cps = Copies(send, recv)
    rows, depth = tok.shape
    kk = lt.shape[1]
    peers = [at.X, at.YP, at.YM, at.CO] + [at.proto_peer(d) for d in range(1, 8)]
    greet(peers)
    me = at.slot(False, 0)
    load_pt = pltpu.make_async_copy(proto_t, pt, lsem.at[1])
    load_pt.start()
    own = pltpu.make_async_copy(w_in, wbuf.at[me], lsem.at[0])
    own.start()
    load_tok = pltpu.make_async_copy(tokens, tok, lsem.at[2])
    load_tok.start()
    t = teacher[...].astype(f32)
    tbuf[at.p] = (t * lax.rsqrt(jnp.sum(t * t, axis=1, keepdims=True) + norm_eps)).astype(bf16)
    met(len(peers))
    halves = [
        gather_rows(cps, at, w_in, wbuf, 0, 128, 80, 64, 32),
        gather_rows(cps, at, w_in, wbuf, 128, 128, 64, 64, 32),
    ]

    def accumulate(*landed):
        block = wbuf.shape[1] * 2
        for (one, chip), (two, _) in zip(*landed):
            one.wait_recv()
            two.wait_recv()
            lhs = tok[:, pl.ds(pl.multiple_of(chip * block, block), block)]

            def tile(j, _):
                cols = pl.ds(pl.multiple_of(j * 256, 256), 256)
                rhs = wbuf[pl.ds(chip * 2, 2), :, cols].reshape(block, 256)
                pre[:, cols] += jnp.dot(lhs, rhs, preferred_element_type=f32)
                return 0

            lax.fori_loop(0, pre.shape[1] // 256, tile, 0)

    teach = gather_small(cps, at, tbuf)
    next(teach)
    a0, b0 = (next(g) for g in halves)
    pre[...] = jnp.zeros_like(pre)
    load_pt.wait()
    next(teach)
    a1 = next(halves[0])
    next(teach)
    tn = tbuf[...].reshape(rows, tbuf.shape[2])
    step = 512

    def score(j, best):
        cols = pl.ds(pl.multiple_of(j * step, step), step)
        v = jnp.dot(tn, pt[:, cols], preferred_element_type=f32)
        v = (v - center[:, cols]) * (1.0 / tau_teacher)
        lt[:, cols] = v
        for q in range(step // 128):
            best = jnp.maximum(best, v[:, q * 128 : (q + 1) * 128])
        return best

    top[...] = lax.fori_loop(0, kk // step, score, jnp.full((rows, 128), -jnp.inf, f32))
    b1 = next(halves[1])
    top[...] = jnp.broadcast_to(jnp.max(top[...], axis=1, keepdims=True), (rows, 128))

    def lift(i, _):
        rs = pl.ds(pl.multiple_of(i * 64, 64), 64)
        peak = top[rs, :]

        def tile(j, acc):
            for q in range(8):
                cols = pl.ds(pl.multiple_of(j * 1024 + q * 128, 128), 128)
                e = jnp.exp(lt[rs, cols] - peak)
                et[rs, cols] = e.astype(bf16)
                acc = acc + e
            return acc

        tot[rs, :] = lax.fori_loop(0, kk // 1024, tile, jnp.zeros((64, 128), f32))
        return 0

    lax.fori_loop(0, rows // 128, lift, 0)
    own.wait()
    load_tok.wait()
    a2 = next(halves[0])
    lax.fori_loop(rows // 128, rows // 64, lift, 0)
    save = pltpu.make_async_copy(et, et_o, lsem.at[3])
    save.start()
    b2 = next(halves[1])
    accumulate(a0, b0)
    accumulate(a1, b1)
    a3 = next(halves[0])
    accumulate(a2, b2)
    b3 = next(halves[1])
    stat_o[...] = jnp.concatenate(
        [
            jnp.transpose(top[...])[0:1],
            jnp.sum(jnp.transpose(tot[...]), axis=0, keepdims=True),
            jnp.zeros((6, rows), f32),
        ],
        axis=0,
    )
    accumulate(a3, b3)

    small = part.shape[1]

    def act(q):
        rs = pl.ds(pl.multiple_of(q * small, small), small)
        value, grade = gelu_parts(pre[rs, :])
        slope[rs, :] = grade
        h = value.astype(bf16)
        hid[rs, :] = h
        part[q] = jnp.dot(h, w_out[...], preferred_element_type=f32)

    base = len(cps.all)

    def act_send(i, _):
        q = (at.p + i + 1) % 8
        act(q)
        pltpu.make_async_remote_copy(
            src_ref=part.at[q],
            dst_ref=rbuf.at[i],
            send_sem=send.at[base + i],
            recv_sem=recv.at[base + i],
            device_id=(at.r, q),
            device_id_type=MESH,
        ).start()
        return 0

    lax.fori_loop(0, 7, act_send, 0)
    act(at.p)
    save_hid = pltpu.make_async_copy(hid, hid_o, lsem.at[4])
    save_hid.start()
    save_slope = pltpu.make_async_copy(slope, slope_o, lsem.at[5])
    save_slope.start()
    total = part[at.p]
    for i in range(7):
        cps.expect(rbuf.at[i], base + i, at.proto_peer(i + 1)).wait_recv()
        total = total + rbuf[i]
    recip = lax.rsqrt(jnp.sum(total * total, axis=1, keepdims=True) + norm_eps)
    unit = total * recip
    sbuf[at.p] = unit.astype(bf16)
    sc = [cps.start(sbuf.at[at.p], sbuf.at[at.p], at.proto_peer(d)) for d in range(1, 8)]
    unit_o[...] = unit
    recip_o[...] = jnp.broadcast_to(recip, recip_o.shape)
    for k in sc:
        k.wait_recv()
    sn_o[...] = sbuf[...].reshape(rows, sbuf.shape[2])
    save.wait()
    save_hid.wait()
    save_slope.wait()
    cps.finish()


def head(tokens, w_in, w_out, teacher_z, proto_teacher, center):
    rows, depth = tokens.shape
    hidden = w_in.shape[1]
    wide = w_out.shape[1]
    kk = proto_teacher.shape[1]
    small = teacher_z.shape[0]
    shp = jax.ShapeDtypeStruct
    copies = 40 + 7 + 7 + 7
    return pl.pallas_call(
        head_kernel,
        out_shape=(
            shp((rows, hidden), bf16), shp((rows, hidden), f32), shp((rows, wide), bf16),
            shp((small, wide), f32), shp((small, 128), f32), shp((rows, kk), bf16), shp((8, rows), f32),
        ),
        in_specs=[aspec(), aspec(), vspec(), vspec(), aspec(), vspec()],
        out_specs=(aspec(), aspec(), vspec(), vspec(), vspec(), aspec(), vspec()),
        scratch_shapes=[
            VMEM((rows, depth), bf16), VMEM((16,) + w_in.shape, bf16),
            VMEM(proto_teacher.shape, bf16), VMEM((rows, kk), f32), VMEM((rows, kk), bf16),
            VMEM((rows, 128), f32), VMEM((rows, 128), f32),
            VMEM((rows, hidden), f32), VMEM((rows, hidden), bf16), VMEM((rows, hidden), f32),
            VMEM((8, small, wide), bf16), VMEM((8, small, wide), f32),
            VMEM((7, small, wide), f32), VMEM((8, small, wide), bf16),
            pltpu.SemaphoreType.DMA((copies,)), pltpu.SemaphoreType.DMA((copies,)),
            pltpu.SemaphoreType.DMA((6,)),
        ],
        compiler_params=pltpu.CompilerParams(
            collective_id=0, has_side_effects=True, vmem_limit_bytes=62 * 2**20
        ),
        name="head",
    )(tokens, w_in, w_out, teacher_z, proto_teacher, center[None, :])


def along(col):
    return jnp.transpose(col)


def rear_kernel(
    sn, proto_s, et_in, stat_t, image, unit, recip, tokens, hid_in, slope_in, w_out,
    pgrad_o, wgrad_o, wout_o, loss_o,
    ps, et, ls, gs, gs_, snt, ms, ss, cs, cbuf, stats,
    S, snd, rc, far, nm, np_, xb, xa, fin, fcore,
    S_, snd_, rc_, far_, nm_, np__, xb_, xa_, fin_, fcore_,
    dacc, dpart, drecv, dbuf, dbott,
    hid, dp, wS, wrc, wfar, wnm, wnp, wxb, wxa, wfcore,
    W, S2, rc2, r2, own2, wbuf, lbuf, send, recv, lsem,
):
    at = Place()
    cps = Copies(send, recv)
    rows, kk = ls.shape
    half = kk // 2
    peers = [at.proto_peer(d) for d in range(1, 8)] + [at.row_peer(d) for d in range(1, 16)]
    greet(peers)
    third = kk // 3
    load_ps = [
        pltpu.make_async_copy(
            proto_s.at[:, pl.ds(i * third, third)], ps.at[:, pl.ds(i * third, third)], lsem.at[2 + i]
        )
        for i in range(3)
    ]
    for k in load_ps:
        k.start()
    load_et = pltpu.make_async_copy(et_in, et, lsem.at[6])
    load_et.start()
    load_hid = pltpu.make_async_copy(hid_in, hid, lsem.at[0])
    load_hid.start()
    snt[...] = jnp.transpose(sn[...])
    images = cbuf.shape[1]
    onehot = (lax.broadcasted_iota(jnp.int32, (images, rows), 0) == image[...]).astype(f32)
    cbuf[at.r] = jnp.broadcast_to(jnp.sum(onehot, axis=1, keepdims=True), cbuf.shape[1:])
    step = 512

    def one(j, top):
        cols = pl.ds(pl.multiple_of(j * step, step), step)
        v = jnp.dot(sn[...], ps[:, cols], preferred_element_type=f32) * (1.0 / tau_student)
        ls[:, cols] = v
        for q in range(step // 128):
            top = jnp.maximum(top, v[:, q * 128 : (q + 1) * 128])
        return top

    ms[...] = jnp.full((rows, 128), -jnp.inf, f32)
    for i in range(3):
        load_ps[i].wait()
        ms[...] = lax.fori_loop(i * third // step, (i + 1) * third // step, one, ms[...])
    met(len(peers))
    cc = [cps.start(cbuf.at[at.r], cbuf.at[at.r], at.row_peer(d)) for d in range(1, 16)]
    ms[...] = jnp.broadcast_to(jnp.max(ms[...], axis=1, keepdims=True), (rows, 128))
    load_et.wait()

    def two(i, _):
        rs = pl.ds(pl.multiple_of(i * 64, 64), 64)
        peak = ms[rs, :]

        def tile(j, acc):
            s, c = acc
            for q in range(8):
                cols = pl.ds(pl.multiple_of(j * 1024 + q * 128, 128), 128)
                d = ls[rs, cols] - peak
                e = jnp.exp(d)
                ls[rs, cols] = e
                s = s + e
                c = c + et[rs, cols].astype(f32) * d
            return s, c

        zero = jnp.zeros((64, 128), f32)
        ss[rs, :], cs[rs, :] = lax.fori_loop(0, kk // 1024, tile, (zero, zero))
        return 0

    lax.fori_loop(0, rows // 64, two, 0)
    stats[at.p] = jnp.concatenate(
        [
            stat_t[0:2],
            along(ms[...])[0:1],
            jnp.sum(along(ss[...]), axis=0, keepdims=True),
            jnp.sum(along(cs[...]), axis=0, keepdims=True),
            jnp.zeros((3, rows), f32),
        ],
        axis=0,
    )
    sc = [cps.start(stats.at[at.p], stats.at[at.p], at.proto_peer(d)) for d in range(1, 8)]
    for k in cc:
        k.wait_recv()
    counts = jnp.sum(cbuf[...], axis=0)[:, 0:1]
    w_row = 1.0 / (images * jnp.sum(onehot * counts, axis=0, keepdims=True))
    for k in sc:
        k.wait_recv()
    table = [stats[q] for q in range(8)]
    top_t = table[0][0:1]
    top_s = table[0][2:3]
    for q in table[1:]:
        top_t = jnp.maximum(top_t, q[0:1])
        top_s = jnp.maximum(top_s, q[2:3])
    total_t = total_s = cross = jnp.zeros((1, rows), f32)
    for q in table:
        scale = jnp.exp(q[0:1] - top_t)
        total_t = total_t + q[1:2] * scale
        total_s = total_s + q[3:4] * jnp.exp(q[2:3] - top_s)
        cross = cross + scale * (q[4:5] + q[1:2] * (q[2:3] - top_s))
    cross = jnp.log(total_s) - cross / total_t
    lbuf[at.r] = jnp.broadcast_to(jnp.sum(w_row * cross, axis=1, keepdims=True), lbuf.shape[1:])
    lc = [cps.start(lbuf.at[at.r], lbuf.at[at.r], at.row_peer(d)) for d in range(1, 16)]
    mine = stats[at.p]
    lift = (loss_scale / tau_student) * w_row
    ss[...] = across(lift * jnp.exp(mine[2:3] - top_s) / total_s)
    cs[...] = across(lift * jnp.exp(mine[0:1] - top_t) / total_t)
    dacc[...] = jnp.zeros_like(dacc)

    mine_at, other_at = at.c * half, (1 - at.c) * half
    quarter = half // 2
    firsts = [
        base + where + j * step
        for where in (0, quarter)
        for base in (other_at, mine_at)
        for j in range(quarter // step)
    ]

    def fill(t):
        dst = (gs, gs_)[t % 2]
        for i in range(0, rows, 64):
            f_s, f_t = ss[i : i + 64, :], cs[i : i + 64, :]
            for q in range(step // 128):
                cols = pl.ds(pl.multiple_of(firsts[t] + q * 128, 128), 128)
                v = ls[i : i + 64, cols] * f_s - et[i : i + 64, cols].astype(f32) * f_t
                dst[i : i + 64, q * 128 : (q + 1) * 128] = v.astype(bf16)

    def grads(segment, dst):
        count = quarter // step
        for j in range(count):
            t = segment * count + j
            g = (gs, gs_)[t % 2][...]
            v = jnp.dot(snt[...], g, preferred_element_type=f32)
            dst[:, :, j * step : (j + 1) * step] = v.astype(bf16).reshape(
                dst.shape[0], dst.shape[1], step
            )
            cols = pl.ds(pl.multiple_of(firsts[t], step), step)
            dacc[...] += lax.dot_general(
                g, ps[:, cols], (((1,), (1,)), ((), ())), preferred_element_type=f32
            )
            if t + 1 < len(firsts):
                fill(t + 1)

    one = Scatter(cps, at, S, (far, nm, np_, xb, xa), 1, 896, 384, 256)
    two = Scatter(cps, at, S_, (far_, nm_, np__, xb_, xa_), 1, 896, 512, 384)

    def merge_pg(rs, S, rc, swap):
        swap.wait_recv()
        for other, dy in ORDER:
            g = at.chip(other, dy)
            S[g] = (S[g].astype(f32) + rc[g].astype(f32)).astype(bf16)
            rs.ready(other, dy)
            if other:
                rs.ready_x(dy)

    fill(0)
    grads(0, snd)
    swap = cps.start(snd, rc, at.CO)
    grads(1, S)
    grads(2, snd_)
    swap_ = cps.start(snd_, rc_, at.CO)
    merge_pg(one, S, rc, swap)
    grads(3, S_)
    load_tok = pltpu.make_async_copy(tokens, et.at[:, pl.ds(0, tokens.shape[1])], lsem.at[1])
    load_tok.start()
    hidden = dp.shape[1]
    load_slope = pltpu.make_async_copy(slope_in, ls.at[:, pl.ds(0, hidden)], lsem.at[5])
    load_slope.start()
    dpart[...] = dacc[...].astype(bf16).reshape(dpart.shape)
    dc = [
        cps.start(dpart.at[(at.p + d) % 8], drecv.at[d], at.proto_peer(d)) for d in range(1, 8)
    ]
    one.mid_a(1)
    merge_pg(two, S_, rc_, swap_)
    one.mid_b(2)
    one.mid_a(0)
    total = dpart[at.p].astype(f32)
    for d in range(1, 8):
        dc[d - 1].wait_recv()
        total = total + drecv[d].astype(f32)
    u, r = unit[...], recip[:, 0:1]
    dbuf[at.p] = (r * (total - u * jnp.sum(u * total, axis=1, keepdims=True))).astype(bf16)
    bc = [cps.start(dbuf.at[at.p], dbuf.at[at.p], at.proto_peer(d)) for d in range(1, 8)]
    load_hid.wait()
    one.mid_b(1)
    one.late_a()
    one.mid_b(3)
    two.mid_a(1)
    one.late_b()
    two.mid_b(2)
    for k in bc:
        k.wait_recv()
    dbott[...] = dbuf[...].reshape(dbott.shape)
    small = W.shape[2]
    for j in range(hidden // 256):
        cols = slice(j * 256, (j + 1) * 256)
        v = lax.dot_general(
            hid[:, cols], dbott[...], (((0,), (0,)), ((), ())), preferred_element_type=f32
        ).astype(bf16)
        for i in range(256 // small):
            k = j * (256 // small) + i
            W[k % 2, k // 2] = v[i * small : (i + 1) * small]
    swap2 = cps.start(W.at[1 - at.c], rc2, at.CO)
    two.mid_a(0)
    load_slope.wait()

    def back(j, _):
        cols = pl.ds(pl.multiple_of(j * 256, 256), 256)
        v = lax.dot_general(
            dbott[...], w_out[cols, :], (((1,), (1,)), ((), ())), preferred_element_type=f32
        )
        dp[:, cols] = (v * ls[:, cols]).astype(bf16)
        return 0

    lax.fori_loop(0, hidden // 256, back, 0)
    two.mid_b(1)
    swap2.wait_recv()
    S2[...] = (W[at.c].astype(f32) + rc2[...].astype(f32)).astype(bf16)
    around = [k for k in ORDER if k != (False, 0)]
    sums = [
        cps.start(S2.at[at.chip(o, dy)], r2.at[k], at.dev(at.slot(o, dy)))
        for k, (o, dy) in enumerate(around)
    ]
    load_tok.wait()
    rs = Scatter(cps, at, wS, (wfar, wnm, wnp, wxb, wxa), 0, 288, 128, 112)
    swaps = {}
    side = hidden // 2

    def chunk(i):
        other, dy = ORDER[i]
        g = at.chip(other, dy)
        lhs = pl.ds(pl.multiple_of(g * 512, 512), 512)

        def product(core):
            rhs = pl.ds(pl.multiple_of(core * side, side), side)
            return lax.dot_general(
                et[:, lhs], dp[:, rhs], (((0,), (0,)), ((), ())), preferred_element_type=f32
            ).astype(bf16)

        slot = et.at[:, pl.ds(tokens.shape[1] + (i % 4) * 512, 512)]
        if i >= 4:
            cps.drained(swaps[i - 4])
        slot[...] = product(1 - at.c)
        swaps[i] = cps.start(slot, wrc.at[g], at.CO)
        wS[g] = product(at.c)

    def merge(i):
        other, dy = ORDER[i]
        g = at.chip(other, dy)
        swaps[i].wait_recv()
        wS[g] = (wS[g].astype(f32) + wrc[g].astype(f32)).astype(bf16)
        rs.ready(other, dy)
        if other:
            rs.ready_x(dy)

    chunk(0)
    two.late_a()
    two.mid_b(3)
    two.late_b()
    for i in range(1, 8):
        chunk(i)
        merge(i - 1)
        if i == 4:
            total = S2[at.chip(False, 0)].astype(f32)
            for k, cp in enumerate(sums):
                cp.wait_recv()
                total = total + r2[k].astype(f32)
            own2[...] = total.astype(bf16)
            wbuf[at.r] = own2[...]
            spread = [
                cps.start(own2, wbuf.at[at.r], at.dev(at.slot(o, dy))) for o, dy in around
            ]
            spread.append(cps.start(own2, wbuf.at[at.r], at.CO))
        if i == 6:
            rs.mid_a(1)
    rs.mid_b(2)
    merge(7)
    n = fcore.shape[0]
    keep, give = pl.ds(pl.multiple_of(at.c * n, 8), n), pl.ds(pl.multiple_of((1 - at.c) * n, 8), n)

    def settle(rs, fin, fcore, where):
        rs.final(fin)
        fc = cps.start(fin.at[give], fcore, at.CO)
        pgrad_o[:, pl.ds(pl.multiple_of(mine_at + where, quarter), quarter)] = fin[keep, :]
        return fc

    fc = settle(one, fin, fcore, 0)
    rs.mid_a(0)
    rs.mid_b(1)
    fc_ = settle(two, fin_, fcore_, quarter)
    rs.late_a()
    rs.mid_b(3)
    landed = [spread[-1]]
    for (o, dy), cp in zip(around, spread):
        cp.wait_recv()
        ref = wbuf.at[at.slot(o, (4 - dy) % 4)]
        landed.append(cps.start(ref, ref, at.CO))
    fc.wait_recv()
    pgrad_o[:, pl.ds(pl.multiple_of(other_at, half), quarter)] = fcore[...]
    fc_.wait_recv()
    pgrad_o[:, pl.ds(pl.multiple_of(other_at + quarter, quarter), quarter)] = fcore_[...]
    for k in lc:
        k.wait_recv()
    loss_o[...] = jnp.sum(lbuf[...], axis=0)
    rs.late_b()
    wfin = ls.at[:, pl.ds(2 * hidden, side)]
    rs.final(wfin)
    n = wfcore.shape[0]
    wfc = cps.start(wfin.at[pl.ds(pl.multiple_of((1 - at.c) * n, n), n)], wfcore, at.CO)
    wgrad_o[:, pl.ds(pl.multiple_of(at.c * side, side), side)] = ls[
        pl.ds(pl.multiple_of(at.c * n, n), n), 2 * hidden : 2 * hidden + side
    ]
    for copy in landed:
        copy.wait_recv()
    wout_o[...] = wbuf[...].reshape(wout_o.shape)
    wfc.wait_recv()
    wgrad_o[:, pl.ds(pl.multiple_of((1 - at.c) * side, side), side)] = wfcore[...]
    cps.finish()


def rear(sn, proto_s, et, stat_t, image, unit, recip, tokens, hid, slope, w_out):
    rows, wide = sn.shape
    kk = proto_s.shape[1]
    small = unit.shape[0]
    depth = tokens.shape[1]
    hidden = w_out.shape[0]
    shp = jax.ShapeDtypeStruct
    chunk = (wide // 8, kk // 4)
    block = (depth // 8, hidden // 2)
    slab = (hidden // 16, wide)
    copies = 15 + 7 + 7 + 7 + 2 * (1 + 23 + 1) + 15 + 1 + 8 + 23 + 7 + 8 + 7 + 1
    lane = VMEM((rows, 128), f32)
    part = [VMEM((8,) + chunk, bf16)] * 3 + scatter_bufs(chunk)
    part += [VMEM(chunk, f32), VMEM((chunk[0] // 2, chunk[1]), f32)]
    row_block = VMEM((8, small, wide), bf16)
    return pl.pallas_call(
        rear_kernel,
        out_shape=(
            shp((wide // 16, kk), f32), shp((depth // 16, hidden), f32), shp((hidden, wide), bf16),
            shp((8, 128), f32),
        ),
        in_specs=[vspec(), aspec(), aspec()] + [vspec()] * 4 + [aspec()] * 3 + [vspec()],
        out_specs=(vspec(),) * 4,
        scratch_shapes=[
            VMEM((wide, kk), bf16), VMEM((rows, kk), bf16), VMEM((rows, kk), f32),
            VMEM((rows, 512), bf16), VMEM((rows, 512), bf16), VMEM((wide, rows), bf16),
            lane, lane, lane, VMEM((16, 64, 128), f32), VMEM((8, 8, rows), f32),
            *(part + part),
            VMEM((rows, wide), f32), row_block, row_block, row_block, VMEM((rows, wide), bf16),
            VMEM((rows, hidden), bf16), VMEM((rows, hidden), bf16),
            VMEM((8,) + block, bf16), VMEM((8,) + block, bf16), *scatter_bufs(block),
            VMEM((block[0] // 2, block[1]), f32),
            VMEM((2, 8) + slab, bf16), VMEM((8,) + slab, bf16), VMEM((8,) + slab, bf16),
            VMEM((7,) + slab, bf16), VMEM(slab, bf16), VMEM((16,) + slab, bf16),
            VMEM((16, 8, 128), f32),
            pltpu.SemaphoreType.DMA((copies,)), pltpu.SemaphoreType.DMA((copies,)),
            pltpu.SemaphoreType.DMA((7,)),
        ],
        compiler_params=pltpu.CompilerParams(
            collective_id=1, has_side_effects=True, vmem_limit_bytes=67043328
        ),
        name="rear",
    )(sn, proto_s, et, stat_t, image, unit, recip, tokens, hid, slope, w_out)


def close_kernel(wg, wo, pg, loss, wg_o, wo_o, pg_o, loss_o):
    wg_o[...] = wg[...]
    wo_o[...] = wo[...].astype(f32)
    pg_o[...] = pg[...]
    loss_o[0, 0] = loss[0, 0]


def close(wg, wo, pg, loss):
    shp = jax.ShapeDtypeStruct
    n = 2
    specs = [
        pl.BlockSpec((wg.shape[0] // n, wg.shape[1]), lambda i: (i, 0)),
        pl.BlockSpec((wo.shape[0] // n, wo.shape[1]), lambda i: (i, 0)),
        pl.BlockSpec((pg.shape[0], pg.shape[1] // n), lambda i: (0, i)),
    ]
    return pl.pallas_call(
        close_kernel,
        grid=(n,),
        out_shape=(shp(wg.shape, f32), shp(wo.shape, f32), shp(pg.shape, f32), shp((1, 1), f32)),
        in_specs=specs + [pl.BlockSpec((8, 128), lambda i: (0, 0))],
        out_specs=tuple(specs) + (pl.BlockSpec((1, 1), lambda i: (0, 0), memory_space=pltpu.SMEM),),
        name="close",
    )(wg, wo, pg, loss)


def on_device(tokens, w_in, w_out, teacher_z, proto_student, proto_teacher, center, image_of):
    hidden, slope, student_n, unit, recip, exp_t, stat_t = head(
        tokens, w_in, w_out, teacher_z, proto_teacher, center
    )
    proto_grad, w_in_grad, w_out_grad, loss = rear(
        student_n, proto_student, exp_t, stat_t, image_of[None, :], unit, recip,
        tokens, hidden, slope, w_out,
    )
    w_in_grad, w_out_grad, proto_grad, loss = close(w_in_grad, w_out_grad, proto_grad, loss)
    return (loss[0, 0], w_in_grad, w_out_grad, proto_grad)


def solution(mesh):
    return jax.shard_map(
        on_device,
        mesh=mesh,
        in_specs=(
            P("row", None),
            P("row", "proto"),
            P("proto", None),
            P(("row", "proto"), None),
            P(None, "proto"),
            P(None, "proto"),
            P("proto"),
            P("row"),
        ),
        out_specs=(P(), P("row", "proto"), P("proto", None), P("row", "proto")),
        check_vma=False,
    )
```

```python
import jax
import jax.numpy as jnp
from jax import lax
from jax.sharding import PartitionSpec as P
from jax.experimental import pallas as pl
from jax.experimental.pallas import tpu as pltpu

tau_teacher = 0.07
tau_student = 0.1
loss_scale = 1048576.0
norm_eps = 1e-06
MESH = pl.DeviceIdType.MESH
VMEM = pltpu.VMEM
f32 = jnp.float32
bf16 = jnp.bfloat16


def vspec():
    return pl.BlockSpec(memory_space=pltpu.VMEM)


def aspec():
    return pl.BlockSpec(memory_space=pl.ANY)


class Place:
    def __init__(self):
        self.r = lax.axis_index("row")
        self.p = lax.axis_index("proto")
        self.xh = self.r // 8
        self.y = (self.r // 2) % 4
        self.c = self.r % 2

    def chip(self, other, dy):
        fam = 1 - self.xh if other else self.xh
        return fam * 4 + (self.y + dy) % 4

    def slot(self, other, dy, core=None):
        return self.chip(other, dy) * 2 + (self.c if core is None else core)

    def dev(self, row):
        return (row, self.p)

    @property
    def X(self):
        return self.dev(self.slot(True, 0))

    @property
    def YP(self):
        return self.dev(self.slot(False, 1))

    @property
    def YM(self):
        return self.dev(self.slot(False, 3))

    @property
    def CO(self):
        return self.dev(self.slot(False, 0, 1 - self.c))

    def row_peer(self, d):
        return ((self.r + d) % 16, self.p)

    def proto_peer(self, d):
        return (self.r, (self.p + d) % 8)


class Copies:
    def __init__(self, send, recv):
        self.send, self.recv, self.all, self.sent = send, recv, [], []

    def start(self, src, dst, dev):
        i = len(self.all)
        cp = pltpu.make_async_remote_copy(
            src_ref=src,
            dst_ref=dst,
            send_sem=self.send.at[i],
            recv_sem=self.recv.at[i],
            device_id=dev,
            device_id_type=MESH,
        )
        cp.start()
        self.all.append(cp)
        return cp

    def expect(self, dst, i, dev):
        cp = pltpu.make_async_remote_copy(
            src_ref=dst,
            dst_ref=dst,
            send_sem=self.send.at[i],
            recv_sem=self.recv.at[i],
            device_id=dev,
            device_id_type=MESH,
        )
        self.all.append(cp)
        return cp

    def drained(self, cp):
        cp.wait_send()
        self.sent.append(cp)

    def finish(self):
        for cp in self.all:
            if not any(cp is k for k in self.sent):
                cp.wait_send()


def greet(peers):
    bar = pltpu.get_barrier_semaphore()
    for dev in peers:
        pl.semaphore_signal(bar, inc=1, device_id=dev, device_id_type=MESH)


def met(count):
    pl.semaphore_wait(pltpu.get_barrier_semaphore(), count)


def gather_rows(cps, at, own, buf, base, n, a, h, al):
    every = (0, n)
    up, lo = (h, n - h), (0, h)
    A, B = (0, a), (a, n - a)
    aup, alo = (al, a - al), (0, al)

    def on(slot, part, dev, src=None):
        ref = buf.at[slot, pl.ds(base + part[0], part[1])]
        return cps.start(ref if src is None else src, ref, dev)

    me = at.slot(False, 0)
    mine = own.at[pl.ds(base, n)]
    x0 = on(me, every, at.X, mine)
    p0 = on(me, every, at.YP, mine)
    m0 = on(me, every, at.YM, mine)
    c0 = on(me, every, at.CO, mine)
    yield [(c0, at.chip(False, 0))]
    sx = at.slot(True, 0)
    sm, sp, sf = at.slot(False, 3), at.slot(False, 1), at.slot(False, 2)
    xm, xp, xf = at.slot(True, 3), at.slot(True, 1), at.slot(True, 2)
    x0.wait_recv()
    xap = on(sx, A, at.YP)
    xam = on(sx, A, at.YM)
    xc = on(sx, every, at.CO)
    p0.wait_recv()
    fup = on(sm, up, at.YP)
    bm = on(sm, B, at.X)
    cm = on(sm, every, at.CO)
    m0.wait_recv()
    flo = on(sp, lo, at.YM)
    bp = on(sp, B, at.X)
    cp = on(sp, every, at.CO)
    yield [(xc, at.chip(True, 0)), (cm, at.chip(False, 3)), (cp, at.chip(False, 1))]
    xap.wait_recv()
    gup = on(xm, aup, at.YP)
    xam.wait_recv()
    glo = on(xp, alo, at.YM)
    fup.wait_recv()
    flo.wait_recv()
    bf = on(sf, B, at.X)
    cf = on(sf, every, at.CO)
    bm.wait_recv()
    cxm = on(xm, every, at.CO)
    bp.wait_recv()
    cxp = on(xp, every, at.CO)
    yield [(cf, at.chip(False, 2)), (cxm, at.chip(True, 3)), (cxp, at.chip(True, 1))]
    gup.wait_recv()
    glo.wait_recv()
    bf.wait_recv()
    cxf = on(xf, every, at.CO)
    yield [(cxf, at.chip(True, 2))]


def gather_small(cps, at, buf):
    xl = at.p % 2
    other = at.p + 1 - 2 * xl
    ring = [(at.r, (at.p + 2 * k) % 8) for k in (1, 2, 3)]
    over = cps.start(buf.at[at.p], buf.at[at.p], (at.r, other))
    first = [cps.start(buf.at[at.p], buf.at[at.p], dev) for dev in ring]
    yield
    over.wait_recv()
    second = [cps.start(buf.at[other], buf.at[other], dev) for dev in ring]
    yield
    for k in first + second:
        k.wait_recv()
    yield


def across(row):
    return jnp.transpose(jnp.broadcast_to(row, (128, row.shape[1])))


def gelu_parts(values):
    cumul = 0.5 * (1.0 + lax.erf(values * 0.7071067811865476))
    density = jnp.exp(-0.5 * values * values) * 0.3989422804014327
    return (values * cumul, cumul + values * density)


class Scatter:
    def __init__(self, cps, at, S, bufs, axis, a, al, bl):
        self.cps, self.at, self.S, self.axis = cps, at, S, axis
        self.far, self.nm, self.np, self.xb, self.xa = bufs
        n = S.shape[1 + axis]
        self.A, self.B = (0, a), (a, n - a)
        self.Alo, self.Aup = (0, al), (al, a - al)
        self.Blo, self.Bup = (a, bl), (a + bl, n - a - bl)
        self.got = {}

    def idx(self, i, part):
        cut = pl.ds(*part)
        return (i, cut) if self.axis == 0 else (i, slice(None), cut)

    def send(self, key, g, dst, i, part, dev):
        self.got[key] = self.cps.start(
            self.S.at[self.idx(g, part)], dst.at[self.idx(i, part)], dev
        )

    def add(self, g, part, *terms):
        where = self.idx(g, part)
        v = self.S[where].astype(f32)
        for ref, i in terms:
            v = v + ref[self.idx(i, part)].astype(f32)
        self.S[where] = v.astype(bf16)

    def wait(self, key):
        self.got[key].wait_recv()

    def ready(self, other, dy):
        g, k = self.at.chip(other, dy), int(other)
        if dy == 2:
            self.send(("fu", k), g, self.far, k, self.Aup, self.at.YP)
            self.send(("fl", k), g, self.far, k, self.Alo, self.at.YM)
        if dy == 1:
            self.send(("ml", k), g, self.nm, k, self.Alo, self.at.YP)
        if dy == 3:
            self.send(("pu", k), g, self.np, k, self.Aup, self.at.YM)

    def ready_x(self, dy):
        self.send(("x", dy), self.at.chip(True, dy), self.xb, dy, self.B, self.at.X)

    def mid_a(self, k):
        g1, g3 = self.at.chip(bool(k), 1), self.at.chip(bool(k), 3)
        self.wait(("fu", k))
        self.add(g1, self.Aup, (self.far, k))
        self.send(("mu", k), g1, self.nm, k, self.Aup, self.at.YP)
        self.wait(("fl", k))
        self.add(g3, self.Alo, (self.far, k))
        self.send(("pl", k), g3, self.np, k, self.Alo, self.at.YM)

    def mid_b(self, dy):
        g = self.at.chip(False, dy)
        self.wait(("x", dy))
        self.add(g, self.B, (self.xb, dy))
        if dy == 2:
            self.send("bfu", g, self.far, 0, self.Bup, self.at.YP)
            self.send("bfl", g, self.far, 0, self.Blo, self.at.YM)
        elif dy == 1:
            self.send("bml", g, self.nm, 0, self.Blo, self.at.YP)
        else:
            self.send("bpu", g, self.np, 0, self.Bup, self.at.YM)

    def late_a(self):
        for key in ("ml", "mu", "pl", "pu"):
            self.wait((key, 1))
        g = self.at.chip(True, 0)
        self.add(g, self.A, (self.nm, 1), (self.np, 1))
        self.send("xa", g, self.xa, 0, self.A, self.at.X)

    def late_b(self):
        g1, g3 = self.at.chip(False, 1), self.at.chip(False, 3)
        self.wait("bfu")
        self.add(g1, self.Bup, (self.far, 0))
        self.send("bmu", g1, self.nm, 0, self.Bup, self.at.YP)
        self.wait("bfl")
        self.add(g3, self.Blo, (self.far, 0))
        self.send("bpl", g3, self.np, 0, self.Blo, self.at.YM)

    def final(self, fin):
        g = self.at.chip(False, 0)
        for key in ("ml", "mu", "pl", "pu"):
            self.wait((key, 0))
        for key in ("xa", ("x", 0), "bml", "bmu", "bpl", "bpu"):
            self.wait(key)
        for part, last, i in ((self.A, self.xa, 0), (self.B, self.xb, 0)):
            v = self.S[self.idx(g, part)].astype(f32)
            for ref, j in ((self.nm, 0), (self.np, 0), (last, i)):
                v = v + ref[self.idx(j, part)].astype(f32)
            fin[self.idx(0, part)[1:]] = v


def scatter_bufs(shape):
    return [VMEM((n,) + shape, bf16) for n in (2, 2, 2, 4, 1)]


ORDER = [(True, 2), (True, 1), (True, 3), (True, 0), (False, 2), (False, 1), (False, 3), (False, 0)]


def head_kernel(
    tokens, w_in, w_out, teacher, proto_t, center,
    hid_o, slope_o, sn_o, unit_o, recip_o, et_o, stat_o,
    tok, wbuf, pt, lt, et, top, tot, pre, hid, slope, tbuf, part, rbuf, sbuf, send, recv, lsem,
):
    at = Place()
    cps = Copies(send, recv)
    rows, depth = tok.shape
    kk = lt.shape[1]
    peers = [at.X, at.YP, at.YM, at.CO] + [at.proto_peer(d) for d in range(1, 8)]
    greet(peers)
    me = at.slot(False, 0)
    load_pt = pltpu.make_async_copy(proto_t, pt, lsem.at[1])
    load_pt.start()
    own = pltpu.make_async_copy(w_in, wbuf.at[me], lsem.at[0])
    own.start()
    load_tok = pltpu.make_async_copy(tokens, tok, lsem.at[2])
    load_tok.start()
    t = teacher[...].astype(f32)
    tbuf[at.p] = (t * lax.rsqrt(jnp.sum(t * t, axis=1, keepdims=True) + norm_eps)).astype(bf16)
    met(len(peers))
    halves = [
        gather_rows(cps, at, w_in, wbuf, 0, 128, 80, 64, 32),
        gather_rows(cps, at, w_in, wbuf, 128, 128, 64, 64, 32),
    ]

    def accumulate(*landed):
        block = wbuf.shape[1] * 2
        for (one, chip), (two, _) in zip(*landed):
            one.wait_recv()
            two.wait_recv()
            lhs = tok[:, pl.ds(pl.multiple_of(chip * block, block), block)]

            def tile(j, _):
                cols = pl.ds(pl.multiple_of(j * 256, 256), 256)
                rhs = wbuf[pl.ds(chip * 2, 2), :, cols].reshape(block, 256)
                pre[:, cols] += jnp.dot(lhs, rhs, preferred_element_type=f32)
                return 0

            lax.fori_loop(0, pre.shape[1] // 256, tile, 0)

    teach = gather_small(cps, at, tbuf)
    next(teach)
    a0, b0 = (next(g) for g in halves)
    pre[...] = jnp.zeros_like(pre)
    load_pt.wait()
    next(teach)
    a1 = next(halves[0])
    next(teach)
    tn = tbuf[...].reshape(rows, tbuf.shape[2])
    step = 512

    def score(j, best):
        cols = pl.ds(pl.multiple_of(j * step, step), step)
        v = jnp.dot(tn, pt[:, cols], preferred_element_type=f32)
        v = (v - center[:, cols]) * (1.0 / tau_teacher)
        lt[:, cols] = v
        for q in range(step // 128):
            best = jnp.maximum(best, v[:, q * 128 : (q + 1) * 128])
        return best

    top[...] = lax.fori_loop(0, kk // step, score, jnp.full((rows, 128), -jnp.inf, f32))
    b1 = next(halves[1])
    top[...] = jnp.broadcast_to(jnp.max(top[...], axis=1, keepdims=True), (rows, 128))

    def lift(i, _):
        rs = pl.ds(pl.multiple_of(i * 64, 64), 64)
        peak = top[rs, :]

        def tile(j, acc):
            for q in range(8):
                cols = pl.ds(pl.multiple_of(j * 1024 + q * 128, 128), 128)
                e = jnp.exp(lt[rs, cols] - peak)
                et[rs, cols] = e.astype(bf16)
                acc = acc + e
            return acc

        tot[rs, :] = lax.fori_loop(0, kk // 1024, tile, jnp.zeros((64, 128), f32))
        return 0

    lax.fori_loop(0, rows // 128, lift, 0)
    own.wait()
    load_tok.wait()
    a2 = next(halves[0])
    lax.fori_loop(rows // 128, rows // 64, lift, 0)
    save = pltpu.make_async_copy(et, et_o, lsem.at[3])
    save.start()
    b2 = next(halves[1])
    accumulate(a0, b0)
    accumulate(a1, b1)
    a3 = next(halves[0])
    accumulate(a2, b2)
    b3 = next(halves[1])
    stat_o[...] = jnp.concatenate(
        [
            jnp.transpose(top[...])[0:1],
            jnp.sum(jnp.transpose(tot[...]), axis=0, keepdims=True),
            jnp.zeros((6, rows), f32),
        ],
        axis=0,
    )
    accumulate(a3, b3)

    small = part.shape[1]

    def act(q):
        rs = pl.ds(pl.multiple_of(q * small, small), small)
        value, grade = gelu_parts(pre[rs, :])
        slope[rs, :] = grade
        h = value.astype(bf16)
        hid[rs, :] = h
        part[q] = jnp.dot(h, w_out[...], preferred_element_type=f32)

    base = len(cps.all)

    def act_send(i, _):
        q = (at.p + i + 1) % 8
        act(q)
        pltpu.make_async_remote_copy(
            src_ref=part.at[q],
            dst_ref=rbuf.at[i],
            send_sem=send.at[base + i],
            recv_sem=recv.at[base + i],
            device_id=(at.r, q),
            device_id_type=MESH,
        ).start()
        return 0

    lax.fori_loop(0, 7, act_send, 0)
    act(at.p)
    save_hid = pltpu.make_async_copy(hid, hid_o, lsem.at[4])
    save_hid.start()
    save_slope = pltpu.make_async_copy(slope, slope_o, lsem.at[5])
    save_slope.start()
    total = part[at.p]
    for i in range(7):
        cps.expect(rbuf.at[i], base + i, at.proto_peer(i + 1)).wait_recv()
        total = total + rbuf[i]
    recip = lax.rsqrt(jnp.sum(total * total, axis=1, keepdims=True) + norm_eps)
    unit = total * recip
    sbuf[at.p] = unit.astype(bf16)
    sc = [cps.start(sbuf.at[at.p], sbuf.at[at.p], at.proto_peer(d)) for d in range(1, 8)]
    unit_o[...] = unit
    recip_o[...] = jnp.broadcast_to(recip, recip_o.shape)
    for k in sc:
        k.wait_recv()
    sn_o[...] = sbuf[...].reshape(rows, sbuf.shape[2])
    save.wait()
    save_hid.wait()
    save_slope.wait()
    cps.finish()


def head(tokens, w_in, w_out, teacher_z, proto_teacher, center):
    rows, depth = tokens.shape
    hidden = w_in.shape[1]
    wide = w_out.shape[1]
    kk = proto_teacher.shape[1]
    small = teacher_z.shape[0]
    shp = jax.ShapeDtypeStruct
    copies = 40 + 7 + 7 + 7
    return pl.pallas_call(
        head_kernel,
        out_shape=(
            shp((rows, hidden), bf16), shp((rows, hidden), f32), shp((rows, wide), bf16),
            shp((small, wide), f32), shp((small, 128), f32), shp((rows, kk), bf16), shp((8, rows), f32),
        ),
        in_specs=[aspec(), aspec(), vspec(), vspec(), aspec(), vspec()],
        out_specs=(aspec(), aspec(), vspec(), vspec(), vspec(), aspec(), vspec()),
        scratch_shapes=[
            VMEM((rows, depth), bf16), VMEM((16,) + w_in.shape, bf16),
            VMEM(proto_teacher.shape, bf16), VMEM((rows, kk), f32), VMEM((rows, kk), bf16),
            VMEM((rows, 128), f32), VMEM((rows, 128), f32),
            VMEM((rows, hidden), f32), VMEM((rows, hidden), bf16), VMEM((rows, hidden), f32),
            VMEM((8, small, wide), bf16), VMEM((8, small, wide), f32),
            VMEM((7, small, wide), f32), VMEM((8, small, wide), bf16),
            pltpu.SemaphoreType.DMA((copies,)), pltpu.SemaphoreType.DMA((copies,)),
            pltpu.SemaphoreType.DMA((6,)),
        ],
        compiler_params=pltpu.CompilerParams(
            collective_id=0, has_side_effects=True, vmem_limit_bytes=62 * 2**20
        ),
        name="head",
    )(tokens, w_in, w_out, teacher_z, proto_teacher, center[None, :])


def along(col):
    return jnp.transpose(col)


def rear_kernel(
    sn, proto_s, et_in, stat_t, image, unit, recip, tokens, hid_in, slope_in, w_out,
    pgrad_o, wgrad_o, wout_o, loss_o,
    ps, et, ls, gs, gs_, snt, ms, ss, cs, cbuf, stats,
    S, snd, rc, far, nm, np_, xb, xa, fin, fcore,
    S_, snd_, rc_, far_, nm_, np__, xb_, xa_, fin_, fcore_,
    dacc, dpart, drecv, dbuf, dbott,
    hid, dp, wS, wrc, wfar, wnm, wnp, wxb, wxa, wfcore,
    W, S2, rc2, r2, own2, wbuf, lbuf, send, recv, lsem,
):
    at = Place()
    cps = Copies(send, recv)
    rows, kk = ls.shape
    half = kk // 2
    peers = [at.proto_peer(d) for d in range(1, 8)] + [at.row_peer(d) for d in range(1, 16)]
    greet(peers)
    third = kk // 3
    load_ps = [
        pltpu.make_async_copy(
            proto_s.at[:, pl.ds(i * third, third)], ps.at[:, pl.ds(i * third, third)], lsem.at[2 + i]
        )
        for i in range(3)
    ]
    for k in load_ps:
        k.start()
    load_et = pltpu.make_async_copy(et_in, et, lsem.at[6])
    load_et.start()
    load_hid = pltpu.make_async_copy(hid_in, hid, lsem.at[0])
    load_hid.start()
    snt[...] = jnp.transpose(sn[...])
    images = cbuf.shape[1]
    onehot = (lax.broadcasted_iota(jnp.int32, (images, rows), 0) == image[...]).astype(f32)
    cbuf[at.r] = jnp.broadcast_to(jnp.sum(onehot, axis=1, keepdims=True), cbuf.shape[1:])
    step = 512

    def one(j, top):
        cols = pl.ds(pl.multiple_of(j * step, step), step)
        v = jnp.dot(sn[...], ps[:, cols], preferred_element_type=f32) * (1.0 / tau_student)
        ls[:, cols] = v
        for q in range(step // 128):
            top = jnp.maximum(top, v[:, q * 128 : (q + 1) * 128])
        return top

    ms[...] = jnp.full((rows, 128), -jnp.inf, f32)
    for i in range(3):
        load_ps[i].wait()
        ms[...] = lax.fori_loop(i * third // step, (i + 1) * third // step, one, ms[...])
    met(len(peers))
    cc = [cps.start(cbuf.at[at.r], cbuf.at[at.r], at.row_peer(d)) for d in range(1, 16)]
    ms[...] = jnp.broadcast_to(jnp.max(ms[...], axis=1, keepdims=True), (rows, 128))
    load_et.wait()

    def two(i, _):
        rs = pl.ds(pl.multiple_of(i * 64, 64), 64)
        peak = ms[rs, :]

        def tile(j, acc):
            s, c = acc
            for q in range(8):
                cols = pl.ds(pl.multiple_of(j * 1024 + q * 128, 128), 128)
                d = ls[rs, cols] - peak
                e = jnp.exp(d)
                ls[rs, cols] = e
                s = s + e
                c = c + et[rs, cols].astype(f32) * d
            return s, c

        zero = jnp.zeros((64, 128), f32)
        ss[rs, :], cs[rs, :] = lax.fori_loop(0, kk // 1024, tile, (zero, zero))
        return 0

    lax.fori_loop(0, rows // 64, two, 0)
    stats[at.p] = jnp.concatenate(
        [
            stat_t[0:2],
            along(ms[...])[0:1],
            jnp.sum(along(ss[...]), axis=0, keepdims=True),
            jnp.sum(along(cs[...]), axis=0, keepdims=True),
            jnp.zeros((3, rows), f32),
        ],
        axis=0,
    )
    sc = [cps.start(stats.at[at.p], stats.at[at.p], at.proto_peer(d)) for d in range(1, 8)]
    for k in cc:
        k.wait_recv()
    counts = jnp.sum(cbuf[...], axis=0)[:, 0:1]
    w_row = 1.0 / (images * jnp.sum(onehot * counts, axis=0, keepdims=True))
    for k in sc:
        k.wait_recv()
    table = [stats[q] for q in range(8)]
    top_t = table[0][0:1]
    top_s = table[0][2:3]
    for q in table[1:]:
        top_t = jnp.maximum(top_t, q[0:1])
        top_s = jnp.maximum(top_s, q[2:3])
    total_t = total_s = cross = jnp.zeros((1, rows), f32)
    for q in table:
        scale = jnp.exp(q[0:1] - top_t)
        total_t = total_t + q[1:2] * scale
        total_s = total_s + q[3:4] * jnp.exp(q[2:3] - top_s)
        cross = cross + scale * (q[4:5] + q[1:2] * (q[2:3] - top_s))
    cross = jnp.log(total_s) - cross / total_t
    lbuf[at.r] = jnp.broadcast_to(jnp.sum(w_row * cross, axis=1, keepdims=True), lbuf.shape[1:])
    lc = [cps.start(lbuf.at[at.r], lbuf.at[at.r], at.row_peer(d)) for d in range(1, 16)]
    mine = stats[at.p]
    lift = (loss_scale / tau_student) * w_row
    ss[...] = across(lift * jnp.exp(mine[2:3] - top_s) / total_s)
    cs[...] = across(lift * jnp.exp(mine[0:1] - top_t) / total_t)
    dacc[...] = jnp.zeros_like(dacc)

    mine_at, other_at = at.c * half, (1 - at.c) * half
    quarter = half // 2
    firsts = [
        base + where + j * step
        for where in (0, quarter)
        for base in (other_at, mine_at)
        for j in range(quarter // step)
    ]

    def fill(t):
        dst = (gs, gs_)[t % 2]
        for i in range(0, rows, 64):
            f_s, f_t = ss[i : i + 64, :], cs[i : i + 64, :]
            for q in range(step // 128):
                cols = pl.ds(pl.multiple_of(firsts[t] + q * 128, 128), 128)
                v = ls[i : i + 64, cols] * f_s - et[i : i + 64, cols].astype(f32) * f_t
                dst[i : i + 64, q * 128 : (q + 1) * 128] = v.astype(bf16)

    def grads(segment, dst):
        count = quarter // step
        for j in range(count):
            t = segment * count + j
            g = (gs, gs_)[t % 2][...]
            v = jnp.dot(snt[...], g, preferred_element_type=f32)
            dst[:, :, j * step : (j + 1) * step] = v.astype(bf16).reshape(
                dst.shape[0], dst.shape[1], step
            )
            cols = pl.ds(pl.multiple_of(firsts[t], step), step)
            dacc[...] += lax.dot_general(
                g, ps[:, cols], (((1,), (1,)), ((), ())), preferred_element_type=f32
            )
            if t + 1 < len(firsts):
                fill(t + 1)

    one = Scatter(cps, at, S, (far, nm, np_, xb, xa), 1, 896, 384, 256)
    two = Scatter(cps, at, S_, (far_, nm_, np__, xb_, xa_), 1, 896, 512, 384)

    def merge_pg(rs, S, rc, swap):
        swap.wait_recv()
        for other, dy in ORDER:
            g = at.chip(other, dy)
            S[g] = (S[g].astype(f32) + rc[g].astype(f32)).astype(bf16)
            rs.ready(other, dy)
            if other:
                rs.ready_x(dy)

    fill(0)
    grads(0, snd)
    swap = cps.start(snd, rc, at.CO)
    grads(1, S)
    grads(2, snd_)
    swap_ = cps.start(snd_, rc_, at.CO)
    merge_pg(one, S, rc, swap)
    grads(3, S_)
    load_tok = pltpu.make_async_copy(tokens, et.at[:, pl.ds(0, tokens.shape[1])], lsem.at[1])
    load_tok.start()
    hidden = dp.shape[1]
    load_slope = pltpu.make_async_copy(slope_in, ls.at[:, pl.ds(0, hidden)], lsem.at[5])
    load_slope.start()
    dpart[...] = dacc[...].astype(bf16).reshape(dpart.shape)
    dc = [
        cps.start(dpart.at[(at.p + d) % 8], drecv.at[d], at.proto_peer(d)) for d in range(1, 8)
    ]
    one.mid_a(1)
    one.mid_b(2)
    one.mid_a(0)
    total = dpart[at.p].astype(f32)
    for d in range(1, 8):
        dc[d - 1].wait_recv()
        total = total + drecv[d].astype(f32)
    u, r = unit[...], recip[:, 0:1]
    dbuf[at.p] = (r * (total - u * jnp.sum(u * total, axis=1, keepdims=True))).astype(bf16)
    bc = [cps.start(dbuf.at[at.p], dbuf.at[at.p], at.proto_peer(d)) for d in range(1, 8)]
    merge_pg(two, S_, rc_, swap_)
    load_hid.wait()
    one.mid_b(1)
    one.late_a()
    one.mid_b(3)
    two.mid_a(1)
    one.late_b()
    two.mid_b(2)
    for k in bc:
        k.wait_recv()
    dbott[...] = dbuf[...].reshape(dbott.shape)
    small = W.shape[2]
    for j in range(hidden // 256):
        cols = slice(j * 256, (j + 1) * 256)
        v = lax.dot_general(
            hid[:, cols], dbott[...], (((0,), (0,)), ((), ())), preferred_element_type=f32
        ).astype(bf16)
        for i in range(256 // small):
            k = j * (256 // small) + i
            W[k % 2, k // 2] = v[i * small : (i + 1) * small]
    swap2 = cps.start(W.at[1 - at.c], rc2, at.CO)
    two.mid_a(0)
    load_slope.wait()

    def back(j, _):
        cols = pl.ds(pl.multiple_of(j * 256, 256), 256)
        v = lax.dot_general(
            dbott[...], w_out[cols, :], (((1,), (1,)), ((), ())), preferred_element_type=f32
        )
        dp[:, cols] = (v * ls[:, cols]).astype(bf16)
        return 0

    lax.fori_loop(0, hidden // 256, back, 0)
    two.mid_b(1)
    swap2.wait_recv()
    S2[...] = (W[at.c].astype(f32) + rc2[...].astype(f32)).astype(bf16)
    around = [k for k in ORDER if k != (False, 0)]
    sums = [
        cps.start(S2.at[at.chip(o, dy)], r2.at[k], at.dev(at.slot(o, dy)))
        for k, (o, dy) in enumerate(around)
    ]
    load_tok.wait()
    rs = Scatter(cps, at, wS, (wfar, wnm, wnp, wxb, wxa), 0, 288, 128, 112)
    swaps = {}
    side = hidden // 2

    def chunk(i):
        other, dy = ORDER[i]
        g = at.chip(other, dy)
        lhs = pl.ds(pl.multiple_of(g * 512, 512), 512)

        def product(core):
            rhs = pl.ds(pl.multiple_of(core * side, side), side)
            return lax.dot_general(
                et[:, lhs], dp[:, rhs], (((0,), (0,)), ((), ())), preferred_element_type=f32
            ).astype(bf16)

        slot = et.at[:, pl.ds(tokens.shape[1] + (i % 4) * 512, 512)]
        if i >= 4:
            cps.drained(swaps[i - 4])
        slot[...] = product(1 - at.c)
        swaps[i] = cps.start(slot, wrc.at[g], at.CO)
        wS[g] = product(at.c)

    def merge(i):
        other, dy = ORDER[i]
        g = at.chip(other, dy)
        swaps[i].wait_recv()
        wS[g] = (wS[g].astype(f32) + wrc[g].astype(f32)).astype(bf16)
        rs.ready(other, dy)
        if other:
            rs.ready_x(dy)

    chunk(0)
    two.late_a()
    two.mid_b(3)
    two.late_b()
    for i in range(1, 8):
        chunk(i)
        merge(i - 1)
        if i == 4:
            total = S2[at.chip(False, 0)].astype(f32)
            for k, cp in enumerate(sums):
                cp.wait_recv()
                total = total + r2[k].astype(f32)
            own2[...] = total.astype(bf16)
            wbuf[at.r] = own2[...]
            spread = [
                cps.start(own2, wbuf.at[at.r], at.dev(at.slot(o, dy))) for o, dy in around
            ]
            spread.append(cps.start(own2, wbuf.at[at.r], at.CO))
        if i == 6:
            rs.mid_a(1)
    rs.mid_b(2)
    merge(7)
    n = fcore.shape[0]
    keep, give = pl.ds(pl.multiple_of(at.c * n, 8), n), pl.ds(pl.multiple_of((1 - at.c) * n, 8), n)

    def settle(rs, fin, fcore, where):
        rs.final(fin)
        fc = cps.start(fin.at[give], fcore, at.CO)
        pgrad_o[:, pl.ds(pl.multiple_of(mine_at + where, quarter), quarter)] = fin[keep, :]
        return fc

    fc = settle(one, fin, fcore, 0)
    rs.mid_a(0)
    rs.mid_b(1)
    fc_ = settle(two, fin_, fcore_, quarter)
    rs.late_a()
    rs.mid_b(3)
    landed = [spread[-1]]
    for (o, dy), cp in zip(around, spread):
        cp.wait_recv()
        ref = wbuf.at[at.slot(o, (4 - dy) % 4)]
        landed.append(cps.start(ref, ref, at.CO))
    fc.wait_recv()
    pgrad_o[:, pl.ds(pl.multiple_of(other_at, half), quarter)] = fcore[...]
    fc_.wait_recv()
    pgrad_o[:, pl.ds(pl.multiple_of(other_at + quarter, quarter), quarter)] = fcore_[...]
    for k in lc:
        k.wait_recv()
    loss_o[...] = jnp.sum(lbuf[...], axis=0)
    rs.late_b()
    wfin = ls.at[:, pl.ds(2 * hidden, side)]
    rs.final(wfin)
    n = wfcore.shape[0]
    wfc = cps.start(wfin.at[pl.ds(pl.multiple_of((1 - at.c) * n, n), n)], wfcore, at.CO)
    wgrad_o[:, pl.ds(pl.multiple_of(at.c * side, side), side)] = ls[
        pl.ds(pl.multiple_of(at.c * n, n), n), 2 * hidden : 2 * hidden + side
    ]
    for copy in landed:
        copy.wait_recv()
    wout_o[...] = wbuf[...].reshape(wout_o.shape)
    wfc.wait_recv()
    wgrad_o[:, pl.ds(pl.multiple_of((1 - at.c) * side, side), side)] = wfcore[...]
    cps.finish()


def rear(sn, proto_s, et, stat_t, image, unit, recip, tokens, hid, slope, w_out):
    rows, wide = sn.shape
    kk = proto_s.shape[1]
    small = unit.shape[0]
    depth = tokens.shape[1]
    hidden = w_out.shape[0]
    shp = jax.ShapeDtypeStruct
    chunk = (wide // 8, kk // 4)
    block = (depth // 8, hidden // 2)
    slab = (hidden // 16, wide)
    copies = 15 + 7 + 7 + 7 + 2 * (1 + 23 + 1) + 15 + 1 + 8 + 23 + 7 + 8 + 7 + 1
    lane = VMEM((rows, 128), f32)
    part = [VMEM((8,) + chunk, bf16)] * 3 + scatter_bufs(chunk)
    part += [VMEM(chunk, f32), VMEM((chunk[0] // 2, chunk[1]), f32)]
    row_block = VMEM((8, small, wide), bf16)
    return pl.pallas_call(
        rear_kernel,
        out_shape=(
            shp((wide // 16, kk), f32), shp((depth // 16, hidden), f32), shp((hidden, wide), bf16),
            shp((8, 128), f32),
        ),
        in_specs=[vspec(), aspec(), aspec()] + [vspec()] * 4 + [aspec()] * 3 + [vspec()],
        out_specs=(vspec(),) * 4,
        scratch_shapes=[
            VMEM((wide, kk), bf16), VMEM((rows, kk), bf16), VMEM((rows, kk), f32),
            VMEM((rows, 512), bf16), VMEM((rows, 512), bf16), VMEM((wide, rows), bf16),
            lane, lane, lane, VMEM((16, 64, 128), f32), VMEM((8, 8, rows), f32),
            *(part + part),
            VMEM((rows, wide), f32), row_block, row_block, row_block, VMEM((rows, wide), bf16),
            VMEM((rows, hidden), bf16), VMEM((rows, hidden), bf16),
            VMEM((8,) + block, bf16), VMEM((8,) + block, bf16), *scatter_bufs(block),
            VMEM((block[0] // 2, block[1]), f32),
            VMEM((2, 8) + slab, bf16), VMEM((8,) + slab, bf16), VMEM((8,) + slab, bf16),
            VMEM((7,) + slab, bf16), VMEM(slab, bf16), VMEM((16,) + slab, bf16),
            VMEM((16, 8, 128), f32),
            pltpu.SemaphoreType.DMA((copies,)), pltpu.SemaphoreType.DMA((copies,)),
            pltpu.SemaphoreType.DMA((7,)),
        ],
        compiler_params=pltpu.CompilerParams(
            collective_id=1, has_side_effects=True, vmem_limit_bytes=67043328
        ),
        name="rear",
    )(sn, proto_s, et, stat_t, image, unit, recip, tokens, hid, slope, w_out)


def close_kernel(wg, wo, pg, loss, wg_o, wo_o, pg_o, loss_o):
    wg_o[...] = wg[...]
    wo_o[...] = wo[...].astype(f32)
    pg_o[...] = pg[...]
    loss_o[0, 0] = loss[0, 0]


def close(wg, wo, pg, loss):
    shp = jax.ShapeDtypeStruct
    n = 2
    specs = [
        pl.BlockSpec((wg.shape[0] // n, wg.shape[1]), lambda i: (i, 0)),
        pl.BlockSpec((wo.shape[0] // n, wo.shape[1]), lambda i: (i, 0)),
        pl.BlockSpec((pg.shape[0], pg.shape[1] // n), lambda i: (0, i)),
    ]
    return pl.pallas_call(
        close_kernel,
        grid=(n,),
        out_shape=(shp(wg.shape, f32), shp(wo.shape, f32), shp(pg.shape, f32), shp((1, 1), f32)),
        in_specs=specs + [pl.BlockSpec((8, 128), lambda i: (0, 0))],
        out_specs=tuple(specs) + (pl.BlockSpec((1, 1), lambda i: (0, 0), memory_space=pltpu.SMEM),),
        name="close",
    )(wg, wo, pg, loss)


def on_device(tokens, w_in, w_out, teacher_z, proto_student, proto_teacher, center, image_of):
    hidden, slope, student_n, unit, recip, exp_t, stat_t = head(
        tokens, w_in, w_out, teacher_z, proto_teacher, center
    )
    proto_grad, w_in_grad, w_out_grad, loss = rear(
        student_n, proto_student, exp_t, stat_t, image_of[None, :], unit, recip,
        tokens, hidden, slope, w_out,
    )
    w_in_grad, w_out_grad, proto_grad, loss = close(w_in_grad, w_out_grad, proto_grad, loss)
    return (loss[0, 0], w_in_grad, w_out_grad, proto_grad)


def solution(mesh):
    return jax.shard_map(
        on_device,
        mesh=mesh,
        in_specs=(
            P("row", None),
            P("row", "proto"),
            P("proto", None),
            P(("row", "proto"), None),
            P(None, "proto"),
            P(None, "proto"),
            P("proto"),
            P("row"),
        ),
        out_specs=(P(), P("row", "proto"), P("proto", None), P("row", "proto")),
        check_vma=False,
    )
```
